32 devices in a mesh: hid: 8 (over y, x, core), tok: 4 (over z).
Axes of the slice: x: 2, y: 2, z: 4, core: 2. Of those that a mesh axis runs over, the one named last changes fastest.
Arguments:
- tokens: bfloat16 [896, 8192], P('tok', 'hid'), may hold values from -6 to 6
- in_blocks: bfloat16 [128, 6, 256, 256], P('hid', None, 'tok'), may hold values from -0.15625 to 0.15625
- in_left: bfloat16 [8192, 256], P(('hid', 'tok')), may hold values from -0.0625 to 0.0625
- in_right: bfloat16 [256, 32768], P(None, ('hid', 'tok')), may hold values from -0.375 to 0.375
- in_lists: int32 [128, 6], replicated, may hold values from 0 to 31, as said below
- out_blocks: bfloat16 [128, 6, 256, 256], P('hid', None, 'tok'), may hold values from -0.078125 to 0.078125
- out_left: bfloat16 [32768, 256], P(('hid', 'tok')), may hold values from -0.03125 to 0.03125
- out_right: bfloat16 [256, 8192], P(None, ('hid', 'tok')), may hold values from -0.375 to 0.375
- out_lists: int32 [128, 6], replicated, may hold values from 0 to 31, as said below
- cotangent: bfloat16 [896, 8192], P('tok', 'hid'), may hold values from -6 to 6
Outputs:
- layer_out: bfloat16 [896, 8192], P('tok', 'hid')
- grad_tokens: bfloat16 [896, 8192], P('tok', 'hid')
- grad_in_blocks: bfloat16 [128, 6, 256, 256], P('hid', None, 'tok')
- grad_in_left: bfloat16 [8192, 256], P(('hid', 'tok'))
- grad_in_right: bfloat16 [256, 32768], P(None, ('hid', 'tok'))
- grad_out_blocks: bfloat16 [128, 6, 256, 256], P('hid', None, 'tok')
- grad_out_left: bfloat16 [32768, 256], P(('hid', 'tok'))
- grad_out_right: bfloat16 [256, 8192], P(None, ('hid', 'tok'))
The draws below stay inside these ranges and needn't reach their ends.
Inputs may be any that keep to these rules, and one draw needn't show every extreme that they name: There is one whole number m, the same for every row, with in_lists[c, 0] = ((c * 8192) // 32768) XOR m, and in_lists[c, k] = in_lists[c, 0] XOR 2^(k-1) for k = 1 to 5. `out_lists`: the same butterfly form as in_lists, with its own number m, which differs from that of in_lists.
All inputs are finite; a program needn't handle non-finite values.
Results may differ from the reference program's by a relative error of at most 0.012.
Values may be sent and summed in bfloat16 or wider, within the bound.
A program may use at most 256 MiB of HBM per device.

```python
import jax
import jax.numpy as jnp
from jax import lax

D = 8192
FF = 32768
BLK = 256
LEVELS = 5
SLOTS = 6
RANK = 256
TOK_DEV = 224
TOKENS = 896
N_TOK = 4


def butterfly_codes(key):
    first_key, second_key = jax.random.split(key)
    code_one = jax.random.randint(first_key, (), 0, D // BLK, dtype=jnp.int32)
    offset = jax.random.randint(second_key, (), 1, D // BLK, dtype=jnp.int32)
    code_two = jnp.bitwise_xor(code_one, offset)
    return (code_one, code_two)


def butterfly_table(xor_code):
    hidden_ids = jnp.arange(FF // BLK, dtype=jnp.int32)
    base_ids = jnp.bitwise_xor(hidden_ids * D // FF, xor_code)
    powers = jnp.left_shift(jnp.ones((LEVELS,), jnp.int32), jnp.arange(LEVELS, dtype=jnp.int32))
    distances = jnp.concatenate([jnp.zeros((1,), jnp.int32), powers])
    return jnp.bitwise_xor(base_ids[:, None], distances[None, :]).astype(jnp.int32)


def draw_in_lists(key, part):
    code_one, code_two = butterfly_codes(jax.random.fold_in(key, 7))
    return butterfly_table(code_one)


def draw_out_lists(key, part):
    code_one, code_two = butterfly_codes(jax.random.fold_in(key, 7))
    return butterfly_table(code_two)


def block_scale(key, dims, cuts, low, high):
    factor_of, own = 1.0, jax.random.fold_in(key, 6)
    for axis_at, parts in cuts:
        heights = jnp.exp(jax.random.uniform(jax.random.fold_in(own, axis_at), (parts,), jnp.float32, low / len(cuts), high / len(cuts)))
        factor_of = factor_of * jnp.repeat(heights, dims[axis_at] // parts).reshape([-1 if axis == axis_at else 1 for axis in range(len(dims))])
    return factor_of


def bell_draw(key, extent, width, bound, cuts=(), kind=jnp.bfloat16):
    result = jax.random.normal(key, extent, jnp.float32) * width
    if len(cuts) > 0:
        result = block_scale(key, extent, cuts, -0.22, 0.18) * result
    return jnp.clip(result, min=-bound, max=bound).astype(kind)


def setup_inputs(seed: int = 0) -> dict:
    key_list = jax.random.split(jax.random.key(seed), 11)
    return {
        "tokens": bell_draw(key_list[0], (TOKENS, D), 1.0, 6.0, ((0, 4), (1, 8))),
        "in_blocks": bell_draw(key_list[1], (FF // BLK, SLOTS, BLK, BLK), (SLOTS * BLK) ** -0.5, 0.15625, ((0, 8), (2, 4))),
        "in_left": bell_draw(key_list[2], (D, RANK), D ** -0.5, 0.0625, ((0, 32),)),
        "in_right": bell_draw(key_list[3], (RANK, FF), RANK ** -0.5, 0.375, ((1, 32),)),
        "in_lists": draw_in_lists(jax.random.fold_in(key_list[10], 71), 0),
        "out_blocks": bell_draw(key_list[5], (FF // BLK, SLOTS, BLK, BLK), (4 * SLOTS * BLK) ** -0.5, 0.078125, ((0, 8), (2, 4))),
        "out_left": bell_draw(key_list[6], (FF, RANK), FF ** -0.5, 0.03125, ((0, 32),)),
        "out_right": bell_draw(key_list[7], (RANK, D), RANK ** -0.5, 0.375, ((1, 32),)),
        "out_lists": draw_out_lists(jax.random.fold_in(key_list[10], 71), 0),
        "cotangent": bell_draw(key_list[9], (TOKENS, D), 1.0, 6.0, ((0, 4), (1, 8))),
    }


def gelu_parts(preact):
    inner_coef = 0.7978845608028654
    cubic_coef = 0.044715
    inner_arg = inner_coef * (preact + cubic_coef * preact * preact * preact)
    tanh_val = jnp.tanh(inner_arg)
    active = 0.5 * preact * (1.0 + tanh_val)
    slopes = 0.5 * (1.0 + tanh_val) + 0.5 * preact * (1.0 - tanh_val * tanh_val) * inner_coef * (1.0 + 3.0 * cubic_coef * preact * preact)
    return (active, slopes)

def dot_rows(left_arr, right_arr):
    return lax.dot_general(left_arr, right_arr, (((0,), (0,)), ((), ())), preferred_element_type=jnp.float32)

def dot_cols(left_arr, right_arr):
    return lax.dot_general(left_arr, right_arr, (((1,), (1,)), ((), ())), preferred_element_type=jnp.float32)

def rounded(values):
    return lax.optimization_barrier(values.astype(jnp.bfloat16)).astype(jnp.float32)

def reference(tokens, in_blocks, in_left, in_right, in_lists, out_blocks, out_left, out_right, out_lists, cotangent):
    in_count = D // BLK
    hid_count = FF // BLK
    loss_scale = lax.rsqrt(jnp.float32(TOKENS))
    pick_in = (in_lists.T[:, :, None] == jnp.arange(in_count, dtype=jnp.int32)[None, None, :]).astype(jnp.float32)
    pick_out = (out_lists.T[:, :, None] == jnp.arange(in_count, dtype=jnp.int32)[None, None, :]).astype(jnp.float32)
    first_w = in_blocks.astype(jnp.float32)
    second_w = out_blocks.astype(jnp.float32)

    def one_group(running, pieces):
        tok_group, cot_group = pieces
        row_count = tok_group.shape[0]
        low_in = jnp.dot(tok_group, in_left, preferred_element_type=jnp.float32).astype(jnp.bfloat16)
        low_back = dot_cols(cot_group, out_right).astype(jnp.bfloat16)
        gathered = tok_group.reshape(row_count, in_count, BLK)[:, in_lists.T].astype(jnp.float32)
        preact = jnp.einsum('nshb,hsbf->nhf', gathered, first_w).reshape(row_count, FF)
        preact = preact + jnp.dot(low_in, in_right, preferred_element_type=jnp.float32)
        active, slopes = gelu_parts(preact)
        hidden = active.astype(jnp.bfloat16)
        low_mid = jnp.dot(hidden, out_left, preferred_element_type=jnp.float32).astype(jnp.bfloat16)
        hidden_f = hidden.astype(jnp.float32).reshape(row_count, hid_count, BLK)
        out_parts = jnp.einsum('nhf,hsfo->nsho', hidden_f, second_w)
        sparse_out = jnp.einsum('nsho,shc->nco', out_parts, pick_out, precision=lax.Precision.HIGHEST).reshape(row_count, D)
        layer_out = (sparse_out + jnp.dot(low_mid, out_right, preferred_element_type=jnp.float32)).astype(jnp.bfloat16)
        grad_in = cot_group.reshape(row_count, in_count, BLK)[:, out_lists.T].astype(jnp.float32)
        grad_hidden = jnp.einsum('nsho,hsfo->nhf', grad_in, second_w).reshape(row_count, FF)
        grad_hidden = grad_hidden + dot_cols(low_back, out_left)
        grad_pre = (grad_hidden * slopes).astype(jnp.bfloat16)
        low_grad = dot_cols(grad_pre, in_right).astype(jnp.bfloat16)
        grad_pre_f = grad_pre.astype(jnp.float32).reshape(row_count, hid_count, BLK)
        back_parts = jnp.einsum('nhf,hsbf->nshb', grad_pre_f, first_w)
        sparse_back = jnp.einsum('nshb,shc->ncb', back_parts, pick_in, precision=lax.Precision.HIGHEST).reshape(row_count, D)
        grad_tokens = (sparse_back + dot_cols(low_grad, in_left)).astype(jnp.bfloat16)
        terms = (rounded(loss_scale * jnp.einsum('nshb,nhf->hsbf', gathered, grad_pre_f)), rounded(loss_scale * jnp.einsum('nhf,nsho->hsfo', hidden_f, grad_in)), rounded(loss_scale * dot_rows(tok_group, low_grad)), rounded(loss_scale * dot_rows(low_in, grad_pre)), rounded(loss_scale * dot_rows(hidden, low_back)), rounded(loss_scale * dot_rows(low_mid, cot_group)))
        running = tuple((acc_val + new_val for acc_val, new_val in zip(running, terms)))
        return (running, (layer_out, grad_tokens))
    zero_sums = (jnp.zeros(in_blocks.shape, jnp.float32), jnp.zeros(out_blocks.shape, jnp.float32), jnp.zeros(in_left.shape, jnp.float32), jnp.zeros(in_right.shape, jnp.float32), jnp.zeros(out_left.shape, jnp.float32), jnp.zeros(out_right.shape, jnp.float32))
    grouped = (tokens.reshape(N_TOK, TOK_DEV, D), cotangent.reshape(N_TOK, TOK_DEV, D))
    sums, (outs_all, grads_all) = lax.scan(one_group, zero_sums, grouped)
    return (outs_all.reshape(TOKENS, D), grads_all.reshape(TOKENS, D), sums[0].astype(jnp.bfloat16), sums[2].astype(jnp.bfloat16), sums[3].astype(jnp.bfloat16), sums[1].astype(jnp.bfloat16), sums[4].astype(jnp.bfloat16), sums[5].astype(jnp.bfloat16))
```

```python
import jax
import jax.numpy as jnp
from jax import lax
from jax.experimental import pallas as pl
from jax.experimental.pallas import tpu as pltpu
from jax.sharding import PartitionSpec as P

D = 8192
BLK = 256


def gelu_parts(preact):
    inner_coef = 0.7978845608028654
    cubic_coef = 0.044715
    inner_arg = inner_coef * (preact + cubic_coef * preact * preact * preact)
    tanh_val = jnp.tanh(inner_arg)
    active = 0.5 * preact * (1.0 + tanh_val)
    slopes = 0.5 * (1.0 + tanh_val) + 0.5 * preact * (1.0 - tanh_val * tanh_val) * inner_coef * (
        1.0 + 3.0 * cubic_coef * preact * preact
    )
    return (active, slopes)


def dot_rows(left_arr, right_arr):
    return lax.dot_general(
        left_arr, right_arr, (((0,), (0,)), ((), ())), preferred_element_type=jnp.float32
    )


def dot_cols(left_arr, right_arr):
    return lax.dot_general(
        left_arr, right_arr, (((1,), (1,)), ((), ())), preferred_element_type=jnp.float32
    )


def rank_sum(values):
    return lax.psum(values, "hid")


def own_lists(lists, hid_blocks):
    return lax.dynamic_slice_in_dim(lists, lax.axis_index("hid") * hid_blocks, hid_blocks, 0)


def gather_in(values, lists, hid_blocks, blk_width):
    whole = lax.all_gather(values, "hid", axis=1, tiled=True)
    mine = own_lists(lists, hid_blocks)
    blocks = whole.reshape(whole.shape[0], whole.shape[1] // blk_width, blk_width)
    return jnp.stack(
        [
            jnp.stack(
                [
                    lax.dynamic_index_in_dim(blocks, mine[at, slot], axis=1, keepdims=False)
                    for at in range(hid_blocks)
                ],
                axis=1,
            )
            for slot in range(mine.shape[1])
        ],
        axis=1,
    )


def scatter_out(parts, lists, hid_blocks):
    mine = own_lists(lists, hid_blocks)
    picker = (mine.T[:, :, None] == jnp.arange(D // BLK, dtype=jnp.int32)[None, None, :]).astype(
        jnp.float32
    )
    dense = jnp.einsum("nsho,shc->nco", parts, picker, precision=lax.Precision.HIGHEST)
    return lax.psum_scatter(
        dense.reshape(dense.shape[0], -1), "hid", scatter_dimension=1, tiled=True
    )


def route_in(values, lists, hid_blocks, blk_width):
    return gather_in(values, lists, hid_blocks, blk_width)


def route_out(parts, lists, hid_blocks):
    return scatter_out(parts, lists, hid_blocks)


def local_gathered(
    tokens,
    in_blocks,
    in_left,
    in_right,
    in_lists,
    out_blocks,
    out_left,
    out_right,
    out_lists,
    cotangent,
):
    row_count, col_span = tokens.shape
    hid_blocks = in_blocks.shape[0]
    slot_count = in_blocks.shape[1]
    blk_width = in_blocks.shape[3]
    tok_count = lax.axis_size("tok")
    w_first, w_second, left_one, right_one, left_two, right_two = (
        lax.all_gather(in_blocks, "tok", axis=2, tiled=True),
        lax.all_gather(out_blocks, "tok", axis=2, tiled=True),
        lax.all_gather(in_left, "tok", axis=0, tiled=True),
        lax.all_gather(in_right, "tok", axis=1, tiled=True),
        lax.all_gather(out_left, "tok", axis=0, tiled=True),
        lax.all_gather(out_right, "tok", axis=1, tiled=True),
    )
    low_in, low_back = rank_sum(
        (
            jnp.dot(tokens, left_one, preferred_element_type=jnp.float32),
            dot_cols(cotangent, right_two),
        )
    )
    low_in = low_in.astype(jnp.bfloat16)
    low_back = low_back.astype(jnp.bfloat16)
    gathered = route_in(tokens, in_lists, hid_blocks, blk_width)
    group_count = gathered.shape[2]
    per_group = hid_blocks // group_count
    first_r = w_first.reshape(group_count, per_group, slot_count, blk_width, blk_width)
    second_r = w_second.reshape(group_count, per_group, slot_count, blk_width, blk_width)
    preact = jnp.einsum(
        "nseb,eqsbf->neqf", gathered, first_r, preferred_element_type=jnp.float32
    ).reshape(row_count, -1)
    preact = preact + jnp.dot(low_in, right_one, preferred_element_type=jnp.float32)
    active, slopes = gelu_parts(preact)
    hidden = active.astype(jnp.bfloat16)
    low_mid = rank_sum(jnp.dot(hidden, left_two, preferred_element_type=jnp.float32)).astype(
        jnp.bfloat16
    )
    hidden_r = hidden.reshape(row_count, group_count, per_group, blk_width)
    out_parts = jnp.einsum(
        "neqf,eqsfo->nseo", hidden_r, second_r, preferred_element_type=jnp.float32
    )
    sparse_out = route_out(out_parts, out_lists, hid_blocks)
    layer_out = (
        sparse_out + jnp.dot(low_mid, right_two, preferred_element_type=jnp.float32)
    ).astype(jnp.bfloat16)
    grad_in = route_in(cotangent, out_lists, hid_blocks, blk_width)
    grad_hidden = jnp.einsum(
        "nseo,eqsfo->neqf", grad_in, second_r, preferred_element_type=jnp.float32
    ).reshape(row_count, -1)
    grad_hidden = grad_hidden + dot_cols(low_back, left_two)
    grad_pre = (grad_hidden * slopes).astype(jnp.bfloat16)
    low_grad = rank_sum(dot_cols(grad_pre, right_one)).astype(jnp.bfloat16)
    grad_pre_r = grad_pre.reshape(row_count, group_count, per_group, blk_width)
    back_parts = jnp.einsum(
        "neqf,eqsbf->nseb", grad_pre_r, first_r, preferred_element_type=jnp.float32
    )
    sparse_back = route_out(back_parts, in_lists, hid_blocks)
    grad_tokens = (sparse_back + dot_cols(low_grad, left_one)).astype(jnp.bfloat16)
    loss_scale = lax.rsqrt(jnp.float32(row_count * tok_count))
    terms = (
        loss_scale
        * jnp.einsum(
            "nseb,neqf->eqsbf", gathered, grad_pre_r, preferred_element_type=jnp.float32
        ).reshape(w_first.shape),
        loss_scale
        * jnp.einsum(
            "neqf,nseo->eqsfo", hidden_r, grad_in, preferred_element_type=jnp.float32
        ).reshape(w_second.shape),
        loss_scale * dot_rows(tokens, low_grad),
        loss_scale * dot_rows(low_in, grad_pre),
        loss_scale * dot_rows(hidden, low_back),
        loss_scale * dot_rows(low_mid, cotangent),
    )
    shares = (
        lax.psum_scatter(
            terms[0].astype(jnp.bfloat16), "tok", scatter_dimension=2, tiled=True
        ).astype(jnp.float32),
        lax.psum_scatter(
            terms[1].astype(jnp.bfloat16), "tok", scatter_dimension=2, tiled=True
        ).astype(jnp.float32),
        lax.psum_scatter(
            terms[2].astype(jnp.bfloat16), "tok", scatter_dimension=0, tiled=True
        ).astype(jnp.float32),
        lax.psum_scatter(
            terms[3].astype(jnp.bfloat16), "tok", scatter_dimension=1, tiled=True
        ).astype(jnp.float32),
        lax.psum_scatter(
            terms[4].astype(jnp.bfloat16), "tok", scatter_dimension=0, tiled=True
        ).astype(jnp.float32),
        lax.psum_scatter(
            terms[5].astype(jnp.bfloat16), "tok", scatter_dimension=1, tiled=True
        ).astype(jnp.float32),
    )
    return (
        layer_out,
        grad_tokens,
        shares[0].astype(jnp.bfloat16),
        shares[2].astype(jnp.bfloat16),
        shares[3].astype(jnp.bfloat16),
        shares[1].astype(jnp.bfloat16),
        shares[4].astype(jnp.bfloat16),
        shares[5].astype(jnp.bfloat16),
    )


def in_group_shifts(count):
    return [0] + [1 << bit for bit in range(count.bit_length() - 1)]


def hid_shifts(count):
    return [1 << bit for bit in range(count.bit_length() - 1)]


def span(index, size):
    return pl.ds(pl.multiple_of(index * size, size), size)


def greet(partners):
    me_tok, me_hid = lax.axis_index("tok"), lax.axis_index("hid")
    barrier = pltpu.get_barrier_semaphore()
    for tok_dist, hid_dist in partners:
        pl.semaphore_signal(
            barrier,
            inc=1,
            device_id={"hid": me_hid ^ hid_dist, "tok": me_tok ^ tok_dist},
            device_id_type=pl.DeviceIdType.MESH,
        )
    pl.semaphore_wait(barrier, len(partners))


class Mover:
    def __init__(self, send, recv):
        self.send, self.recv, self.used = send, recv, 0
        self.open_copies = []

    def start(self, src, dst, tok_dist=0, hid_dist=0):
        at = self.used
        self.used += 1
        if tok_dist == 0 and hid_dist == 0:
            copy = pltpu.make_async_copy(src, dst, self.recv.at[at])
            copy.start()
            entry = [copy, True, False]
        else:
            copy = pltpu.make_async_remote_copy(
                src_ref=src,
                dst_ref=dst,
                send_sem=self.send.at[at],
                recv_sem=self.recv.at[at],
                device_id={
                    "hid": lax.axis_index("hid") ^ hid_dist,
                    "tok": lax.axis_index("tok") ^ tok_dist,
                },
                device_id_type=pl.DeviceIdType.MESH,
            )
            copy.start()
            entry = [copy, False, False]
        self.open_copies.append(entry)
        return entry

    def arrived(self, entry):
        if not entry[2]:
            if entry[1]:
                entry[0].wait()
            else:
                entry[0].wait_recv()
            entry[2] = True

    def finish(self):
        for entry in self.open_copies:
            self.arrived(entry)
        for entry in self.open_copies:
            if not entry[1]:
                entry[0].wait_send()


def double_sum(mover, far, totals, held):
    for pos, dist in enumerate(far):
        mover.arrived(mover.start(totals.at[pos], held.at[pos], 0, dist))
        totals[pos + 1] = totals[pos] + held[pos]
    return totals[len(far)]


def run_exchange(body, inputs, shapes, copies, ident, in_vmem=(), scratch=()):
    any_spec = pl.BlockSpec(memory_space=pl.ANY)
    return pl.pallas_call(
        body,
        out_shape=[jax.ShapeDtypeStruct(shape, jnp.bfloat16) for shape in shapes],
        in_specs=[
            pl.BlockSpec(memory_space=pltpu.VMEM) if at in in_vmem else any_spec
            for at in range(len(inputs))
        ],
        out_specs=[any_spec] * len(shapes),
        scratch_shapes=[
            pltpu.SemaphoreType.DMA((copies,)),
            pltpu.SemaphoreType.DMA((copies,)),
            *scratch,
        ],
        compiler_params=pltpu.CompilerParams(
            collective_id=ident, has_side_effects=True, vmem_limit_bytes=40 * 2**20
        ),
        cost_estimate=pl.CostEstimate(
            flops=0, bytes_accessed=200_000_000, transcendentals=0
        ),
    )(*inputs)


def gather_order(n_hid, turn):
    shifts = hid_shifts(n_hid)
    wide = shifts[1:]
    turn = turn % len(wide)
    return wide[turn:] + wide[:turn] + shifts[:1]


def tok_peers(n_tok):
    return [(dist, 0) for dist in range(1, n_tok)]


class Gather:
    def __init__(self, mover, src, dst, order):
        self.mover, self.src, self.dst, self.order = mover, src, dst, order
        self.have = {0: None}
        self.depth = 0
        mover.start(src, dst.at[0])
        for dist in order:
            self.have[dist] = mover.start(src, dst.at[dist], 0, dist)

    def relay(self):
        order = self.order
        for at, dist in enumerate(order[:-1]):
            for known in [
                sum(bits) for bits in subsets(order[:at])
            ]:
                held = known ^ dist
                self.mover.arrived(self.have[held])
                for later in order[at + 1 :]:
                    self.have[held ^ later] = self.mover.start(
                        self.dst.at[held], self.dst.at[held ^ later], 0, later
                    )


def subsets(items):
    found = [()]
    for item in items:
        found = found + [entry + (item,) for entry in found]
    return found


def weights_in(first_t, in_left, out_right, tokens, cotangent):
    n_tok, n_hid = lax.axis_size("tok"), lax.axis_size("hid")
    _, groups, slots, deep, blk = first_t.shape
    rank = in_left.shape[1]
    wide = in_left.shape[0]

    shifts = hid_shifts(n_hid)

    def body(
        first, left, right, tok, cot, first_o, left_o, right_o, tok_o, cot_o, send, recv
    ):
        me = lax.axis_index("tok")
        greet(tok_peers(n_tok) + [(0, dist) for dist in shifts])
        mover = Mover(send, recv)
        gathers = [
            Gather(mover, cot, cot_o, gather_order(n_hid, 0)),
            Gather(mover, tok, tok_o, gather_order(n_hid, 1)),
        ]
        for dist in (2, 3, 1, 0):
            for group in range(groups):
                mover.start(
                    first.at[me ^ dist, group],
                    first_o.at[group, :, span(me, deep), :],
                    dist,
                )
            mover.start(left, left_o.at[span(me, wide), :], dist)
            mover.start(right, right_o.at[:, span(me, wide)], dist)
        for gather in gathers:
            gather.relay()
        mover.finish()

    return run_exchange(
        body,
        (first_t, in_left, out_right, tokens, cotangent),
        [
            (groups, slots, deep * n_tok, blk),
            (wide * n_tok, rank),
            (rank, wide * n_tok),
            (n_hid,) + tokens.shape,
            (n_hid,) + cotangent.shape,
        ],
        (groups + 2) * n_tok + 2 * n_hid,
        1,
    )


def slots_in(low, group_in, group_cot, right_t, left_t):
    n_tok, n_hid = lax.axis_size("tok"), lax.axis_size("hid")
    rows, width = group_in.shape
    far = hid_shifts(n_hid)

    def body(
        low_i, in_i, cot_i, right_i, left_i, low_o, in_o, cot_o, right_o, left_o,
        send, recv, totals, held, low_sum,
    ):
        me = lax.axis_index("tok")
        greet(tok_peers(n_tok) + [(0, dist) for dist in far])
        mover = Mover(send, recv)
        pairs = ((cot_i, cot_o), (in_i, in_o))
        got = {}
        for dist in (2, 1, 0):
            for at, (src, dst) in enumerate(pairs):
                got[at, dist] = mover.start(src, dst.at[0, pl.ds(dist * rows, rows), :], dist)
        totals[0] = low_i[...]

        def spread(src, dst, dist):
            for pos, far_dist in enumerate(far):
                part = pl.ds(dist * rows, rows)
                mover.start(src, dst.at[1 + pos, part, :], 0, far_dist)

        for src, dst in pairs:
            spread(src, dst, 0)
        low_sum[...] = double_sum(mover, far, totals, held).astype(jnp.bfloat16)
        low_own = mover.start(low_sum, low_o.at[pl.ds(0, rows), :], 0)
        low_near = mover.start(low_sum, low_o.at[pl.ds(rows, rows), :], 1)
        low_far = mover.start(low_sum, low_o.at[pl.ds(2 * rows, rows), :], 2)
        for at, (_, dst) in enumerate(pairs):
            mover.arrived(got[at, 1])
            spread(dst.at[0, pl.ds(rows, rows), :], dst, 1)
        for at, (_, dst) in enumerate(pairs):
            mover.arrived(got[at, 2])
            have = dst.at[0, pl.ds(2 * rows, rows), :]
            got[at, 3] = mover.start(have, dst.at[0, pl.ds(3 * rows, rows), :], 1)
            spread(have, dst, 2)
        mover.arrived(low_far)
        mover.start(low_o.at[pl.ds(2 * rows, rows), :], low_o.at[pl.ds(3 * rows, rows), :], 1)
        for dist in (2, 3, 1, 0):
            mover.start(right_i.at[me ^ dist], right_o.at[me], dist)
            mover.start(left_i.at[:, me ^ dist], left_o.at[me], dist)
        for at, (_, dst) in enumerate(pairs):
            mover.arrived(got[at, 3])
            spread(dst.at[0, pl.ds(3 * rows, rows), :], dst, 3)
        mover.finish()

    whole = rows * n_tok
    places = 1 + len(far)
    _, rank, blk = right_t.shape
    return run_exchange(
        body,
        (low, group_in, group_cot, right_t, left_t),
        [
            (whole, low.shape[1]),
            (places, whole, width),
            (places, whole, width),
            (n_tok, rank, blk),
            (n_tok, left_t.shape[0], left_t.shape[2], rank),
        ],
        n_tok * (2 * (1 + len(far)) + 3) + len(far),
        2,
        (0,),
        (
            pltpu.VMEM((len(far) + 1,) + low.shape, jnp.float32),
            pltpu.VMEM((len(far),) + low.shape, jnp.float32),
            pltpu.VMEM(low.shape, jnp.bfloat16),
        ),
    )


def slots_out(low_parts, out_parts, back_parts, grads):
    n_tok, n_hid = lax.axis_size("tok"), lax.axis_size("hid")
    far = hid_shifts(n_hid)
    places, whole, wide = out_parts.shape
    rows = whole // n_tok
    width = low_parts.shape[1]
    count, slots, full, blk = grads.shape
    deep = full // n_tok

    def body(
        low_i, out_i, back_i, grad_i, low_o, sum_o, grad_o, send, recv,
        held, kept, got_one, pair, got_two, low_got, totals, low_held, low_sum,
    ):
        me = lax.axis_index("tok")
        greet(tok_peers(n_tok) + [(0, dist) for dist in far])
        mover = Mover(send, recv)
        srcs = (out_i, back_i)
        part = [pl.ds(dist * rows, rows) for dist in range(n_tok)]
        lows = [mover.start(low_i.at[part[dist], :], low_got.at[dist], dist) for dist in range(n_tok)]
        waits = {}
        for dist in (3, 1, 2, 0):
            for which, src in enumerate(srcs):
                for pos, far_dist in enumerate(far):
                    waits[dist, which, pos] = mover.start(
                        src.at[1 + pos, part[dist], :],
                        held.at[which, pos, part[dist], :],
                        0,
                        far_dist,
                    )
        for dist in (2, 3, 1, 0):
            for group in range(count):
                mover.start(
                    grad_i.at[group, :, span(me ^ dist, deep), :],
                    grad_o.at[me, group],
                    dist,
                )
        for entry in lows:
            mover.arrived(entry)
        totals[0] = sum(low_got[dist].astype(jnp.float32) for dist in range(n_tok))
        low_sum[...] = double_sum(mover, far, totals, low_held).astype(jnp.bfloat16)
        for dist in range(n_tok):
            mover.start(low_sum, low_o.at[part[dist], :], dist)
        first = {}
        for dist in (3, 1, 2, 0):
            for which, src in enumerate(srcs):
                total = src[0, part[dist], :].astype(jnp.float32)
                for pos in range(len(far)):
                    mover.arrived(waits[dist, which, pos])
                    total = total + held[which, pos, part[dist], :].astype(jnp.float32)
                kept[which, part[dist], :] = total.astype(jnp.bfloat16)
                if dist % 2 == 1:
                    first[which, dist - 1] = mover.start(
                        kept.at[which, part[dist], :], got_one.at[which, dist // 2], 1
                    )
        second = {}
        for which in range(2):
            mover.arrived(first[which, 2])
            pair[which] = (
                kept[which, part[2], :].astype(jnp.float32)
                + got_one[which, 1].astype(jnp.float32)
            ).astype(jnp.bfloat16)
            second[which] = mover.start(pair.at[which], got_two.at[which], 2)
        for which in range(2):
            mover.arrived(first[which, 0])
            mover.arrived(second[which])
            pair[which + 2] = (
                kept[which, part[0], :].astype(jnp.float32)
                + got_one[which, 0].astype(jnp.float32)
                + got_two[which].astype(jnp.float32)
            ).astype(jnp.bfloat16)
            mover.start(pair.at[which + 2], sum_o.at[which])
        mover.finish()

    return run_exchange(
        body,
        (low_parts, out_parts, back_parts, grads),
        [
            (whole, width),
            (2, rows, wide),
            (n_tok, count, slots, deep, blk),
        ],
        n_tok * (2 * len(far) + 2 + count) + len(far) + 8,
        3,
        (0, 1, 2),
        (
            pltpu.VMEM((2, len(far), whole, wide), jnp.bfloat16),
            pltpu.VMEM((2, whole, wide), jnp.bfloat16),
            pltpu.VMEM((2, 2, rows, wide), jnp.bfloat16),
            pltpu.VMEM((4, rows, wide), jnp.bfloat16),
            pltpu.VMEM((2, rows, wide), jnp.bfloat16),
            pltpu.VMEM((n_tok, rows, width), jnp.bfloat16),
            pltpu.VMEM((len(far) + 1, rows, width), jnp.float32),
            pltpu.VMEM((len(far), rows, width), jnp.float32),
            pltpu.VMEM((rows, width), jnp.bfloat16),
        ),
    )


def weights_out(grads, right_g, left_g, sums, low_grads):
    n_tok, n_hid = lax.axis_size("tok"), lax.axis_size("hid")
    shifts = hid_shifts(n_hid)
    count, slots, full, blk = grads.shape
    deep = full // n_tok
    rank = right_g.shape[1]
    _, per, fine, _ = left_g.shape

    def body(
        grad_i, right_i, left_i, sum_i, low_i, grad_o, right_o, left_o, sum_o, low_o, send, recv
    ):
        me = lax.axis_index("tok")
        greet(tok_peers(n_tok) + [(0, dist) for dist in shifts])
        mover = Mover(send, recv)
        gathers = [
            Gather(mover, src.at[which], dst.at[which], gather_order(n_hid, which))
            for src, dst in ((sum_i, sum_o), (low_i, low_o))
            for which in range(2)
        ]
        for dist in (2, 3, 1, 0):
            for group in range(count):
                mover.start(
                    grad_i.at[group, :, span(me ^ dist, deep), :],
                    grad_o.at[me, group],
                    dist,
                )
            mover.start(right_i.at[me ^ dist], right_o.at[me], dist)
            mover.start(left_i.at[me ^ dist], left_o.at[:, me], dist)
        for gather in gathers:
            gather.relay()
        mover.finish()

    return run_exchange(
        body,
        (grads, right_g, left_g, sums, low_grads),
        [
            (n_tok, count, slots, deep, blk),
            (n_tok, rank, blk),
            (per, n_tok, fine, rank),
            (2, n_hid) + sums.shape[1:],
            (2, n_hid) + low_grads.shape[1:],
        ],
        (count + 2) * n_tok + 4 * n_hid,
        4,
    )


def pick_group(whole, code, blk, n_tok):
    rows = whole.shape[1]
    return jnp.concatenate(
        [
            lax.dynamic_slice(
                whole,
                (code // n_tok, 0, (place ^ (code % n_tok)) * blk),
                (1, rows, blk),
            )[0]
            for place in range(n_tok)
        ],
        axis=1,
    )


def local_moved(
    tokens,
    in_blocks,
    in_left,
    in_right,
    in_lists,
    out_blocks,
    out_left,
    out_right,
    out_lists,
    cotangent,
):
    rows = tokens.shape[0]
    hid_blocks, slots, deep, blk = in_blocks.shape
    n_tok = lax.axis_size("tok")
    groups = tokens.shape[1] // blk
    per = hid_blocks // groups
    rank = in_left.shape[1]
    fine = blk // n_tok
    whole_rows = rows * n_tok
    code_in = in_lists[0, 0]
    code_out = out_lists[0, 0]
    first_t = (
        in_blocks.reshape(groups, per, slots, deep, n_tok, fine)
        .transpose(4, 0, 2, 3, 1, 5)
        .reshape(n_tok, groups, slots, deep, per * fine)
    )
    right_t = (
        in_right.reshape(rank, per, n_tok, fine)
        .transpose(2, 0, 1, 3)
        .reshape(n_tok, rank, per * fine)
    )
    second = (
        out_blocks.reshape(groups, per, slots, fine, blk)
        .transpose(0, 2, 1, 3, 4)
        .reshape(groups, slots, per * fine, blk)
    )
    first, left_one, right_two, all_tok, all_cot = weights_in(
        first_t, in_left, out_right, tokens, cotangent
    )
    group_in = pick_group(all_tok, code_in, blk, n_tok)
    group_cot = pick_group(all_cot, code_out, blk, n_tok)
    own_low = jnp.concatenate(
        [
            jnp.dot(tokens, left_one, preferred_element_type=jnp.float32),
            dot_cols(cotangent, right_two),
        ],
        axis=1,
    )
    low_all, x_in, x_cot, right_own, left_own = slots_in(
        own_low, group_in, group_cot, right_t, out_left.reshape(per, n_tok, fine, rank)
    )
    left_own = left_own.reshape(groups, per * fine, rank)
    low_in = low_all[:, :rank]
    low_back = low_all[:, rank:]

    def block(arr, group, slot):
        if slot < 3:
            place, at = 0, group ^ ((0, 1, 2)[slot])
        else:
            place, at = slot - 2, group
        return arr[place, :, at * blk : (at + 1) * blk]

    hidden_q, grad_q = [], []
    for group in range(groups):
        preact = sum(
            jnp.dot(block(x_in, group, k), first[group, k], preferred_element_type=jnp.float32)
            for k in range(slots)
        ) + jnp.dot(low_in, right_own[group], preferred_element_type=jnp.float32)
        active, slopes = gelu_parts(preact)
        hidden_q.append(active.astype(jnp.bfloat16))
        grad_hidden = sum(
            dot_cols(block(x_cot, group, k), second[group, k]) for k in range(slots)
        ) + dot_cols(low_back, left_own[group])
        grad_q.append((grad_hidden * slopes).astype(jnp.bfloat16))

    low_parts = jnp.concatenate(
        [
            sum(
                jnp.dot(hidden_q[at], left_own[at], preferred_element_type=jnp.float32)
                for at in range(groups)
            ),
            sum(dot_cols(grad_q[at], right_own[at]) for at in range(groups)),
        ],
        axis=1,
    ).astype(jnp.bfloat16)

    def contributions(values, weights, product):
        places = [
            jnp.concatenate(
                [
                    sum(
                        product(values[at ^ shift], weights[at ^ shift, k])
                        for k, shift in enumerate((0, 1, 2))
                    )
                    for at in range(groups)
                ],
                axis=1,
            )
        ]
        for k in range(3, slots):
            places.append(
                jnp.concatenate(
                    [product(values[at], weights[at, k]) for at in range(groups)], axis=1
                )
            )
        return jnp.stack(places).astype(jnp.bfloat16)

    def dot_plain(left_arr, right_arr):
        return jnp.dot(left_arr, right_arr, preferred_element_type=jnp.float32)

    out_parts = contributions(hidden_q, second, dot_plain)
    back_parts = contributions(grad_q, first, dot_cols)
    scale = lax.rsqrt(jnp.float32(whole_rows))
    grad_first = [
        jnp.stack(
            [
                (scale * dot_rows(block(x_in, at, k), grad_q[at])).astype(jnp.bfloat16)
                for k in range(slots)
            ]
        )
        for at in range(groups)
    ]
    half = groups // 2
    low_sum_all, sums, grad_one = slots_out(
        low_parts, out_parts, back_parts, jnp.stack(grad_first[:half])
    )
    me_tok = lax.axis_index("tok")
    own_in = lax.dynamic_slice(
        x_in[0], (0, (me_tok ^ (code_in % n_tok)) * blk), (whole_rows, blk)
    )
    own_cot = lax.dynamic_slice(
        x_cot[0], (0, (me_tok ^ (code_out % n_tok)) * blk), (whole_rows, blk)
    )
    low_grads = jnp.stack(
        [
            (scale * dot_rows(own_in, low_sum_all[:, rank:])).astype(jnp.bfloat16),
            (scale * dot_rows(low_sum_all[:, :rank], own_cot)).astype(jnp.bfloat16),
        ]
    )
    right_g = jnp.stack(
        [(scale * dot_rows(low_in, grad_q[at])).astype(jnp.bfloat16) for at in range(groups)]
    )
    left_g = jnp.stack(
        [(scale * dot_rows(hidden_q[at], low_back)).astype(jnp.bfloat16) for at in range(groups)]
    ).reshape(groups, per, fine, rank)
    grad_two, right_got, left_got, sums_all, low_got = weights_out(
        jnp.stack(grad_first[half:]), right_g, left_g, sums, low_grads
    )
    sparse_out = pick_group(sums_all[0], code_out, blk, n_tok)
    sparse_back = pick_group(sums_all[1], code_in, blk, n_tok)
    low_mid = low_sum_all[:rows, :rank]
    low_grad = low_sum_all[:rows, rank:]
    layer_out = (
        sparse_out.astype(jnp.float32)
        + jnp.dot(low_mid, right_two, preferred_element_type=jnp.float32)
    ).astype(jnp.bfloat16)
    grad_tokens = (sparse_back.astype(jnp.float32) + dot_cols(low_grad, left_one)).astype(
        jnp.bfloat16
    )
    grad_in_blocks = (
        jnp.concatenate([grad_one, grad_two], axis=1)
        .reshape(n_tok, groups, slots, deep, per, fine)
        .transpose(1, 4, 2, 3, 0, 5)
        .reshape(hid_blocks, slots, deep, blk)
    )
    grad_out_blocks = jnp.stack(
        [
            jnp.stack(
                [
                    (scale * dot_rows(hidden_q[at], block(x_cot, at, k)))
                    .astype(jnp.bfloat16)
                    .reshape(per, fine, blk)
                    for k in range(slots)
                ],
                axis=1,
            )
            for at in range(groups)
        ]
    ).reshape(hid_blocks, slots, fine, blk)
    grad_in_right = (
        right_got.reshape(n_tok, rank, per, fine).transpose(1, 2, 0, 3).reshape(in_right.shape)
    )
    grad_out_left = left_got.reshape(out_left.shape)
    return (
        layer_out,
        grad_tokens,
        grad_in_blocks,
        lax.dynamic_index_in_dim(low_got[0], code_in // n_tok, keepdims=False),
        grad_in_right,
        grad_out_blocks,
        grad_out_left,
        lax.dynamic_index_in_dim(low_got[1], code_out // n_tok, keepdims=False),
    )


def power_of_two(count):
    return count & (count - 1) == 0


def local(*arrays):
    tokens, in_blocks = arrays[0], arrays[1]
    n_tok = lax.axis_size("tok")
    n_hid = lax.axis_size("hid")
    whole_groups = (
        n_tok == 4
        and power_of_two(n_hid)
        and n_hid >= 4
        and tokens.shape[1] == n_tok * in_blocks.shape[3]
        and in_blocks.shape[0] == n_tok * n_tok
    )
    return local_moved(*arrays) if whole_groups else local_gathered(*arrays)


def solution(mesh):
    return jax.shard_map(
        local,
        mesh=mesh,
        in_specs=(
            P("tok", "hid"),
            P("hid", None, "tok", None),
            P(("hid", "tok"), None),
            P(None, ("hid", "tok")),
            P(),
            P("hid", None, "tok", None),
            P(("hid", "tok"), None),
            P(None, ("hid", "tok")),
            P(),
            P("tok", "hid"),
        ),
        out_specs=(
            P("tok", "hid"),
            P("tok", "hid"),
            P("hid", None, "tok", None),
            P(("hid", "tok"), None),
            P(None, ("hid", "tok")),
            P("hid", None, "tok", None),
            P(("hid", "tok"), None),
            P(None, ("hid", "tok")),
        ),
        check_vma=False,
    )
```

```python
import jax
import jax.numpy as jnp
from jax import lax
from jax.experimental import pallas as pl
from jax.experimental.pallas import tpu as pltpu
from jax.sharding import PartitionSpec as P

D = 8192
BLK = 256


def gelu_parts(preact):
    inner_coef = 0.7978845608028654
    cubic_coef = 0.044715
    inner_arg = inner_coef * (preact + cubic_coef * preact * preact * preact)
    tanh_val = jnp.tanh(inner_arg)
    active = 0.5 * preact * (1.0 + tanh_val)
    slopes = 0.5 * (1.0 + tanh_val) + 0.5 * preact * (1.0 - tanh_val * tanh_val) * inner_coef * (
        1.0 + 3.0 * cubic_coef * preact * preact
    )
    return (active, slopes)


def dot_rows(left_arr, right_arr):
    return lax.dot_general(
        left_arr, right_arr, (((0,), (0,)), ((), ())), preferred_element_type=jnp.float32
    )


def dot_cols(left_arr, right_arr):
    return lax.dot_general(
        left_arr, right_arr, (((1,), (1,)), ((), ())), preferred_element_type=jnp.float32
    )


def rank_sum(values):
    return lax.psum(values, "hid")


def own_lists(lists, hid_blocks):
    return lax.dynamic_slice_in_dim(lists, lax.axis_index("hid") * hid_blocks, hid_blocks, 0)


def gather_in(values, lists, hid_blocks, blk_width):
    whole = lax.all_gather(values, "hid", axis=1, tiled=True)
    mine = own_lists(lists, hid_blocks)
    blocks = whole.reshape(whole.shape[0], whole.shape[1] // blk_width, blk_width)
    return jnp.stack(
        [
            jnp.stack(
                [
                    lax.dynamic_index_in_dim(blocks, mine[at, slot], axis=1, keepdims=False)
                    for at in range(hid_blocks)
                ],
                axis=1,
            )
            for slot in range(mine.shape[1])
        ],
        axis=1,
    )


def scatter_out(parts, lists, hid_blocks):
    mine = own_lists(lists, hid_blocks)
    picker = (mine.T[:, :, None] == jnp.arange(D // BLK, dtype=jnp.int32)[None, None, :]).astype(
        jnp.float32
    )
    dense = jnp.einsum("nsho,shc->nco", parts, picker, precision=lax.Precision.HIGHEST)
    return lax.psum_scatter(
        dense.reshape(dense.shape[0], -1), "hid", scatter_dimension=1, tiled=True
    )


def route_in(values, lists, hid_blocks, blk_width):
    return gather_in(values, lists, hid_blocks, blk_width)


def route_out(parts, lists, hid_blocks):
    return scatter_out(parts, lists, hid_blocks)


def local_gathered(
    tokens,
    in_blocks,
    in_left,
    in_right,
    in_lists,
    out_blocks,
    out_left,
    out_right,
    out_lists,
    cotangent,
):
    row_count, col_span = tokens.shape
    hid_blocks = in_blocks.shape[0]
    slot_count = in_blocks.shape[1]
    blk_width = in_blocks.shape[3]
    tok_count = lax.axis_size("tok")
    w_first, w_second, left_one, right_one, left_two, right_two = (
        lax.all_gather(in_blocks, "tok", axis=2, tiled=True),
        lax.all_gather(out_blocks, "tok", axis=2, tiled=True),
        lax.all_gather(in_left, "tok", axis=0, tiled=True),
        lax.all_gather(in_right, "tok", axis=1, tiled=True),
        lax.all_gather(out_left, "tok", axis=0, tiled=True),
        lax.all_gather(out_right, "tok", axis=1, tiled=True),
    )
    low_in, low_back = rank_sum(
        (
            jnp.dot(tokens, left_one, preferred_element_type=jnp.float32),
            dot_cols(cotangent, right_two),
        )
    )
    low_in = low_in.astype(jnp.bfloat16)
    low_back = low_back.astype(jnp.bfloat16)
    gathered = route_in(tokens, in_lists, hid_blocks, blk_width)
    group_count = gathered.shape[2]
    per_group = hid_blocks // group_count
    first_r = w_first.reshape(group_count, per_group, slot_count, blk_width, blk_width)
    second_r = w_second.reshape(group_count, per_group, slot_count, blk_width, blk_width)
    preact = jnp.einsum(
        "nseb,eqsbf->neqf", gathered, first_r, preferred_element_type=jnp.float32
    ).reshape(row_count, -1)
    preact = preact + jnp.dot(low_in, right_one, preferred_element_type=jnp.float32)
    active, slopes = gelu_parts(preact)
    hidden = active.astype(jnp.bfloat16)
    low_mid = rank_sum(jnp.dot(hidden, left_two, preferred_element_type=jnp.float32)).astype(
        jnp.bfloat16
    )
    hidden_r = hidden.reshape(row_count, group_count, per_group, blk_width)
    out_parts = jnp.einsum(
        "neqf,eqsfo->nseo", hidden_r, second_r, preferred_element_type=jnp.float32
    )
    sparse_out = route_out(out_parts, out_lists, hid_blocks)
    layer_out = (
        sparse_out + jnp.dot(low_mid, right_two, preferred_element_type=jnp.float32)
    ).astype(jnp.bfloat16)
    grad_in = route_in(cotangent, out_lists, hid_blocks, blk_width)
    grad_hidden = jnp.einsum(
        "nseo,eqsfo->neqf", grad_in, second_r, preferred_element_type=jnp.float32
    ).reshape(row_count, -1)
    grad_hidden = grad_hidden + dot_cols(low_back, left_two)
    grad_pre = (grad_hidden * slopes).astype(jnp.bfloat16)
    low_grad = rank_sum(dot_cols(grad_pre, right_one)).astype(jnp.bfloat16)
    grad_pre_r = grad_pre.reshape(row_count, group_count, per_group, blk_width)
    back_parts = jnp.einsum(
        "neqf,eqsbf->nseb", grad_pre_r, first_r, preferred_element_type=jnp.float32
    )
    sparse_back = route_out(back_parts, in_lists, hid_blocks)
    grad_tokens = (sparse_back + dot_cols(low_grad, left_one)).astype(jnp.bfloat16)
    loss_scale = lax.rsqrt(jnp.float32(row_count * tok_count))
    terms = (
        loss_scale
        * jnp.einsum(
            "nseb,neqf->eqsbf", gathered, grad_pre_r, preferred_element_type=jnp.float32
        ).reshape(w_first.shape),
        loss_scale
        * jnp.einsum(
            "neqf,nseo->eqsfo", hidden_r, grad_in, preferred_element_type=jnp.float32
        ).reshape(w_second.shape),
        loss_scale * dot_rows(tokens, low_grad),
        loss_scale * dot_rows(low_in, grad_pre),
        loss_scale * dot_rows(hidden, low_back),
        loss_scale * dot_rows(low_mid, cotangent),
    )
    shares = (
        lax.psum_scatter(
            terms[0].astype(jnp.bfloat16), "tok", scatter_dimension=2, tiled=True
        ).astype(jnp.float32),
        lax.psum_scatter(
            terms[1].astype(jnp.bfloat16), "tok", scatter_dimension=2, tiled=True
        ).astype(jnp.float32),
        lax.psum_scatter(
            terms[2].astype(jnp.bfloat16), "tok", scatter_dimension=0, tiled=True
        ).astype(jnp.float32),
        lax.psum_scatter(
            terms[3].astype(jnp.bfloat16), "tok", scatter_dimension=1, tiled=True
        ).astype(jnp.float32),
        lax.psum_scatter(
            terms[4].astype(jnp.bfloat16), "tok", scatter_dimension=0, tiled=True
        ).astype(jnp.float32),
        lax.psum_scatter(
            terms[5].astype(jnp.bfloat16), "tok", scatter_dimension=1, tiled=True
        ).astype(jnp.float32),
    )
    return (
        layer_out,
        grad_tokens,
        shares[0].astype(jnp.bfloat16),
        shares[2].astype(jnp.bfloat16),
        shares[3].astype(jnp.bfloat16),
        shares[1].astype(jnp.bfloat16),
        shares[4].astype(jnp.bfloat16),
        shares[5].astype(jnp.bfloat16),
    )


def in_group_shifts(count):
    return [0] + [1 << bit for bit in range(count.bit_length() - 1)]


def hid_shifts(count):
    return [1 << bit for bit in range(count.bit_length() - 1)]


def span(index, size):
    return pl.ds(pl.multiple_of(index * size, size), size)


def greet(partners):
    me_tok, me_hid = lax.axis_index("tok"), lax.axis_index("hid")
    barrier = pltpu.get_barrier_semaphore()
    for tok_dist, hid_dist in partners:
        pl.semaphore_signal(
            barrier,
            inc=1,
            device_id={"hid": me_hid ^ hid_dist, "tok": me_tok ^ tok_dist},
            device_id_type=pl.DeviceIdType.MESH,
        )
    pl.semaphore_wait(barrier, len(partners))


class Mover:
    def __init__(self, send, recv):
        self.send, self.recv, self.used = send, recv, 0
        self.open_copies = []

    def start(self, src, dst, tok_dist=0, hid_dist=0):
        at = self.used
        self.used += 1
        if tok_dist == 0 and hid_dist == 0:
            copy = pltpu.make_async_copy(src, dst, self.recv.at[at])
            copy.start()
            entry = [copy, True, False]
        else:
            copy = pltpu.make_async_remote_copy(
                src_ref=src,
                dst_ref=dst,
                send_sem=self.send.at[at],
                recv_sem=self.recv.at[at],
                device_id={
                    "hid": lax.axis_index("hid") ^ hid_dist,
                    "tok": lax.axis_index("tok") ^ tok_dist,
                },
                device_id_type=pl.DeviceIdType.MESH,
            )
            copy.start()
            entry = [copy, False, False]
        self.open_copies.append(entry)
        return entry

    def arrived(self, entry):
        if not entry[2]:
            if entry[1]:
                entry[0].wait()
            else:
                entry[0].wait_recv()
            entry[2] = True

    def finish(self):
        for entry in self.open_copies:
            self.arrived(entry)
        for entry in self.open_copies:
            if not entry[1]:
                entry[0].wait_send()


def double_sum(mover, far, totals, held):
    for pos, dist in enumerate(far):
        mover.arrived(mover.start(totals.at[pos], held.at[pos], 0, dist))
        totals[pos + 1] = totals[pos] + held[pos]
    return totals[len(far)]


def run_exchange(
    body, inputs, shapes, copies, ident, in_vmem=(), scratch=(), in_smem=(), out_vmem=()
):
    any_spec = pl.BlockSpec(memory_space=pl.ANY)
    vmem_spec = pl.BlockSpec(memory_space=pltpu.VMEM)
    smem_spec = pl.BlockSpec(memory_space=pltpu.SMEM)
    return pl.pallas_call(
        body,
        out_shape=[jax.ShapeDtypeStruct(shape, jnp.bfloat16) for shape in shapes],
        in_specs=[
            vmem_spec if at in in_vmem else smem_spec if at in in_smem else any_spec
            for at in range(len(inputs))
        ],
        out_specs=[
            vmem_spec if at in out_vmem else any_spec for at in range(len(shapes))
        ],
        scratch_shapes=[
            pltpu.SemaphoreType.DMA((copies,)),
            pltpu.SemaphoreType.DMA((copies,)),
            *scratch,
        ],
        compiler_params=pltpu.CompilerParams(
            collective_id=ident, has_side_effects=True, vmem_limit_bytes=48 * 2**20
        ),
        cost_estimate=pl.CostEstimate(
            flops=0, bytes_accessed=200_000_000, transcendentals=0
        ),
    )(*inputs)


def gather_order(n_hid, turn):
    shifts = hid_shifts(n_hid)
    wide = shifts[1:]
    turn = turn % len(wide)
    return wide[turn:] + wide[:turn] + shifts[:1]


def tok_peers(n_tok):
    return [(dist, 0) for dist in range(1, n_tok)]


class Gather:
    def __init__(self, mover, src, dst, order):
        self.mover, self.src, self.dst, self.order = mover, src, dst, order
        self.have = {0: None}
        self.depth = 0
        self.own = mover.start(src, dst.at[0])
        for dist in order:
            self.have[dist] = mover.start(src, dst.at[dist], 0, dist)

    def relay(self):
        order = self.order
        for at, dist in enumerate(order[:-1]):
            for known in [
                sum(bits) for bits in subsets(order[:at])
            ]:
                held = known ^ dist
                self.mover.arrived(self.have[held])
                for later in order[at + 1 :]:
                    self.have[held ^ later] = self.mover.start(
                        self.dst.at[held], self.dst.at[held ^ later], 0, later
                    )


    def settle(self):
        self.mover.arrived(self.own)
        for entry in self.have.values():
            if entry is not None:
                self.mover.arrived(entry)


def subsets(items):
    found = [()]
    for item in items:
        found = found + [entry + (item,) for entry in found]
    return found


def swap_halves(first, second, odd):
    lane = lax.broadcasted_iota(jnp.int32, first.shape, 1)
    half = first.shape[1] // 2

    def turn(values):
        return jnp.concatenate([values[:, half:], values[:, :half]], axis=1)

    if odd:
        return jnp.where(lane < half, turn(first), second)
    return jnp.where(lane < half, first, turn(second))


def swap_pieces(values, count, places, in_major, out_major):
    rows, width = values.shape[-2:]
    lanes = 128

    def block(ref, at, lane):
        if ref.ndim == 2:
            return ref, (slice(None), pl.ds(at * (ref.shape[1] // count) + lane, lanes))
        lead = (0, at) if ref.shape[0] == 1 else (at, 0)
        return ref, lead + (slice(None), pl.ds(lane, lanes))

    def body(src, dst):
        def load(at, lane):
            ref, where = block(src, at, lane)
            return ref[where]

        for to in range(count):
            for pair in range(count // 2):
                lane = (to // 2) * lanes
                ref, where = block(dst, to, pair * lanes)
                ref[where] = swap_halves(
                    load(2 * pair, lane), load(2 * pair + 1, lane), to % 2 == 1
                )

    def spec(major):
        if major is None:
            full = (rows, width if values.ndim == 2 else width * count)
            return full, pl.BlockSpec(full, lambda at: (0, 0))
        piece = width if values.ndim == 4 else width // count
        if major:
            return (places, count, rows, piece), pl.BlockSpec(
                (1, count, rows, piece), lambda at: (at, 0, 0, 0)
            )
        return (count, places, rows, piece), pl.BlockSpec(
            (count, 1, rows, piece), lambda at: (0, at, 0, 0)
        )

    shape, out_spec = spec(out_major)
    return pl.pallas_call(
        body,
        grid=(places,),
        out_shape=jax.ShapeDtypeStruct(shape, values.dtype),
        in_specs=[spec(in_major)[1]],
        out_specs=out_spec,
        compiler_params=pltpu.CompilerParams(vmem_limit_bytes=24 * 2**20),
    )(values)


def choose(load, count, bits, turn=0):
    held = [load(at) for at in range(count)]
    for at, bit in enumerate(bits):
        want = 1 - ((turn >> at) & 1)
        held = [
            jnp.where(bit == want, held[pos + 1], held[pos]) for pos in range(0, len(held), 2)
        ]
    return held[0]


def code_bits(code_i, which, first, count):
    return [code_i[which, first + at] for at in range(count)]


def unpermute(dst, load, low_bits, high_bits, rows, blk, places, turn=0):
    step = 32

    def rows_of(at, carry):
        part = span(at, step)
        for place in range(places):
            held = [
                choose(lambda from_hid: load(from_hid, part, pos), 1 << len(high_bits), high_bits, turn)
                for pos in range(places)
            ] if place == 0 else held
            dst(part, place, choose(lambda pos: held[pos], places, low_bits, place))
        return carry

    lax.fori_loop(0, rows // step, rows_of, 0)


class LowSum:
    def __init__(self, mover, rows, n_tok, n_hid, parts, got, steps, taken, final):
        self.mover, self.n_tok, self.n_hid = mover, n_tok, n_hid
        self.rows, self.half = rows, rows // 2
        self.parts, self.got, self.steps, self.taken, self.final = parts, got, steps, taken, final

    def place(self, hid_index):
        chunk = lax.axis_index("tok") ^ (hid_index // 2)
        return pl.ds(
            pl.multiple_of(chunk * self.rows + (hid_index % 2) * self.half, self.half), self.half
        )

    def begin(self):
        me = lax.axis_index("hid")
        self.waits = [
            self.mover.start(
                self.parts.at[self.place(me ^ dist), :], self.got.at[dist], 0, dist
            )
            for dist in range(self.n_hid)
        ]

    def gather_parts(self):
        total = 0.0
        for dist in range(self.n_hid):
            self.mover.arrived(self.waits[dist])
            total = total + self.got[dist].astype(jnp.float32)
        self.steps[0] = total.astype(jnp.bfloat16)
        self.waits = [self.mover.start(self.steps.at[0], self.taken.at[0], 2)]

    def middle(self):
        self.mover.arrived(self.waits[0])
        self.steps[1] = (
            self.steps[0].astype(jnp.float32) + self.taken[0].astype(jnp.float32)
        ).astype(jnp.bfloat16)
        self.waits = [self.mover.start(self.steps.at[1], self.taken.at[1], 1)]

    def share(self):
        self.mover.arrived(self.waits[0])
        self.steps[2] = (
            self.steps[1].astype(jnp.float32) + self.taken[1].astype(jnp.float32)
        ).astype(jnp.bfloat16)
        me = lax.axis_index("hid")
        self.waits = [
            self.mover.start(self.steps.at[2], self.final.at[self.place(me), :], 0, dist)
            for dist in range(self.n_hid)
        ]

    def settle(self):
        for entry in self.waits:
            self.mover.arrived(entry)

    @staticmethod
    def copies(n_hid):
        return 2 * n_hid + 2

    @staticmethod
    def scratch(rows, width, n_tok, n_hid):
        half = rows // 2
        return (
            pltpu.VMEM((n_hid, half, width), jnp.bfloat16),
            pltpu.VMEM((3, half, width), jnp.bfloat16),
            pltpu.VMEM((2, half, width), jnp.bfloat16),
        )


def bring_in(
    tokens, cotangent, codes, in_left, out_right, first_t, right_t, left_t
):
    n_tok, n_hid = lax.axis_size("tok"), lax.axis_size("hid")
    _, groups, slots, deep, blk = first_t.shape
    wide, rank = in_left.shape
    rows, width = tokens.shape
    whole = rows * n_tok
    far = hid_shifts(n_hid)

    def body(
        tok_i, cot_i, code_i, left_i, right_i, first_i, r_i, l_i,
        first_o, pick_o, own_o, low_o, cot_o, in_o, r_o, l_o,
        send, recv, everyone, lefts, near, first_far, parts, got, steps, taken, final,
    ):
        me = lax.axis_index("tok")
        near_bits = n_tok.bit_length() - 1
        far_bits = n_hid.bit_length() - 1
        lows = [code_bits(code_i, which, 0, near_bits) for which in range(2)]
        highs = [code_bits(code_i, which, near_bits, far_bits) for which in range(2)]
        own_bits = [
            [bit ^ ((me >> at) & 1) for at, bit in enumerate(lows[which])] for which in range(2)
        ]
        greet([(dist, 0) for dist in range(1, n_tok)] + [(0, dist) for dist in range(1, n_hid)])
        mover = Mover(send, recv)
        part = [pl.ds(dist * rows, rows) for dist in range(n_tok)]
        outs = (cot_o, in_o)
        arrived = {}

        def send_first(group):
            for dist in (2, 3, 1, 0):
                mover.start(
                    first_i.at[me ^ dist, group], first_o.at[group, :, span(me, deep), :], dist
                )

        def pick(at, turn, store):
            unpermute(
                store,
                lambda from_hid, rows_at, pos: everyone[
                    at, from_hid, rows_at, pl.ds(pos * blk, blk)
                ],
                lows[at], highs[at], rows, blk, width // blk, turn,
            )

        def spread(at, dist):
            for pos, far_dist in enumerate(far):
                mover.start(
                    near.at[at, part[dist], :], outs[at].at[1 + pos, part[dist], :], 0, far_dist
                )
            mover.start(near.at[at, part[dist], :], outs[at].at[0, part[dist], :])

        for at, src in enumerate((cot_i, tok_i)):
            gather = Gather(mover, src, everyone.at[at], gather_order(n_hid, at))
            send_first(at)
            gather.relay()
            gather.settle()

            def store_near(rows_at, place, value):
                near[at, rows_at, pl.ds(place * blk, blk)] = value

            pick(at, 0, store_near)
            for dist in (1, 2):
                arrived[at, dist] = mover.start(
                    near.at[at, part[0], :], near.at[at, part[dist], :], dist
                )
        send_first(2)
        more = [
            Gather(mover, src, lefts.at[at], gather_order(n_hid, at))
            for at, src in enumerate((right_i, left_i))
        ]
        for at in range(2):
            for pos, far_dist in enumerate(far):

                def store_far(rows_at, place, value):
                    first_far[at, pos, rows_at, pl.ds(place * blk, blk)] = value

                pick(at, far_dist, store_far)
                mover.start(first_far.at[at, pos], outs[at].at[1 + pos, part[0], :])
            mover.start(near.at[at, part[0], :], outs[at].at[0, part[0], :])
        for at in range(2):
            mover.arrived(arrived[at, 1])
            spread(at, 1)
        for gather in more:
            gather.relay()
        for at in range(2):
            mover.arrived(arrived[at, 2])
            arrived[at, 3] = mover.start(
                near.at[at, part[2], :], near.at[at, part[3], :], 1
            )
            spread(at, 2)
        for group in range(3, groups):
            send_first(group)
        for at in range(2):
            more[at].settle()
            pick_o[at] = choose(lambda from_hid: lefts[at, from_hid], n_hid, highs[at])
        for dist in range(n_tok):
            for at in range(2):
                if dist == 3:
                    mover.arrived(arrived[at, 3])
                own_o[at, part[dist], :] = choose(
                    lambda pos: near[at, part[dist], pl.ds(pos * blk, blk)], n_tok, own_bits[at]
                )
            parts[part[dist], :rank] = jnp.dot(
                own_o[1, part[dist], :], pick_o[1], preferred_element_type=jnp.float32
            ).astype(jnp.bfloat16)
            parts[part[dist], rank:] = dot_cols(own_o[0, part[dist], :], pick_o[0]).astype(
                jnp.bfloat16
            )
        low = LowSum(mover, rows, n_tok, n_hid, parts, got, steps, taken, final)
        low.begin()
        spread(0, 3)
        low.gather_parts()
        low.middle()
        low.share()
        spread(1, 3)
        for dist in (2, 3, 1, 0):
            mover.start(r_i.at[me ^ dist], r_o.at[me], dist)
            mover.start(l_i.at[:, me ^ dist], l_o.at[me], dist)
        low.settle()
        low_o[...] = final[...]
        mover.finish()

    places = 1 + len(far)
    return run_exchange(
        body,
        (tokens, cotangent, codes, in_left, out_right, first_t, right_t, left_t),
        [
            (groups, slots, deep * n_tok, blk),
            (2, wide, rank),
            (2, whole, blk),
            (whole, 2 * rank),
            (places, whole, width),
            (places, whole, width),
            (n_tok, rank, blk),
            (n_tok, left_t.shape[0], left_t.shape[2], rank),
        ],
        4 * n_hid + groups * n_tok + 6 + 2 * n_tok * (1 + len(far)) + 2 * n_tok
        + LowSum.copies(n_hid),
        1,
        (0, 1, 3, 4),
        (
            pltpu.VMEM((2, n_hid, rows, width), jnp.bfloat16),
            pltpu.VMEM((2, n_hid, wide, rank), jnp.bfloat16),
            pltpu.VMEM((2, whole, width), jnp.bfloat16),
            pltpu.VMEM((2, len(far), rows, width), jnp.bfloat16),
            pltpu.VMEM((whole, 2 * rank), jnp.bfloat16),
        )
        + LowSum.scratch(rows, 2 * rank, n_tok, n_hid)
        + (pltpu.VMEM((whole, 2 * rank), jnp.bfloat16),),
        in_smem=(2,),
        out_vmem=(1, 2, 3),
    )


def send_out(
    low_parts, own_sums, codes, own, picks,
    out_far, back_far, grads, right_g, left_g,
):
    n_tok, n_hid = lax.axis_size("tok"), lax.axis_size("hid")
    far = hid_shifts(n_hid)
    _, whole, width = out_far.shape
    rows = whole // n_tok
    rank = picks.shape[2]
    groups, slots, full, blk = grads.shape
    deep = full // n_tok
    _, per, fine, _ = left_g.shape
    wide = picks.shape[1]

    def body(
        low_i, sum_i, code_i, own_i, pick_i,
        outf_i, backf_i, grad_i, r_i, l_i,
        layer_o, gtok_o, gleft_o, gright_o, grad_o, r_o, l_o,
        send, recv, held, kept, got_one, pair, got_two, low_grad, everyone, low_every, spots,
        low_got, steps, taken, low_all,
    ):
        me = lax.axis_index("tok")
        scale = lax.rsqrt(jnp.float32(whole))
        near_bits = n_tok.bit_length() - 1
        far_bits = n_hid.bit_length() - 1
        lows = [code_bits(code_i, which, 0, near_bits) for which in range(2)]
        highs = [code_bits(code_i, which, near_bits, far_bits) for which in range(2)]
        own_bits = [
            [bit ^ ((me >> at) & 1) for at, bit in enumerate(lows[which])] for which in range(2)
        ]
        greet([(dist, 0) for dist in range(1, n_tok)] + [(0, dist) for dist in range(1, n_hid)])
        mover = Mover(send, recv)
        part = [pl.ds(dist * rows, rows) for dist in range(n_tok)]
        fars = (outf_i, backf_i)
        low = LowSum(mover, rows, n_tok, n_hid, low_i, low_got, steps, taken, low_all)
        low.begin()
        waits = {}

        def send_far(which, dist):
            for pos, far_dist in enumerate(far):
                waits[which, dist, pos] = mover.start(
                    fars[which].at[pos, part[dist], :],
                    held.at[which, pos, part[dist], :],
                    0,
                    far_dist,
                )

        def send_grads(group):
            for dist in (2, 3, 1, 0):
                mover.start(
                    grad_i.at[group, :, span(me ^ dist, deep), :], grad_o.at[me, group], dist
                )

        first, second = {}, {}

        def settle(which, dist):
            total = sum_i[which, part[dist], :].astype(jnp.float32) + jnp.dot(
                low_all[part[dist], pl.ds(which * rank, rank)],
                spots[which],
                preferred_element_type=jnp.float32,
            )
            for pos in range(len(far)):
                mover.arrived(waits[which, dist, pos])
                total = total + held[which, pos, part[dist], :].astype(jnp.float32)
            kept[which, part[dist], :] = total.astype(jnp.bfloat16)
            if dist % 2 == 1:
                first[which, dist - 1] = mover.start(
                    kept.at[which, part[dist], :], got_one.at[which, dist // 2], 1
                )

        def pass_on(which):
            mover.arrived(first[which, 2])
            pair[which] = (
                kept[which, part[2], :].astype(jnp.float32)
                + got_one[which, 1].astype(jnp.float32)
            ).astype(jnp.bfloat16)
            second[which] = mover.start(pair.at[which], got_two.at[which], 2)

        def close(which):
            mover.arrived(first[which, 0])
            mover.arrived(second[which])
            pair[which + 2] = (
                kept[which, part[0], :].astype(jnp.float32)
                + got_one[which, 0].astype(jnp.float32)
                + got_two[which].astype(jnp.float32)
            ).astype(jnp.bfloat16)
            return Gather(mover, pair.at[which + 2], everyone.at[which], gather_order(n_hid, which))

        send_far(0, 3)
        for which in range(2):
            weight = pick_i[which].astype(jnp.float32)
            if which == 1:
                weight = weight.T
            for place in range(width // blk):
                here = 1
                for at, bit in enumerate(own_bits[which]):
                    here = here * (bit if (place >> at) & 1 else 1 - bit)
                spots[which, :, pl.ds(place * blk, blk)] = (
                    weight * here.astype(jnp.float32)
                ).astype(jnp.bfloat16)
        low.gather_parts()
        send_far(0, 1)
        low.middle()
        low.share()
        send_grads(0)
        send_far(0, 2)
        send_far(0, 0)
        low.settle()
        settle(0, 3)
        settle(0, 1)
        for dist in (3, 1, 2, 0):
            send_far(1, dist)
        settle(0, 2)
        pass_on(0)
        send_grads(1)
        settle(0, 0)
        low_grad[0] = (scale * dot_rows(low_all[:, :rank], own_i[0])).astype(jnp.bfloat16)
        low_grad[1] = (scale * dot_rows(own_i[1], low_all[:, rank:])).astype(jnp.bfloat16)
        settle(1, 3)
        settle(1, 1)
        gathers = [close(0)]
        settle(1, 2)
        pass_on(1)
        send_grads(2)
        gathers[0].relay()
        settle(1, 0)
        gathers.append(close(1))
        gathers += [
            Gather(mover, low_grad.at[which], low_every.at[which], gather_order(n_hid, which))
            for which in range(2)
        ]
        for group in range(3, groups):
            send_grads(group)
        for dist in (2, 3, 1, 0):
            mover.start(r_i.at[me ^ dist], r_o.at[me], dist)
            mover.start(l_i.at[me ^ dist], l_o.at[:, me], dist)
        for gather in gathers[1:]:
            gather.relay()
        for gather in gathers:
            gather.settle()
        gright_o[...] = choose(lambda from_hid: low_every[0, from_hid], n_hid, highs[0])
        gleft_o[...] = choose(lambda from_hid: low_every[1, from_hid], n_hid, highs[1])
        for which, dst in ((0, layer_o), (1, gtok_o)):

            def store_out(rows_at, place, value):
                dst[rows_at, pl.ds(place * blk, blk)] = value

            unpermute(
                store_out,
                lambda from_hid, rows_at, pos: everyone[
                    which, from_hid, rows_at, pl.ds(pos * blk, blk)
                ],
                lows[which], highs[which], rows, blk, width // blk,
            )
        mover.finish()

    return run_exchange(
        body,
        (
            low_parts, own_sums, codes, own, picks,
            out_far, back_far, grads, right_g, left_g,
        ),
        [
            (rows, width),
            (rows, width),
            (wide, rank),
            (rank, wide),
            (n_tok, groups, slots, deep, blk),
            (n_tok, rank, blk),
            (per, n_tok, fine, rank),
        ],
        n_tok * (2 * len(far) + groups + 2) + 8 + 4 * n_hid + LowSum.copies(n_hid),
        2,
        (0, 1, 3, 4),
        (
            pltpu.VMEM((2, len(far), whole, width), jnp.bfloat16),
            pltpu.VMEM((2, whole, width), jnp.bfloat16),
            pltpu.VMEM((2, 2, rows, width), jnp.bfloat16),
            pltpu.VMEM((4, rows, width), jnp.bfloat16),
            pltpu.VMEM((2, rows, width), jnp.bfloat16),
            pltpu.VMEM((2, wide, rank), jnp.bfloat16),
            pltpu.VMEM((2, n_hid, rows, width), jnp.bfloat16),
            pltpu.VMEM((2, n_hid, wide, rank), jnp.bfloat16),
            pltpu.VMEM((2, rank, width), jnp.bfloat16),
        )
        + LowSum.scratch(rows, 2 * rank, n_tok, n_hid)
        + (pltpu.VMEM((whole, 2 * rank), jnp.bfloat16),),
        in_smem=(2,),
        out_vmem=(0, 1, 2, 3),
    )


def work(x_in, x_cot, first, out_blocks, low_all, right_own, left_own):
    places, whole, width = x_in.shape
    groups, slots, blk, _ = first.shape
    per, fine = out_blocks.shape[0] // groups, out_blocks.shape[2]
    rank = right_own.shape[1]
    rows = whole // groups
    near = in_group_shifts(groups)

    def body(
        xin_i, xcot_i, first_i, second_i, low_i, r_i, l_i,
        own_o, outf_o, backf_o, low_o, gfirst_o, gsecond_o, gr_o, gl_o,
        own_sum, low_sum, hidden, slope,
    ):
        group = pl.program_id(0)
        scale = lax.rsqrt(jnp.float32(whole))

        @pl.when(group == 0)
        def _():
            own_sum[...] = jnp.zeros_like(own_sum)
            low_sum[...] = jnp.zeros_like(low_sum)

        def spot(k):
            if k < len(near):
                return 0, span(group ^ near[k], blk)
            return k - len(near) + 1, span(group, blk)

        def second(k):
            return second_i[:, k].reshape(per * fine, blk)

        left = l_i[0].reshape(per * fine, rank)

        def rows_of(at, carry):
            part = pl.ds(pl.multiple_of(at * rows, rows), rows)
            total = jnp.dot(low_i[part, :rank], r_i[0], preferred_element_type=jnp.float32)
            for k in range(slots):
                place, lanes = spot(k)
                total = total + jnp.dot(
                    xin_i[place, part, lanes], first_i[0, k], preferred_element_type=jnp.float32
                )
            active, slopes = gelu_parts(total)
            hid = active.astype(jnp.bfloat16)
            total = dot_cols(low_i[part, rank:], left)
            for k in range(slots):
                place, lanes = spot(k)
                total = total + dot_cols(xcot_i[place, part, lanes], second(k))
            pre = (total * slopes).astype(jnp.bfloat16)
            hidden[part, :] = hid
            slope[part, :] = pre
            low_sum[part, :rank] += jnp.dot(hid, left, preferred_element_type=jnp.float32)
            low_sum[part, rank:] += dot_cols(pre, r_i[0])
            for k in range(slots):
                out = jnp.dot(hid, second(k), preferred_element_type=jnp.float32)
                back = dot_cols(pre, first_i[0, k])
                if k < len(near):
                    _, lanes = spot(k)
                    own_sum[0, part, lanes] += out
                    own_sum[1, part, lanes] += back
                else:
                    outf_o[k - len(near), part, :] = out.astype(jnp.bfloat16)
                    backf_o[k - len(near), part, :] = back.astype(jnp.bfloat16)
            return carry

        lax.fori_loop(0, groups, rows_of, 0)
        for k in range(slots):
            place, lanes = spot(k)
            gfirst_o[0, k] = (scale * dot_rows(xin_i[place, :, lanes], slope[...])).astype(
                jnp.bfloat16
            )
            gsecond_o[:, k] = (
                (scale * dot_rows(hidden[...], xcot_i[place, :, lanes]))
                .astype(jnp.bfloat16)
                .reshape(per, fine, blk)
            )
        gr_o[0] = (scale * dot_rows(low_i[:, :rank], slope[...])).astype(jnp.bfloat16)
        gl_o[0] = (
            (scale * dot_rows(hidden[...], low_i[:, rank:]))
            .astype(jnp.bfloat16)
            .reshape(per, fine, rank)
        )

        @pl.when(group == groups - 1)
        def _():
            own_o[...] = own_sum[...].astype(jnp.bfloat16)
            low_o[...] = low_sum[...].astype(jnp.bfloat16)

    def once(shape):
        return pl.BlockSpec(
            shape, lambda at: (0,) * len(shape), pipeline_mode=pl.Buffered(1)
        )

    def each(*shape):
        return pl.BlockSpec((1,) + shape, lambda at: (at,) + (0,) * len(shape))

    def array(*shape):
        return jax.ShapeDtypeStruct(shape, jnp.bfloat16)

    second_spec = pl.BlockSpec((per, slots, fine, blk), lambda at: (at, 0, 0, 0))
    far_spec = pl.BlockSpec((places - 1, whole, blk), lambda at: (0, 0, at))
    return pl.pallas_call(
        body,
        grid=(groups,),
        in_specs=[
            once(x_in.shape),
            once(x_cot.shape),
            each(slots, blk, blk),
            second_spec,
            once(low_all.shape),
            each(rank, blk),
            each(per, fine, rank),
        ],
        out_shape=[
            array(2, whole, width),
            array(places - 1, whole, width),
            array(places - 1, whole, width),
            array(whole, 2 * rank),
            array(groups, slots, blk, blk),
            array(*out_blocks.shape),
            array(groups, rank, blk),
            array(groups, per, fine, rank),
        ],
        out_specs=[
            once((2, whole, width)),
            far_spec,
            far_spec,
            once((whole, 2 * rank)),
            each(slots, blk, blk),
            second_spec,
            each(rank, blk),
            each(per, fine, rank),
        ],
        scratch_shapes=[
            pltpu.VMEM((2, whole, width), jnp.float32),
            pltpu.VMEM((whole, 2 * rank), jnp.float32),
            pltpu.VMEM((whole, blk), jnp.bfloat16),
            pltpu.VMEM((whole, blk), jnp.bfloat16),
        ],
        compiler_params=pltpu.CompilerParams(vmem_limit_bytes=60 * 2**20),
    )(x_in, x_cot, first, out_blocks, low_all, right_own, left_own)


def local_moved(
    tokens,
    in_blocks,
    in_left,
    in_right,
    in_lists,
    out_blocks,
    out_left,
    out_right,
    out_lists,
    cotangent,
):
    hid_blocks, slots, deep, blk = in_blocks.shape
    n_tok = lax.axis_size("tok")
    groups = tokens.shape[1] // blk
    per = hid_blocks // groups
    rank = in_left.shape[1]
    fine = blk // n_tok
    heads = jnp.stack([out_lists, in_lists])[:, 0, 0]
    codes = (heads[:, None] >> jnp.arange(8, dtype=jnp.int32)[None, :]) & 1
    first_t = swap_pieces(
        in_blocks.reshape(groups, per, slots * deep, blk), per, groups, True, False
    ).reshape(n_tok, groups, slots, deep, blk)
    right_t = swap_pieces(in_right, per, 1, None, False).reshape(n_tok, rank, blk)
    first, picks, own, low_all, x_cot, x_in, right_own, left_own = bring_in(
        tokens,
        cotangent,
        codes,
        in_left,
        out_right,
        first_t,
        right_t,
        out_left.reshape(per, n_tok, fine, rank),
    )
    own_sums, out_far, back_far, low_parts, grad_first, grad_out_blocks, right_g, left_g = work(
        x_in, x_cot, first, out_blocks, low_all, right_own, left_own
    )
    layer_out, grad_tokens, grad_in_left, grad_out_right, grad_got, right_got, left_got = send_out(
        low_parts,
        own_sums,
        codes,
        own,
        picks,
        out_far,
        back_far,
        grad_first,
        right_g,
        left_g,
    )
    grad_in_blocks = swap_pieces(
        grad_got.reshape(n_tok, groups, slots * deep, blk), per, groups, False, True
    ).reshape(hid_blocks, slots, deep, blk)
    grad_in_right = swap_pieces(right_got.reshape(n_tok, 1, rank, blk), per, 1, False, None)
    return (
        layer_out,
        grad_tokens,
        grad_in_blocks,
        grad_in_left,
        grad_in_right,
        grad_out_blocks,
        left_got.reshape(out_left.shape),
        grad_out_right,
    )


def power_of_two(count):
    return count & (count - 1) == 0


def local(*arrays):
    tokens, in_blocks = arrays[0], arrays[1]
    n_tok = lax.axis_size("tok")
    n_hid = lax.axis_size("hid")
    whole_groups = (
        n_tok == 4
        and n_hid == 2 * n_tok
        and tokens.shape[1] == n_tok * in_blocks.shape[3]
        and in_blocks.shape[0] == n_tok * n_tok
    )
    return local_moved(*arrays) if whole_groups else local_gathered(*arrays)


def solution(mesh):
    return jax.shard_map(
        local,
        mesh=mesh,
        in_specs=(
            P("tok", "hid"),
            P("hid", None, "tok", None),
            P(("hid", "tok"), None),
            P(None, ("hid", "tok")),
            P(),
            P("hid", None, "tok", None),
            P(("hid", "tok"), None),
            P(None, ("hid", "tok")),
            P(),
            P("tok", "hid"),
        ),
        out_specs=(
            P("tok", "hid"),
            P("tok", "hid"),
            P("hid", None, "tok", None),
            P(("hid", "tok"), None),
            P(None, ("hid", "tok")),
            P("hid", None, "tok", None),
            P(("hid", "tok"), None),
            P(None, ("hid", "tok")),
        ),
        check_vma=False,
    )
```

```python
import jax
import jax.numpy as jnp
from jax import lax
from jax.experimental import pallas as pl
from jax.experimental.pallas import tpu as pltpu
from jax.sharding import PartitionSpec as P

D = 8192
BLK = 256


def gelu_parts(preact):
    inner_coef = 0.7978845608028654
    cubic_coef = 0.044715
    inner_arg = inner_coef * (preact + cubic_coef * preact * preact * preact)
    tanh_val = jnp.tanh(inner_arg)
    active = 0.5 * preact * (1.0 + tanh_val)
    slopes = 0.5 * (1.0 + tanh_val) + 0.5 * preact * (1.0 - tanh_val * tanh_val) * inner_coef * (
        1.0 + 3.0 * cubic_coef * preact * preact
    )
    return (active, slopes)


def dot_rows(left_arr, right_arr):
    return lax.dot_general(
        left_arr, right_arr, (((0,), (0,)), ((), ())), preferred_element_type=jnp.float32
    )


def dot_cols(left_arr, right_arr):
    return lax.dot_general(
        left_arr, right_arr, (((1,), (1,)), ((), ())), preferred_element_type=jnp.float32
    )


def rank_sum(values):
    return lax.psum(values, "hid")


def own_lists(lists, hid_blocks):
    return lax.dynamic_slice_in_dim(lists, lax.axis_index("hid") * hid_blocks, hid_blocks, 0)


def gather_in(values, lists, hid_blocks, blk_width):
    whole = lax.all_gather(values, "hid", axis=1, tiled=True)
    mine = own_lists(lists, hid_blocks)
    blocks = whole.reshape(whole.shape[0], whole.shape[1] // blk_width, blk_width)
    return jnp.stack(
        [
            jnp.stack(
                [
                    lax.dynamic_index_in_dim(blocks, mine[at, slot], axis=1, keepdims=False)
                    for at in range(hid_blocks)
                ],
                axis=1,
            )
            for slot in range(mine.shape[1])
        ],
        axis=1,
    )


def scatter_out(parts, lists, hid_blocks):
    mine = own_lists(lists, hid_blocks)
    picker = (mine.T[:, :, None] == jnp.arange(D // BLK, dtype=jnp.int32)[None, None, :]).astype(
        jnp.float32
    )
    dense = jnp.einsum("nsho,shc->nco", parts, picker, precision=lax.Precision.HIGHEST)
    return lax.psum_scatter(
        dense.reshape(dense.shape[0], -1), "hid", scatter_dimension=1, tiled=True
    )


def route_in(values, lists, hid_blocks, blk_width):
    return gather_in(values, lists, hid_blocks, blk_width)


def route_out(parts, lists, hid_blocks):
    return scatter_out(parts, lists, hid_blocks)


def local_gathered(
    tokens,
    in_blocks,
    in_left,
    in_right,
    in_lists,
    out_blocks,
    out_left,
    out_right,
    out_lists,
    cotangent,
):
    row_count, col_span = tokens.shape
    hid_blocks = in_blocks.shape[0]
    slot_count = in_blocks.shape[1]
    blk_width = in_blocks.shape[3]
    tok_count = lax.axis_size("tok")
    w_first, w_second, left_one, right_one, left_two, right_two = (
        lax.all_gather(in_blocks, "tok", axis=2, tiled=True),
        lax.all_gather(out_blocks, "tok", axis=2, tiled=True),
        lax.all_gather(in_left, "tok", axis=0, tiled=True),
        lax.all_gather(in_right, "tok", axis=1, tiled=True),
        lax.all_gather(out_left, "tok", axis=0, tiled=True),
        lax.all_gather(out_right, "tok", axis=1, tiled=True),
    )
    low_in, low_back = rank_sum(
        (
            jnp.dot(tokens, left_one, preferred_element_type=jnp.float32),
            dot_cols(cotangent, right_two),
        )
    )
    low_in = low_in.astype(jnp.bfloat16)
    low_back = low_back.astype(jnp.bfloat16)
    gathered = route_in(tokens, in_lists, hid_blocks, blk_width)
    group_count = gathered.shape[2]
    per_group = hid_blocks // group_count
    first_r = w_first.reshape(group_count, per_group, slot_count, blk_width, blk_width)
    second_r = w_second.reshape(group_count, per_group, slot_count, blk_width, blk_width)
    preact = jnp.einsum(
        "nseb,eqsbf->neqf", gathered, first_r, preferred_element_type=jnp.float32
    ).reshape(row_count, -1)
    preact = preact + jnp.dot(low_in, right_one, preferred_element_type=jnp.float32)
    active, slopes = gelu_parts(preact)
    hidden = active.astype(jnp.bfloat16)
    low_mid = rank_sum(jnp.dot(hidden, left_two, preferred_element_type=jnp.float32)).astype(
        jnp.bfloat16
    )
    hidden_r = hidden.reshape(row_count, group_count, per_group, blk_width)
    out_parts = jnp.einsum(
        "neqf,eqsfo->nseo", hidden_r, second_r, preferred_element_type=jnp.float32
    )
    sparse_out = route_out(out_parts, out_lists, hid_blocks)
    layer_out = (
        sparse_out + jnp.dot(low_mid, right_two, preferred_element_type=jnp.float32)
    ).astype(jnp.bfloat16)
    grad_in = route_in(cotangent, out_lists, hid_blocks, blk_width)
    grad_hidden = jnp.einsum(
        "nseo,eqsfo->neqf", grad_in, second_r, preferred_element_type=jnp.float32
    ).reshape(row_count, -1)
    grad_hidden = grad_hidden + dot_cols(low_back, left_two)
    grad_pre = (grad_hidden * slopes).astype(jnp.bfloat16)
    low_grad = rank_sum(dot_cols(grad_pre, right_one)).astype(jnp.bfloat16)
    grad_pre_r = grad_pre.reshape(row_count, group_count, per_group, blk_width)
    back_parts = jnp.einsum(
        "neqf,eqsbf->nseb", grad_pre_r, first_r, preferred_element_type=jnp.float32
    )
    sparse_back = route_out(back_parts, in_lists, hid_blocks)
    grad_tokens = (sparse_back + dot_cols(low_grad, left_one)).astype(jnp.bfloat16)
    loss_scale = lax.rsqrt(jnp.float32(row_count * tok_count))
    terms = (
        loss_scale
        * jnp.einsum(
            "nseb,neqf->eqsbf", gathered, grad_pre_r, preferred_element_type=jnp.float32
        ).reshape(w_first.shape),
        loss_scale
        * jnp.einsum(
            "neqf,nseo->eqsfo", hidden_r, grad_in, preferred_element_type=jnp.float32
        ).reshape(w_second.shape),
        loss_scale * dot_rows(tokens, low_grad),
        loss_scale * dot_rows(low_in, grad_pre),
        loss_scale * dot_rows(hidden, low_back),
        loss_scale * dot_rows(low_mid, cotangent),
    )
    shares = (
        lax.psum_scatter(
            terms[0].astype(jnp.bfloat16), "tok", scatter_dimension=2, tiled=True
        ).astype(jnp.float32),
        lax.psum_scatter(
            terms[1].astype(jnp.bfloat16), "tok", scatter_dimension=2, tiled=True
        ).astype(jnp.float32),
        lax.psum_scatter(
            terms[2].astype(jnp.bfloat16), "tok", scatter_dimension=0, tiled=True
        ).astype(jnp.float32),
        lax.psum_scatter(
            terms[3].astype(jnp.bfloat16), "tok", scatter_dimension=1, tiled=True
        ).astype(jnp.float32),
        lax.psum_scatter(
            terms[4].astype(jnp.bfloat16), "tok", scatter_dimension=0, tiled=True
        ).astype(jnp.float32),
        lax.psum_scatter(
            terms[5].astype(jnp.bfloat16), "tok", scatter_dimension=1, tiled=True
        ).astype(jnp.float32),
    )
    return (
        layer_out,
        grad_tokens,
        shares[0].astype(jnp.bfloat16),
        shares[2].astype(jnp.bfloat16),
        shares[3].astype(jnp.bfloat16),
        shares[1].astype(jnp.bfloat16),
        shares[4].astype(jnp.bfloat16),
        shares[5].astype(jnp.bfloat16),
    )


def in_group_shifts(count):
    return [0] + [1 << bit for bit in range(count.bit_length() - 1)]


def hid_shifts(count):
    return [1 << bit for bit in range(count.bit_length() - 1)]


def span(index, size):
    return pl.ds(pl.multiple_of(index * size, size), size)


def greet(partners):
    me_tok, me_hid = lax.axis_index("tok"), lax.axis_index("hid")
    barrier = pltpu.get_barrier_semaphore()
    for tok_dist, hid_dist in partners:
        pl.semaphore_signal(
            barrier,
            inc=1,
            device_id={"hid": me_hid ^ hid_dist, "tok": me_tok ^ tok_dist},
            device_id_type=pl.DeviceIdType.MESH,
        )
    pl.semaphore_wait(barrier, len(partners))


class Mover:
    def __init__(self, send, recv):
        self.send, self.recv, self.used = send, recv, 0
        self.open_copies = []

    def start(self, src, dst, tok_dist=0, hid_dist=0):
        at = self.used
        self.used += 1
        if tok_dist == 0 and hid_dist == 0:
            copy = pltpu.make_async_copy(src, dst, self.recv.at[at])
            copy.start()
            entry = [copy, True, False]
        else:
            copy = pltpu.make_async_remote_copy(
                src_ref=src,
                dst_ref=dst,
                send_sem=self.send.at[at],
                recv_sem=self.recv.at[at],
                device_id={
                    "hid": lax.axis_index("hid") ^ hid_dist,
                    "tok": lax.axis_index("tok") ^ tok_dist,
                },
                device_id_type=pl.DeviceIdType.MESH,
            )
            copy.start()
            entry = [copy, False, False]
        self.open_copies.append(entry)
        return entry

    def arrived(self, entry):
        if not entry[2]:
            if entry[1]:
                entry[0].wait()
            else:
                entry[0].wait_recv()
            entry[2] = True

    def finish(self):
        for entry in self.open_copies:
            self.arrived(entry)
        for entry in self.open_copies:
            if not entry[1]:
                entry[0].wait_send()


def double_sum(mover, far, totals, held):
    for pos, dist in enumerate(far):
        mover.arrived(mover.start(totals.at[pos], held.at[pos], 0, dist))
        totals[pos + 1] = totals[pos] + held[pos]
    return totals[len(far)]


def run_exchange(
    body, inputs, shapes, copies, ident, in_vmem=(), scratch=(), in_smem=(), out_vmem=()
):
    any_spec = pl.BlockSpec(memory_space=pl.ANY)
    vmem_spec = pl.BlockSpec(memory_space=pltpu.VMEM)
    smem_spec = pl.BlockSpec(memory_space=pltpu.SMEM)
    return pl.pallas_call(
        body,
        out_shape=[jax.ShapeDtypeStruct(shape, jnp.bfloat16) for shape in shapes],
        in_specs=[
            vmem_spec if at in in_vmem else smem_spec if at in in_smem else any_spec
            for at in range(len(inputs))
        ],
        out_specs=[
            vmem_spec if at in out_vmem else any_spec for at in range(len(shapes))
        ],
        scratch_shapes=[
            pltpu.SemaphoreType.DMA((copies,)),
            pltpu.SemaphoreType.DMA((copies,)),
            *scratch,
        ],
        compiler_params=pltpu.CompilerParams(
            collective_id=ident, has_side_effects=True, vmem_limit_bytes=48 * 2**20
        ),
        cost_estimate=pl.CostEstimate(
            flops=0, bytes_accessed=200_000_000, transcendentals=0
        ),
    )(*inputs)


def gather_order(n_hid, turn):
    shifts = hid_shifts(n_hid)
    wide = shifts[1:]
    turn = turn % len(wide)
    return wide[turn:] + wide[:turn] + shifts[:1]


def tok_peers(n_tok):
    return [(dist, 0) for dist in range(1, n_tok)]


class Route:
    def __init__(self, mover, src, got, held, bits):
        self.mover, self.src, self.got, self.held, self.bits = mover, src, got, held, bits
        top = len(bits) - 1
        self.orders = (
            (top, *range(1, top), 0),
            (*range(1, top), top, 0),
        )
        self.half = src.shape[0] // 2

    def part(self, at):
        return pl.ds(at * self.half, self.half)

    def current(self, stage):
        return self.src if stage == 0 else self.held.at[stage - 1]

    def send(self, stage):
        self.waits = [
            self.mover.start(
                self.current(stage).at[self.part(at), :],
                self.got.at[stage, self.part(at), :],
                0,
                1 << order[stage],
            )
            for at, order in enumerate(self.orders)
        ]

    def take(self, stage):
        for at, order in enumerate(self.orders):
            self.mover.arrived(self.waits[at])
            part = self.part(at)
            self.held[stage, part, :] = jnp.where(
                self.bits[order[stage]] == 1,
                self.got[stage, part, :],
                self.current(stage)[part, :],
            )


def route_all(routes, stages):
    for route in routes:
        route.send(0)
    for stage in range(stages):
        for route in routes:
            route.take(stage)
            if stage + 1 < stages:
                route.send(stage + 1)


def tok_peers(n_tok):
    return [(dist, 0) for dist in range(1, n_tok)]


class Gather:
    def __init__(self, mover, src, dst, order):
        self.mover, self.src, self.dst, self.order = mover, src, dst, order
        self.have = {0: None}
        self.depth = 0
        self.own = mover.start(src, dst.at[0])
        for dist in order:
            self.have[dist] = mover.start(src, dst.at[dist], 0, dist)

    def relay(self):
        order = self.order
        for at, dist in enumerate(order[:-1]):
            for known in [
                sum(bits) for bits in subsets(order[:at])
            ]:
                held = known ^ dist
                self.mover.arrived(self.have[held])
                for later in order[at + 1 :]:
                    self.have[held ^ later] = self.mover.start(
                        self.dst.at[held], self.dst.at[held ^ later], 0, later
                    )


    def settle(self):
        self.mover.arrived(self.own)
        for entry in self.have.values():
            if entry is not None:
                self.mover.arrived(entry)


def subsets(items):
    found = [()]
    for item in items:
        found = found + [entry + (item,) for entry in found]
    return found


def swap_halves(first, second, odd):
    lane = lax.broadcasted_iota(jnp.int32, first.shape, 1)
    half = first.shape[1] // 2

    def turn(values):
        return jnp.concatenate([values[:, half:], values[:, :half]], axis=1)

    if odd:
        return jnp.where(lane < half, turn(first), second)
    return jnp.where(lane < half, first, turn(second))


def swap_pieces(values, count, places, in_major, out_major):
    rows, width = values.shape[-2:]
    lanes = 128

    def block(ref, at, lane):
        if ref.ndim == 2:
            return ref, (slice(None), pl.ds(at * (ref.shape[1] // count) + lane, lanes))
        lead = (0, at) if ref.shape[0] == 1 else (at, 0)
        return ref, lead + (slice(None), pl.ds(lane, lanes))

    def body(src, dst):
        def load(at, lane):
            ref, where = block(src, at, lane)
            return ref[where]

        for to in range(count):
            for pair in range(count // 2):
                lane = (to // 2) * lanes
                ref, where = block(dst, to, pair * lanes)
                ref[where] = swap_halves(
                    load(2 * pair, lane), load(2 * pair + 1, lane), to % 2 == 1
                )

    def spec(major):
        if major is None:
            full = (rows, width if values.ndim == 2 else width * count)
            return full, pl.BlockSpec(full, lambda at: (0, 0))
        piece = width if values.ndim == 4 else width // count
        if major:
            return (places, count, rows, piece), pl.BlockSpec(
                (1, count, rows, piece), lambda at: (at, 0, 0, 0)
            )
        return (count, places, rows, piece), pl.BlockSpec(
            (count, 1, rows, piece), lambda at: (0, at, 0, 0)
        )

    shape, out_spec = spec(out_major)
    return pl.pallas_call(
        body,
        grid=(places,),
        out_shape=jax.ShapeDtypeStruct(shape, values.dtype),
        in_specs=[spec(in_major)[1]],
        out_specs=out_spec,
        compiler_params=pltpu.CompilerParams(vmem_limit_bytes=24 * 2**20),
    )(values)


def choose(load, count, bits, turn=0):
    held = [load(at) for at in range(count)]
    for at, bit in enumerate(bits):
        want = 1 - ((turn >> at) & 1)
        held = [
            jnp.where(bit == want, held[pos + 1], held[pos]) for pos in range(0, len(held), 2)
        ]
    return held[0]


def code_bits(code_i, which, first, count):
    return [code_i[which, first + at] for at in range(count)]


def swap_lanes(store, load, bits, rows, blk, places):
    step = 32

    def rows_of(at, carry):
        part = span(at, step)
        held = [load(part, pl.ds(pos * blk, blk)) for pos in range(places)]
        for place in range(places):
            store(
                part,
                pl.ds(place * blk, blk),
                choose(lambda pos: held[pos], places, bits, place),
            )
        return carry

    lax.fori_loop(0, rows // step, rows_of, 0)


class LowSum:
    def __init__(self, mover, n_tok, parts, core_got, mine, got, steps, taken, final):
        self.mover, self.n_tok = mover, n_tok
        self.parts, self.core_got, self.mine, self.got = parts, core_got, mine, got
        self.steps, self.taken, self.final = steps, taken, final
        self.me_hid = lax.axis_index("hid")
        self.core = self.me_hid % 2
        self.chips = [2 * dist for dist in range(1, n_tok)]

    def chunk(self, hid_index):
        return lax.axis_index("tok") ^ (hid_index // 2)

    def begin(self):
        self.waits = [self.mover.start(self.parts.at[:, 1 - self.core], self.core_got, 0, 1)]

    def fold_core(self):
        self.mover.arrived(self.waits[0])
        for at in range(self.n_tok):
            self.mine[at] = (self.parts[at, self.core] + self.core_got[at]).astype(jnp.bfloat16)
        self.waits = [
            self.mover.start(
                self.mine.at[self.chunk(self.me_hid ^ dist)], self.got.at[at], 0, dist
            )
            for at, dist in enumerate(self.chips)
        ]

    def gather_parts(self):
        total = self.mine[self.chunk(self.me_hid)].astype(jnp.float32)
        for at, entry in enumerate(self.waits):
            self.mover.arrived(entry)
            total = total + self.got[at].astype(jnp.float32)
        self.steps[0] = total.astype(jnp.bfloat16)
        self.waits = [self.mover.start(self.steps.at[0], self.taken.at[0], 2)]

    def step(self, at):
        self.mover.arrived(self.waits[0])
        self.steps[at] = (
            self.steps[at - 1].astype(jnp.float32) + self.taken[at - 1].astype(jnp.float32)
        ).astype(jnp.bfloat16)

    def middle(self):
        self.step(1)
        self.waits = [self.mover.start(self.steps.at[1], self.taken.at[1], 1)]

    def share(self):
        self.step(2)
        here = self.final.at[self.chunk(self.me_hid), self.core]
        self.waits = [
            self.mover.start(self.steps.at[2], here, 0, dist) for dist in [0] + self.chips
        ]

    def spread_core(self):
        for entry in self.waits:
            self.mover.arrived(entry)
        mine = self.final.at[:, self.core]
        self.waits = [self.mover.start(mine, mine, 0, 1)]

    def settle(self):
        self.mover.arrived(self.waits[0])

    def rows(self, dist, lanes):
        found = self.final[dist, :, :, lanes]
        return found.reshape(found.shape[0] * found.shape[1], found.shape[2])

    @staticmethod
    def copies(n_tok):
        return 2 * n_tok + 3

    @staticmethod
    def scratch(rows, width, n_tok):
        half = rows // 2
        return (
            pltpu.VMEM((n_tok, half, width), jnp.float32),
            pltpu.VMEM((n_tok, half, width), jnp.bfloat16),
            pltpu.VMEM((n_tok - 1, half, width), jnp.bfloat16),
            pltpu.VMEM((3, half, width), jnp.bfloat16),
            pltpu.VMEM((2, half, width), jnp.bfloat16),
            pltpu.VMEM((n_tok, 2, half, width), jnp.bfloat16),
        )


def bring_in(
    tokens, cotangent, codes, in_left, out_right, first_t, right_t, left_t
):
    n_tok, n_hid = lax.axis_size("tok"), lax.axis_size("hid")
    _, groups, slots, deep, blk = first_t.shape
    wide, rank = in_left.shape
    rows, width = tokens.shape
    whole = rows * n_tok
    far = hid_shifts(n_hid)

    def body(
        tok_i, cot_i, code_i, left_i, right_i, first_i, r_i, l_i,
        first_o, pick_o, own_o, low_o, cot_o, in_o, r_o, l_o,
        send, recv, got_mid, held_mid, got_low, held_low, near, parts,
        core_got, low_mine, low_got, steps, taken, final,
    ):
        me = lax.axis_index("tok")
        near_bits = n_tok.bit_length() - 1
        far_bits = n_hid.bit_length() - 1
        lows = [code_bits(code_i, which, 0, near_bits) for which in range(2)]
        highs = [code_bits(code_i, which, near_bits, far_bits) for which in range(2)]
        own_bits = [
            [bit ^ ((me >> at) & 1) for at, bit in enumerate(lows[which])] for which in range(2)
        ]
        greet(tok_peers(n_tok) + [(0, dist) for dist in (1, *range(2, n_hid, 2))])
        mover = Mover(send, recv)
        part = [pl.ds(dist * rows, rows) for dist in range(n_tok)]
        outs = (cot_o, in_o)
        arrived = {}

        def send_first(group):
            for dist in (2, 3, 1, 0):
                mover.start(
                    first_i.at[me ^ dist, group], first_o.at[group, :, span(me, deep), :], dist
                )

        def spread(at, dist):
            for pos, far_dist in enumerate(far):
                mover.start(
                    near.at[at, part[dist], :], outs[at].at[1 + pos, part[dist], :], 0, far_dist
                )
            mover.start(near.at[at, part[dist], :], outs[at].at[0, part[dist], :])

        routes = [
            Route(mover, src, got_mid.at[at], held_mid.at[at], highs[at])
            for at, src in enumerate((cot_i, tok_i))
        ]
        for route in routes:
            route.send(0)
        send_first(0)
        last = far_bits - 1
        for stage in range(far_bits):
            for at, route in enumerate(routes):
                route.take(stage)
                if stage < last:
                    route.send(stage + 1)
                    continue

                def store_near(rows_at, lanes, value):
                    near[at, rows_at, lanes] = value

                swap_lanes(
                    store_near,
                    lambda rows_at, lanes: held_mid[at, last, rows_at, lanes],
                    lows[at], rows, blk, width // blk,
                )
                for dist in (1, 2):
                    arrived[at, dist] = mover.start(
                        near.at[at, part[0], :], near.at[at, part[dist], :], dist
                    )
        for at in range(2):
            spread(at, 0)
        more = [
            Route(mover, src, got_low.at[at], held_low.at[at], highs[at])
            for at, src in enumerate((right_i, left_i))
        ]
        route_all(more, far_bits)
        for at in range(2):
            pick_o[at] = held_low[at, last]
        send_first(1)
        for at in range(2):
            mover.arrived(arrived[at, 1])
            spread(at, 1)
        for at in range(2):
            mover.arrived(arrived[at, 2])
            arrived[at, 3] = mover.start(
                near.at[at, part[2], :], near.at[at, part[3], :], 1
            )
        send_first(2)
        for at in range(2):
            spread(at, 2)
        half = rows // 2
        for dist in range(n_tok):
            for at in range(2):
                if dist == 3:
                    mover.arrived(arrived[at, 3])
                own_o[at, part[dist], :] = choose(
                    lambda pos: near[at, part[dist], pl.ds(pos * blk, blk)], n_tok, own_bits[at]
                )
            for side in range(2):
                piece = pl.ds(dist * rows + side * half, half)
                parts[dist, side, :, :rank] = jnp.dot(
                    own_o[1, piece, :], pick_o[1], preferred_element_type=jnp.float32
                )
                parts[dist, side, :, rank:] = dot_cols(own_o[0, piece, :], pick_o[0])
        low = LowSum(mover, n_tok, parts, core_got, low_mine, low_got, steps, taken, final)
        low.begin()
        low.fold_core()
        spread(0, 3)
        low.gather_parts()
        for group in range(3, groups):
            send_first(group)
        low.middle()
        spread(1, 3)
        low.share()
        for dist in (2, 3, 1, 0):
            mover.start(r_i.at[me ^ dist], r_o.at[me], dist)
            mover.start(l_i.at[:, me ^ dist], l_o.at[me], dist)
        low.spread_core()
        low.settle()
        for dist in range(n_tok):
            low_o[part[dist], :] = low.rows(dist, slice(None))
        mover.finish()

    places = 1 + len(far)
    return run_exchange(
        body,
        (tokens, cotangent, codes, in_left, out_right, first_t, right_t, left_t),
        [
            (groups, slots, deep * n_tok, blk),
            (2, wide, rank),
            (2, whole, blk),
            (whole, 2 * rank),
            (places, whole, width),
            (places, whole, width),
            (n_tok, rank, blk),
            (n_tok, left_t.shape[0], left_t.shape[2], rank),
        ],
        8 * len(far) + groups * n_tok + 6 + 2 * n_tok * (1 + len(far)) + 2 * n_tok
        + LowSum.copies(n_tok),
        1,
        (0, 1, 3, 4),
        (
            pltpu.VMEM((2, len(far), rows, width), jnp.bfloat16),
            pltpu.VMEM((2, len(far), rows, width), jnp.bfloat16),
            pltpu.VMEM((2, len(far), wide, rank), jnp.bfloat16),
            pltpu.VMEM((2, len(far), wide, rank), jnp.bfloat16),
            pltpu.VMEM((2, whole, width), jnp.bfloat16),
            pltpu.VMEM((n_tok, 2, rows // 2, 2 * rank), jnp.float32),
        )
        + LowSum.scratch(rows, 2 * rank, n_tok),
        in_smem=(2,),
        out_vmem=(1, 2, 3),
    )


def send_out(
    low_parts, own_sums, codes, own, picks,
    out_far, back_far, grads, right_g, left_g,
):
    n_tok, n_hid = lax.axis_size("tok"), lax.axis_size("hid")
    far = hid_shifts(n_hid)
    _, whole, width = out_far.shape
    rows = whole // n_tok
    rank = picks.shape[2]
    groups, slots, full, blk = grads.shape
    deep = full // n_tok
    _, per, fine, _ = left_g.shape
    wide = picks.shape[1]

    def body(
        low_i, sum_i, code_i, own_i, pick_i,
        outf_i, backf_i, grad_i, r_i, l_i,
        layer_o, gtok_o, gleft_o, gright_o, grad_o, r_o, l_o,
        send, recv, held, kept, got_one, pair, got_two, low_grad, spots,
        got_mid, held_mid, got_low, held_low,
        core_got, low_mine, low_got, steps, taken, final,
    ):
        me = lax.axis_index("tok")
        scale = lax.rsqrt(jnp.float32(whole))
        near_bits = n_tok.bit_length() - 1
        far_bits = n_hid.bit_length() - 1
        lows = [code_bits(code_i, which, 0, near_bits) for which in range(2)]
        highs = [code_bits(code_i, which, near_bits, far_bits) for which in range(2)]
        own_bits = [
            [bit ^ ((me >> at) & 1) for at, bit in enumerate(lows[which])] for which in range(2)
        ]
        greet(tok_peers(n_tok) + [(0, dist) for dist in (1, *range(2, n_hid, 2))])
        mover = Mover(send, recv)
        part = [pl.ds(dist * rows, rows) for dist in range(n_tok)]
        fars = (outf_i, backf_i)
        low = LowSum(mover, n_tok, low_i, core_got, low_mine, low_got, steps, taken, final)
        low.begin()
        waits = {}

        def send_far(which, dist):
            for pos, far_dist in enumerate(far):
                waits[which, dist, pos] = mover.start(
                    fars[which].at[pos, part[dist], :],
                    held.at[which, pos, part[dist], :],
                    0,
                    far_dist,
                )

        def send_grads(group):
            for dist in (2, 3, 1, 0):
                mover.start(
                    grad_i.at[group, :, span(me ^ dist, deep), :], grad_o.at[me, group], dist
                )

        first, second = {}, {}

        def settle(which, dist):
            total = sum_i[which, part[dist], :].astype(jnp.float32) + jnp.dot(
                low.rows(dist, pl.ds(which * rank, rank)),
                spots[which],
                preferred_element_type=jnp.float32,
            )
            for pos in range(len(far)):
                mover.arrived(waits[which, dist, pos])
                total = total + held[which, pos, part[dist], :].astype(jnp.float32)
            kept[which, part[dist], :] = total.astype(jnp.bfloat16)
            if dist % 2 == 1:
                first[which, dist - 1] = mover.start(
                    kept.at[which, part[dist], :], got_one.at[which, dist // 2], 1
                )

        def pass_on(which):
            mover.arrived(first[which, 2])
            pair[which] = (
                kept[which, part[2], :].astype(jnp.float32)
                + got_one[which, 1].astype(jnp.float32)
            ).astype(jnp.bfloat16)
            second[which] = mover.start(pair.at[which], got_two.at[which], 2)

        def close(which):
            mover.arrived(first[which, 0])
            mover.arrived(second[which])
            pair[which + 2] = (
                kept[which, part[0], :].astype(jnp.float32)
                + got_one[which, 0].astype(jnp.float32)
                + got_two[which].astype(jnp.float32)
            ).astype(jnp.bfloat16)
            route = Route(
                mover, pair.at[which + 2], got_mid.at[which], held_mid.at[which], highs[which]
            )
            route.send(0)
            return route

        send_grads(0)
        low.fold_core()
        send_far(0, 3)
        for which in range(2):
            weight = pick_i[which].astype(jnp.float32)
            if which == 1:
                weight = weight.T
            for place in range(width // blk):
                here = 1
                for at, bit in enumerate(own_bits[which]):
                    here = here * (bit if (place >> at) & 1 else 1 - bit)
                spots[which, :, pl.ds(place * blk, blk)] = (
                    weight * here.astype(jnp.float32)
                ).astype(jnp.bfloat16)
        low.gather_parts()
        send_far(0, 1)
        low.middle()
        send_far(0, 2)
        low.share()
        send_far(0, 0)
        send_grads(1)
        for dist in (2, 3, 1, 0):
            mover.start(r_i.at[me ^ dist], r_o.at[me], dist)
            mover.start(l_i.at[me ^ dist], l_o.at[:, me], dist)
        low.spread_core()
        low.settle()
        settle(0, 3)
        settle(0, 1)
        send_grads(2)
        for dist in (3, 1, 2, 0):
            send_far(1, dist)
        settle(0, 2)
        pass_on(0)
        settle(0, 0)
        low_mid = jnp.concatenate([low.rows(dist, pl.ds(0, rank)) for dist in range(n_tok)], axis=0)
        low_grad[0] = (scale * dot_rows(low_mid, own_i[0])).astype(jnp.bfloat16)
        low_back = jnp.concatenate(
            [low.rows(dist, pl.ds(rank, rank)) for dist in range(n_tok)], axis=0
        )
        low_grad[1] = (scale * dot_rows(own_i[1], low_back)).astype(jnp.bfloat16)
        settle(1, 3)
        settle(1, 1)
        routes = [close(0)]
        more = [
            Route(mover, low_grad.at[which], got_low.at[which], held_low.at[which], highs[which])
            for which in range(2)
        ]
        for route in more:
            route.send(0)
        settle(1, 2)
        pass_on(1)
        settle(1, 0)

        def advance(route, stage):
            route.take(stage)
            if stage + 1 < far_bits:
                route.send(stage + 1)

        last = far_bits - 1
        for stage in range(far_bits):
            for route in routes + more:
                advance(route, stage)
        routes.append(close(1))
        send_grads(3)
        gright_o[...] = held_low[0, last]
        gleft_o[...] = held_low[1, last]
        outs = (layer_o, gtok_o)
        for which in range(2):
            if which == 1:
                for stage in range(far_bits):
                    advance(routes[1], stage)

            def store_out(rows_at, lanes, value):
                outs[which][rows_at, lanes] = value

            swap_lanes(
                store_out,
                lambda rows_at, lanes: held_mid[which, last, rows_at, lanes],
                lows[which], rows, blk, width // blk,
            )
        mover.finish()

    return run_exchange(
        body,
        (
            low_parts, own_sums, codes, own, picks,
            out_far, back_far, grads, right_g, left_g,
        ),
        [
            (rows, width),
            (rows, width),
            (wide, rank),
            (rank, wide),
            (n_tok, groups, slots, deep, blk),
            (n_tok, rank, blk),
            (per, n_tok, fine, rank),
        ],
        n_tok * (2 * len(far) + groups + 2) + 8 + 8 * len(far) + LowSum.copies(n_tok),
        2,
        (0, 1, 3, 4),
        (
            pltpu.VMEM((2, len(far), whole, width), jnp.bfloat16),
            pltpu.VMEM((2, whole, width), jnp.bfloat16),
            pltpu.VMEM((2, 2, rows, width), jnp.bfloat16),
            pltpu.VMEM((4, rows, width), jnp.bfloat16),
            pltpu.VMEM((2, rows, width), jnp.bfloat16),
            pltpu.VMEM((2, wide, rank), jnp.bfloat16),
            pltpu.VMEM((2, rank, width), jnp.bfloat16),
            pltpu.VMEM((2, len(far), rows, width), jnp.bfloat16),
            pltpu.VMEM((2, len(far), rows, width), jnp.bfloat16),
            pltpu.VMEM((2, len(far), wide, rank), jnp.bfloat16),
            pltpu.VMEM((2, len(far), wide, rank), jnp.bfloat16),
        )
        + LowSum.scratch(rows, 2 * rank, n_tok),
        in_smem=(2,),
        out_vmem=(0, 1, 2, 3),
    )


def work(x_in, x_cot, first, out_blocks, low_all, right_own, left_own):
    places, whole, width = x_in.shape
    groups, slots, blk, _ = first.shape
    per, fine = out_blocks.shape[0] // groups, out_blocks.shape[2]
    rank = right_own.shape[1]
    rows = whole // groups
    near = in_group_shifts(groups)

    def body(
        xin_i, xcot_i, first_i, second_i, low_i, r_i, l_i,
        own_o, outf_o, backf_o, low_o, gfirst_o, gsecond_o, gr_o, gl_o,
        own_sum, low_sum, hidden, slope,
    ):
        group = pl.program_id(0)
        scale = lax.rsqrt(jnp.float32(whole))

        @pl.when(group == 0)
        def _():
            own_sum[...] = jnp.zeros_like(own_sum)
            low_sum[...] = jnp.zeros_like(low_sum)

        def spot(k):
            if k < len(near):
                return 0, span(group ^ near[k], blk)
            return k - len(near) + 1, span(group, blk)

        def second(k):
            return second_i[:, k].reshape(per * fine, blk)

        left = l_i[0].reshape(per * fine, rank)

        def rows_of(at, carry):
            part = pl.ds(pl.multiple_of(at * rows, rows), rows)
            total = jnp.dot(low_i[part, :rank], r_i[0], preferred_element_type=jnp.float32)
            for k in range(slots):
                place, lanes = spot(k)
                total = total + jnp.dot(
                    xin_i[place, part, lanes], first_i[0, k], preferred_element_type=jnp.float32
                )
            active, slopes = gelu_parts(total)
            hid = active.astype(jnp.bfloat16)
            total = dot_cols(low_i[part, rank:], left)
            for k in range(slots):
                place, lanes = spot(k)
                total = total + dot_cols(xcot_i[place, part, lanes], second(k))
            pre = (total * slopes).astype(jnp.bfloat16)
            hidden[part, :] = hid
            slope[part, :] = pre
            low_sum[part, :rank] += jnp.dot(hid, left, preferred_element_type=jnp.float32)
            low_sum[part, rank:] += dot_cols(pre, r_i[0])
            for k in range(slots):
                out = jnp.dot(hid, second(k), preferred_element_type=jnp.float32)
                back = dot_cols(pre, first_i[0, k])
                if k < len(near):
                    _, lanes = spot(k)
                    own_sum[0, part, lanes] += out
                    own_sum[1, part, lanes] += back
                else:
                    outf_o[k - len(near), part, :] = out.astype(jnp.bfloat16)
                    backf_o[k - len(near), part, :] = back.astype(jnp.bfloat16)
            return carry

        lax.fori_loop(0, groups, rows_of, 0)
        for k in range(slots):
            place, lanes = spot(k)
            gfirst_o[0, k] = (scale * dot_rows(xin_i[place, :, lanes], slope[...])).astype(
                jnp.bfloat16
            )
            gsecond_o[:, k] = (
                (scale * dot_rows(hidden[...], xcot_i[place, :, lanes]))
                .astype(jnp.bfloat16)
                .reshape(per, fine, blk)
            )
        gr_o[0] = (scale * dot_rows(low_i[:, :rank], slope[...])).astype(jnp.bfloat16)
        gl_o[0] = (
            (scale * dot_rows(hidden[...], low_i[:, rank:]))
            .astype(jnp.bfloat16)
            .reshape(per, fine, rank)
        )

        @pl.when(group == groups - 1)
        def _():
            own_o[...] = own_sum[...].astype(jnp.bfloat16)
            low_o[...] = low_sum[...]

    def once(shape):
        return pl.BlockSpec(
            shape, lambda at: (0,) * len(shape), pipeline_mode=pl.Buffered(1)
        )

    def each(*shape):
        return pl.BlockSpec((1,) + shape, lambda at: (at,) + (0,) * len(shape))

    def array(*shape):
        return jax.ShapeDtypeStruct(shape, jnp.bfloat16)

    second_spec = pl.BlockSpec((per, slots, fine, blk), lambda at: (at, 0, 0, 0))
    far_spec = pl.BlockSpec((places - 1, whole, blk), lambda at: (0, 0, at))
    return pl.pallas_call(
        body,
        grid=(groups,),
        in_specs=[
            once(x_in.shape),
            once(x_cot.shape),
            each(slots, blk, blk),
            second_spec,
            once(low_all.shape),
            each(rank, blk),
            each(per, fine, rank),
        ],
        out_shape=[
            array(2, whole, width),
            array(places - 1, whole, width),
            array(places - 1, whole, width),
            jax.ShapeDtypeStruct((whole, 2 * rank), jnp.float32),
            array(groups, slots, blk, blk),
            array(*out_blocks.shape),
            array(groups, rank, blk),
            array(groups, per, fine, rank),
        ],
        out_specs=[
            once((2, whole, width)),
            far_spec,
            far_spec,
            once((whole, 2 * rank)),
            each(slots, blk, blk),
            second_spec,
            each(rank, blk),
            each(per, fine, rank),
        ],
        scratch_shapes=[
            pltpu.VMEM((2, whole, width), jnp.float32),
            pltpu.VMEM((whole, 2 * rank), jnp.float32),
            pltpu.VMEM((whole, blk), jnp.bfloat16),
            pltpu.VMEM((whole, blk), jnp.bfloat16),
        ],
        compiler_params=pltpu.CompilerParams(vmem_limit_bytes=60 * 2**20),
    )(x_in, x_cot, first, out_blocks, low_all, right_own, left_own)


def local_moved(
    tokens,
    in_blocks,
    in_left,
    in_right,
    in_lists,
    out_blocks,
    out_left,
    out_right,
    out_lists,
    cotangent,
):
    hid_blocks, slots, deep, blk = in_blocks.shape
    n_tok = lax.axis_size("tok")
    groups = tokens.shape[1] // blk
    per = hid_blocks // groups
    rank = in_left.shape[1]
    fine = blk // n_tok
    heads = jnp.stack([out_lists, in_lists])[:, 0, 0]
    codes = (heads[:, None] >> jnp.arange(8, dtype=jnp.int32)[None, :]) & 1
    first_t = swap_pieces(
        in_blocks.reshape(groups, per, slots * deep, blk), per, groups, True, False
    ).reshape(n_tok, groups, slots, deep, blk)
    right_t = swap_pieces(in_right, per, 1, None, False).reshape(n_tok, rank, blk)
    first, picks, own, low_all, x_cot, x_in, right_own, left_own = bring_in(
        tokens,
        cotangent,
        codes,
        in_left,
        out_right,
        first_t,
        right_t,
        out_left.reshape(per, n_tok, fine, rank),
    )
    own_sums, out_far, back_far, low_parts, grad_first, grad_out_blocks, right_g, left_g = work(
        x_in, x_cot, first, out_blocks, low_all, right_own, left_own
    )
    layer_out, grad_tokens, grad_in_left, grad_out_right, grad_got, right_got, left_got = send_out(
        low_parts.reshape(n_tok, 2, tokens.shape[0] // 2, 2 * rank),
        own_sums,
        codes,
        own,
        picks,
        out_far,
        back_far,
        grad_first,
        right_g,
        left_g,
    )
    grad_in_blocks = swap_pieces(
        grad_got.reshape(n_tok, groups, slots * deep, blk), per, groups, False, True
    ).reshape(hid_blocks, slots, deep, blk)
    grad_in_right = swap_pieces(right_got.reshape(n_tok, 1, rank, blk), per, 1, False, None)
    return (
        layer_out,
        grad_tokens,
        grad_in_blocks,
        grad_in_left,
        grad_in_right,
        grad_out_blocks,
        left_got.reshape(out_left.shape),
        grad_out_right,
    )


def power_of_two(count):
    return count & (count - 1) == 0


def local(*arrays):
    tokens, in_blocks = arrays[0], arrays[1]
    n_tok = lax.axis_size("tok")
    n_hid = lax.axis_size("hid")
    whole_groups = (
        n_tok == 4
        and n_hid == 2 * n_tok
        and tokens.shape[1] == n_tok * in_blocks.shape[3]
        and in_blocks.shape[0] == n_tok * n_tok
    )
    return local_moved(*arrays) if whole_groups else local_gathered(*arrays)


def solution(mesh):
    return jax.shard_map(
        local,
        mesh=mesh,
        in_specs=(
            P("tok", "hid"),
            P("hid", None, "tok", None),
            P(("hid", "tok"), None),
            P(None, ("hid", "tok")),
            P(),
            P("hid", None, "tok", None),
            P(("hid", "tok"), None),
            P(None, ("hid", "tok")),
            P(),
            P("tok", "hid"),
        ),
        out_specs=(
            P("tok", "hid"),
            P("tok", "hid"),
            P("hid", None, "tok", None),
            P(("hid", "tok"), None),
            P(None, ("hid", "tok")),
            P("hid", None, "tok", None),
            P(("hid", "tok"), None),
            P(None, ("hid", "tok")),
        ),
        check_vma=False,
    )
```

```python
import jax
import jax.numpy as jnp
from jax import lax
from jax.experimental import pallas as pl
from jax.experimental.pallas import tpu as pltpu
from jax.sharding import PartitionSpec as P

D = 8192
BLK = 256


def gelu_parts(preact):
    inner_coef = 0.7978845608028654
    cubic_coef = 0.044715
    inner_arg = inner_coef * (preact + cubic_coef * preact * preact * preact)
    tanh_val = jnp.tanh(inner_arg)
    active = 0.5 * preact * (1.0 + tanh_val)
    slopes = 0.5 * (1.0 + tanh_val) + 0.5 * preact * (1.0 - tanh_val * tanh_val) * inner_coef * (
        1.0 + 3.0 * cubic_coef * preact * preact
    )
    return (active, slopes)


def dot_rows(left_arr, right_arr):
    return lax.dot_general(
        left_arr, right_arr, (((0,), (0,)), ((), ())), preferred_element_type=jnp.float32
    )


def dot_cols(left_arr, right_arr):
    return lax.dot_general(
        left_arr, right_arr, (((1,), (1,)), ((), ())), preferred_element_type=jnp.float32
    )


def rank_sum(values):
    return lax.psum(values, "hid")


def own_lists(lists, hid_blocks):
    return lax.dynamic_slice_in_dim(lists, lax.axis_index("hid") * hid_blocks, hid_blocks, 0)


def gather_in(values, lists, hid_blocks, blk_width):
    whole = lax.all_gather(values, "hid", axis=1, tiled=True)
    mine = own_lists(lists, hid_blocks)
    blocks = whole.reshape(whole.shape[0], whole.shape[1] // blk_width, blk_width)
    return jnp.stack(
        [
            jnp.stack(
                [
                    lax.dynamic_index_in_dim(blocks, mine[at, slot], axis=1, keepdims=False)
                    for at in range(hid_blocks)
                ],
                axis=1,
            )
            for slot in range(mine.shape[1])
        ],
        axis=1,
    )


def scatter_out(parts, lists, hid_blocks):
    mine = own_lists(lists, hid_blocks)
    picker = (mine.T[:, :, None] == jnp.arange(D // BLK, dtype=jnp.int32)[None, None, :]).astype(
        jnp.float32
    )
    dense = jnp.einsum("nsho,shc->nco", parts, picker, precision=lax.Precision.HIGHEST)
    return lax.psum_scatter(
        dense.reshape(dense.shape[0], -1), "hid", scatter_dimension=1, tiled=True
    )


def route_in(values, lists, hid_blocks, blk_width):
    return gather_in(values, lists, hid_blocks, blk_width)


def route_out(parts, lists, hid_blocks):
    return scatter_out(parts, lists, hid_blocks)


def local_gathered(
    tokens,
    in_blocks,
    in_left,
    in_right,
    in_lists,
    out_blocks,
    out_left,
    out_right,
    out_lists,
    cotangent,
):
    row_count, col_span = tokens.shape
    hid_blocks = in_blocks.shape[0]
    slot_count = in_blocks.shape[1]
    blk_width = in_blocks.shape[3]
    tok_count = lax.axis_size("tok")
    w_first, w_second, left_one, right_one, left_two, right_two = (
        lax.all_gather(in_blocks, "tok", axis=2, tiled=True),
        lax.all_gather(out_blocks, "tok", axis=2, tiled=True),
        lax.all_gather(in_left, "tok", axis=0, tiled=True),
        lax.all_gather(in_right, "tok", axis=1, tiled=True),
        lax.all_gather(out_left, "tok", axis=0, tiled=True),
        lax.all_gather(out_right, "tok", axis=1, tiled=True),
    )
    low_in, low_back = rank_sum(
        (
            jnp.dot(tokens, left_one, preferred_element_type=jnp.float32),
            dot_cols(cotangent, right_two),
        )
    )
    low_in = low_in.astype(jnp.bfloat16)
    low_back = low_back.astype(jnp.bfloat16)
    gathered = route_in(tokens, in_lists, hid_blocks, blk_width)
    group_count = gathered.shape[2]
    per_group = hid_blocks // group_count
    first_r = w_first.reshape(group_count, per_group, slot_count, blk_width, blk_width)
    second_r = w_second.reshape(group_count, per_group, slot_count, blk_width, blk_width)
    preact = jnp.einsum(
        "nseb,eqsbf->neqf", gathered, first_r, preferred_element_type=jnp.float32
    ).reshape(row_count, -1)
    preact = preact + jnp.dot(low_in, right_one, preferred_element_type=jnp.float32)
    active, slopes = gelu_parts(preact)
    hidden = active.astype(jnp.bfloat16)
    low_mid = rank_sum(jnp.dot(hidden, left_two, preferred_element_type=jnp.float32)).astype(
        jnp.bfloat16
    )
    hidden_r = hidden.reshape(row_count, group_count, per_group, blk_width)
    out_parts = jnp.einsum(
        "neqf,eqsfo->nseo", hidden_r, second_r, preferred_element_type=jnp.float32
    )
    sparse_out = route_out(out_parts, out_lists, hid_blocks)
    layer_out = (
        sparse_out + jnp.dot(low_mid, right_two, preferred_element_type=jnp.float32)
    ).astype(jnp.bfloat16)
    grad_in = route_in(cotangent, out_lists, hid_blocks, blk_width)
    grad_hidden = jnp.einsum(
        "nseo,eqsfo->neqf", grad_in, second_r, preferred_element_type=jnp.float32
    ).reshape(row_count, -1)
    grad_hidden = grad_hidden + dot_cols(low_back, left_two)
    grad_pre = (grad_hidden * slopes).astype(jnp.bfloat16)
    low_grad = rank_sum(dot_cols(grad_pre, right_one)).astype(jnp.bfloat16)
    grad_pre_r = grad_pre.reshape(row_count, group_count, per_group, blk_width)
    back_parts = jnp.einsum(
        "neqf,eqsbf->nseb", grad_pre_r, first_r, preferred_element_type=jnp.float32
    )
    sparse_back = route_out(back_parts, in_lists, hid_blocks)
    grad_tokens = (sparse_back + dot_cols(low_grad, left_one)).astype(jnp.bfloat16)
    loss_scale = lax.rsqrt(jnp.float32(row_count * tok_count))
    terms = (
        loss_scale
        * jnp.einsum(
            "nseb,neqf->eqsbf", gathered, grad_pre_r, preferred_element_type=jnp.float32
        ).reshape(w_first.shape),
        loss_scale
        * jnp.einsum(
            "neqf,nseo->eqsfo", hidden_r, grad_in, preferred_element_type=jnp.float32
        ).reshape(w_second.shape),
        loss_scale * dot_rows(tokens, low_grad),
        loss_scale * dot_rows(low_in, grad_pre),
        loss_scale * dot_rows(hidden, low_back),
        loss_scale * dot_rows(low_mid, cotangent),
    )
    shares = (
        lax.psum_scatter(
            terms[0].astype(jnp.bfloat16), "tok", scatter_dimension=2, tiled=True
        ).astype(jnp.float32),
        lax.psum_scatter(
            terms[1].astype(jnp.bfloat16), "tok", scatter_dimension=2, tiled=True
        ).astype(jnp.float32),
        lax.psum_scatter(
            terms[2].astype(jnp.bfloat16), "tok", scatter_dimension=0, tiled=True
        ).astype(jnp.float32),
        lax.psum_scatter(
            terms[3].astype(jnp.bfloat16), "tok", scatter_dimension=1, tiled=True
        ).astype(jnp.float32),
        lax.psum_scatter(
            terms[4].astype(jnp.bfloat16), "tok", scatter_dimension=0, tiled=True
        ).astype(jnp.float32),
        lax.psum_scatter(
            terms[5].astype(jnp.bfloat16), "tok", scatter_dimension=1, tiled=True
        ).astype(jnp.float32),
    )
    return (
        layer_out,
        grad_tokens,
        shares[0].astype(jnp.bfloat16),
        shares[2].astype(jnp.bfloat16),
        shares[3].astype(jnp.bfloat16),
        shares[1].astype(jnp.bfloat16),
        shares[4].astype(jnp.bfloat16),
        shares[5].astype(jnp.bfloat16),
    )


def in_group_shifts(count):
    return [0] + [1 << bit for bit in range(count.bit_length() - 1)]


def hid_shifts(count):
    return [1 << bit for bit in range(count.bit_length() - 1)]


def span(index, size):
    return pl.ds(pl.multiple_of(index * size, size), size)


def greet(partners):
    me_tok, me_hid = lax.axis_index("tok"), lax.axis_index("hid")
    barrier = pltpu.get_barrier_semaphore()
    for tok_dist, hid_dist in partners:
        pl.semaphore_signal(
            barrier,
            inc=1,
            device_id={"hid": me_hid ^ hid_dist, "tok": me_tok ^ tok_dist},
            device_id_type=pl.DeviceIdType.MESH,
        )
    pl.semaphore_wait(barrier, len(partners))


class Mover:
    def __init__(self, send, recv):
        self.send, self.recv, self.used = send, recv, 0
        self.open_copies = []

    def start(self, src, dst, tok_dist=0, hid_dist=0):
        at = self.used
        self.used += 1
        if tok_dist == 0 and hid_dist == 0:
            copy = pltpu.make_async_copy(src, dst, self.recv.at[at])
            copy.start()
            entry = [copy, True, False]
        else:
            copy = pltpu.make_async_remote_copy(
                src_ref=src,
                dst_ref=dst,
                send_sem=self.send.at[at],
                recv_sem=self.recv.at[at],
                device_id={
                    "hid": lax.axis_index("hid") ^ hid_dist,
                    "tok": lax.axis_index("tok") ^ tok_dist,
                },
                device_id_type=pl.DeviceIdType.MESH,
            )
            copy.start()
            entry = [copy, False, False]
        self.open_copies.append(entry)
        return entry

    def arrived(self, entry):
        if not entry[2]:
            if entry[1]:
                entry[0].wait()
            else:
                entry[0].wait_recv()
            entry[2] = True

    def finish(self):
        for entry in self.open_copies:
            self.arrived(entry)
        for entry in self.open_copies:
            if not entry[1]:
                entry[0].wait_send()


def double_sum(mover, far, totals, held):
    for pos, dist in enumerate(far):
        mover.arrived(mover.start(totals.at[pos], held.at[pos], 0, dist))
        totals[pos + 1] = totals[pos] + held[pos]
    return totals[len(far)]


def run_exchange(
    body, inputs, shapes, copies, ident, in_vmem=(), scratch=(), in_smem=(), out_vmem=()
):
    any_spec = pl.BlockSpec(memory_space=pl.ANY)
    vmem_spec = pl.BlockSpec(memory_space=pltpu.VMEM)
    smem_spec = pl.BlockSpec(memory_space=pltpu.SMEM)
    return pl.pallas_call(
        body,
        out_shape=[
            jax.ShapeDtypeStruct(*shape)
            if isinstance(shape[0], tuple)
            else jax.ShapeDtypeStruct(shape, jnp.bfloat16)
            for shape in shapes
        ],
        in_specs=[
            vmem_spec if at in in_vmem else smem_spec if at in in_smem else any_spec
            for at in range(len(inputs))
        ],
        out_specs=[
            vmem_spec if at in out_vmem else any_spec for at in range(len(shapes))
        ],
        scratch_shapes=[
            pltpu.SemaphoreType.DMA((copies,)),
            pltpu.SemaphoreType.DMA((copies,)),
            *scratch,
        ],
        compiler_params=pltpu.CompilerParams(
            collective_id=ident, has_side_effects=True, vmem_limit_bytes=62 * 2**20
        ),
        cost_estimate=pl.CostEstimate(
            flops=0, bytes_accessed=200_000_000, transcendentals=0
        ),
    )(*inputs)


def gather_order(n_hid, turn):
    shifts = hid_shifts(n_hid)
    wide = shifts[1:]
    turn = turn % len(wide)
    return wide[turn:] + wide[:turn] + shifts[:1]


def tok_peers(n_tok):
    return [(dist, 0) for dist in range(1, n_tok)]


class Route:
    def __init__(self, mover, src, got, held, bits):
        self.mover, self.src, self.got, self.held, self.bits = mover, src, got, held, bits
        top = len(bits) - 1
        self.orders = (
            (top, *range(1, top), 0),
            (*range(1, top), top, 0),
        )
        self.half = src.shape[0] // 2

    def part(self, at):
        return pl.ds(at * self.half, self.half)

    def current(self, stage):
        return self.src if stage == 0 else self.held.at[stage - 1]

    def send(self, stage):
        self.waits = [
            self.mover.start(
                self.current(stage).at[self.part(at), :],
                self.got.at[stage, self.part(at), :],
                0,
                1 << order[stage],
            )
            for at, order in enumerate(self.orders)
        ]

    def take(self, stage):
        for at, order in enumerate(self.orders):
            self.mover.arrived(self.waits[at])
            part = self.part(at)
            self.held[stage, part, :] = jnp.where(
                self.bits[order[stage]] == 1,
                self.got[stage, part, :],
                self.current(stage)[part, :],
            )


def route_all(routes, stages):
    for route in routes:
        route.send(0)
    for stage in range(stages):
        for route in routes:
            route.take(stage)
            if stage + 1 < stages:
                route.send(stage + 1)


def tok_peers(n_tok):
    return [(dist, 0) for dist in range(1, n_tok)]


class Gather:
    def __init__(self, mover, src, dst, order):
        self.mover, self.src, self.dst, self.order = mover, src, dst, order
        self.have = {0: None}
        self.depth = 0
        self.own = mover.start(src, dst.at[0])
        for dist in order:
            self.have[dist] = mover.start(src, dst.at[dist], 0, dist)

    def relay(self):
        order = self.order
        for at, dist in enumerate(order[:-1]):
            for known in [
                sum(bits) for bits in subsets(order[:at])
            ]:
                held = known ^ dist
                self.mover.arrived(self.have[held])
                for later in order[at + 1 :]:
                    self.have[held ^ later] = self.mover.start(
                        self.dst.at[held], self.dst.at[held ^ later], 0, later
                    )


    def settle(self):
        self.mover.arrived(self.own)
        for entry in self.have.values():
            if entry is not None:
                self.mover.arrived(entry)


def subsets(items):
    found = [()]
    for item in items:
        found = found + [entry + (item,) for entry in found]
    return found


def swap_halves(first, second, odd):
    lane = lax.broadcasted_iota(jnp.int32, first.shape, 1)
    half = first.shape[1] // 2

    def turn(values):
        return jnp.concatenate([values[:, half:], values[:, :half]], axis=1)

    if odd:
        return jnp.where(lane < half, turn(first), second)
    return jnp.where(lane < half, first, turn(second))


def swap_pieces(values, count, places, in_major, out_major):
    rows, width = values.shape[-2:]
    lanes = 128

    def block(ref, at, lane):
        if ref.ndim == 2:
            return ref, (slice(None), pl.ds(at * (ref.shape[1] // count) + lane, lanes))
        lead = (0, at) if ref.shape[0] == 1 else (at, 0)
        return ref, lead + (slice(None), pl.ds(lane, lanes))

    def body(src, dst):
        def load(at, lane):
            ref, where = block(src, at, lane)
            return ref[where]

        for to in range(count):
            for pair in range(count // 2):
                lane = (to // 2) * lanes
                ref, where = block(dst, to, pair * lanes)
                ref[where] = swap_halves(
                    load(2 * pair, lane), load(2 * pair + 1, lane), to % 2 == 1
                )

    def spec(major):
        if major is None:
            full = (rows, width if values.ndim == 2 else width * count)
            return full, pl.BlockSpec(full, lambda at: (0, 0))
        piece = width if values.ndim == 4 else width // count
        if major:
            return (places, count, rows, piece), pl.BlockSpec(
                (1, count, rows, piece), lambda at: (at, 0, 0, 0)
            )
        return (count, places, rows, piece), pl.BlockSpec(
            (count, 1, rows, piece), lambda at: (0, at, 0, 0)
        )

    shape, out_spec = spec(out_major)
    return pl.pallas_call(
        body,
        grid=(places,),
        out_shape=jax.ShapeDtypeStruct(shape, values.dtype),
        in_specs=[spec(in_major)[1]],
        out_specs=out_spec,
        compiler_params=pltpu.CompilerParams(vmem_limit_bytes=60 * 2**20),
    )(values)


def choose(load, count, bits, turn=0):
    held = [load(at) for at in range(count)]
    for at, bit in enumerate(bits):
        want = 1 - ((turn >> at) & 1)
        held = [
            jnp.where(bit == want, held[pos + 1], held[pos]) for pos in range(0, len(held), 2)
        ]
    return held[0]


def code_bits(code_i, which, first, count):
    return [code_i[which, first + at] for at in range(count)]


def swap_lanes(store, load, bits, rows, blk, places):
    step = 32

    def rows_of(at, carry):
        part = span(at, step)
        held = [load(part, pl.ds(pos * blk, blk)) for pos in range(places)]
        for place in range(places):
            store(
                part,
                pl.ds(place * blk, blk),
                choose(lambda pos: held[pos], places, bits, place),
            )
        return carry

    lax.fori_loop(0, rows // step, rows_of, 0)


class LowSum:
    def __init__(self, mover, n_tok, parts, core_got, mine, got, steps, taken, final):
        self.mover, self.n_tok = mover, n_tok
        self.parts, self.core_got, self.mine, self.got = parts, core_got, mine, got
        self.steps, self.taken, self.final = steps, taken, final
        self.me_hid = lax.axis_index("hid")
        self.core = self.me_hid % 2
        self.chips = [2 * dist for dist in range(1, n_tok)]

    def chunk(self, hid_index):
        return lax.axis_index("tok") ^ (hid_index // 2)

    def begin(self):
        self.waits = [self.mover.start(self.parts.at[:, 1 - self.core], self.core_got, 0, 1)]

    def fold_core(self):
        self.mover.arrived(self.waits[0])
        for at in range(self.n_tok):
            self.mine[at] = (self.parts[at, self.core] + self.core_got[at]).astype(jnp.bfloat16)
        self.waits = [
            self.mover.start(
                self.mine.at[self.chunk(self.me_hid ^ dist)], self.got.at[at], 0, dist
            )
            for at, dist in enumerate(self.chips)
        ]

    def gather_parts(self):
        total = self.mine[self.chunk(self.me_hid)].astype(jnp.float32)
        for at, entry in enumerate(self.waits):
            self.mover.arrived(entry)
            total = total + self.got[at].astype(jnp.float32)
        self.steps[0] = total.astype(jnp.bfloat16)
        self.waits = [self.mover.start(self.steps.at[0], self.taken.at[0], 2)]

    def step(self, at):
        self.mover.arrived(self.waits[0])
        self.steps[at] = (
            self.steps[at - 1].astype(jnp.float32) + self.taken[at - 1].astype(jnp.float32)
        ).astype(jnp.bfloat16)

    def middle(self):
        self.step(1)
        self.waits = [self.mover.start(self.steps.at[1], self.taken.at[1], 1)]

    def share(self):
        self.step(2)
        here = self.final.at[self.chunk(self.me_hid), self.core]
        self.waits = [
            self.mover.start(self.steps.at[2], here, 0, dist) for dist in [0] + self.chips
        ]

    def spread_core(self):
        for entry in self.waits:
            self.mover.arrived(entry)
        mine = self.final.at[:, self.core]
        self.waits = [self.mover.start(mine, mine, 0, 1)]

    def settle(self):
        self.mover.arrived(self.waits[0])

    def rows(self, dist, lanes):
        found = self.final[dist, :, :, lanes]
        return found.reshape(found.shape[0] * found.shape[1], found.shape[2])

    @staticmethod
    def copies(n_tok):
        return 2 * n_tok + 3

    @staticmethod
    def scratch(rows, width, n_tok):
        half = rows // 2
        return (
            pltpu.VMEM((n_tok, half, width), jnp.float32),
            pltpu.VMEM((n_tok, half, width), jnp.bfloat16),
            pltpu.VMEM((n_tok - 1, half, width), jnp.bfloat16),
            pltpu.VMEM((3, half, width), jnp.bfloat16),
            pltpu.VMEM((2, half, width), jnp.bfloat16),
            pltpu.VMEM((n_tok, 2, half, width), jnp.bfloat16),
        )


def bring_in(
    tokens, cotangent, codes, in_left, out_right, out_blocks, first_t, right_t, left_t
):
    n_tok, n_hid = lax.axis_size("tok"), lax.axis_size("hid")
    _, groups, slots, deep, blk = first_t.shape
    wide, rank = in_left.shape
    rows, width = tokens.shape
    whole = rows * n_tok
    far = hid_shifts(n_hid)

    places = 1 + len(far)
    near_shifts = in_group_shifts(groups)
    per, fine = left_t.shape[0], left_t.shape[2]

    def body(
        tok_i, cot_i, code_i, left_i, right_i, second_i, first_i, r_i, l_i,
        pick_o, own_o, sum_o, low_o, gr_o, gl_o, outf_o, backf_o, gfirst_o, gsecond_o,
        send, recv, got_mid, held_mid, got_low, held_low, x_all, parts,
        core_got, low_mine, low_got, steps, taken, final,
        first_o, r_o, l_o, hidden, slope, stage_far, stage_first, stage_second,
    ):
        me = lax.axis_index("tok")
        near_bits = n_tok.bit_length() - 1
        far_bits = n_hid.bit_length() - 1
        lows = [code_bits(code_i, which, 0, near_bits) for which in range(2)]
        highs = [code_bits(code_i, which, near_bits, far_bits) for which in range(2)]
        own_bits = [
            [bit ^ ((me >> at) & 1) for at, bit in enumerate(lows[which])] for which in range(2)
        ]
        greet(tok_peers(n_tok) + [(0, dist) for dist in (1, *range(2, n_hid, 2))])
        mover = Mover(send, recv)
        part = [pl.ds(dist * rows, rows) for dist in range(n_tok)]
        first_waits, far_waits, row_waits = {}, [], []
        arrived = {}

        def send_first(group):
            first_waits[group] = [
                mover.start(
                    first_i.at[me ^ dist, group], first_o.at[group, :, span(me, deep), :], dist
                )
                for dist in (2, 3, 1, 0)
            ]

        def spread(at, dist):
            for pos, far_dist in enumerate(far):
                far_waits.append(
                    mover.start(
                        x_all.at[at, 0, part[dist], :],
                        x_all.at[at, 1 + pos, part[dist], :],
                        0,
                        far_dist,
                    )
                )

        routes = [
            Route(mover, src, got_mid.at[at], held_mid.at[at], highs[at])
            for at, src in enumerate((cot_i, tok_i))
        ]
        for route in routes:
            route.send(0)
        send_first(0)
        last = far_bits - 1
        for stage in range(far_bits):
            for at, route in enumerate(routes):
                route.take(stage)
                if stage < last:
                    route.send(stage + 1)
                    continue

                def store_near(rows_at, lanes, value):
                    x_all[at, 0, rows_at, lanes] = value

                swap_lanes(
                    store_near,
                    lambda rows_at, lanes: held_mid[at, last, rows_at, lanes],
                    lows[at], rows, blk, width // blk,
                )
                for dist in (1, 2):
                    arrived[at, dist] = mover.start(
                        x_all.at[at, 0, part[0], :], x_all.at[at, 0, part[dist], :], dist
                    )
        for at in range(2):
            spread(at, 0)
        more = [
            Route(mover, src, got_low.at[at], held_low.at[at], highs[at])
            for at, src in enumerate((right_i, left_i))
        ]
        route_all(more, far_bits)
        for at in range(2):
            pick_o[at] = held_low[at, last]
        send_first(1)
        for at in range(2):
            mover.arrived(arrived[at, 1])
            spread(at, 1)
        for at in range(2):
            mover.arrived(arrived[at, 2])
            arrived[at, 3] = mover.start(
                x_all.at[at, 0, part[2], :], x_all.at[at, 0, part[3], :], 1
            )
        send_first(2)
        for at in range(2):
            spread(at, 2)
        half = rows // 2
        for dist in range(n_tok):
            for at in range(2):
                if dist == 3:
                    mover.arrived(arrived[at, 3])
                own_o[at, part[dist], :] = choose(
                    lambda pos: x_all[at, 0, part[dist], pl.ds(pos * blk, blk)], n_tok, own_bits[at]
                )
            for side in range(2):
                piece = pl.ds(dist * rows + side * half, half)
                parts[dist, side, :, :rank] = jnp.dot(
                    own_o[1, piece, :], pick_o[1], preferred_element_type=jnp.float32
                )
                parts[dist, side, :, rank:] = dot_cols(own_o[0, piece, :], pick_o[0])
        low = LowSum(mover, n_tok, parts, core_got, low_mine, low_got, steps, taken, final)
        low.begin()
        low.fold_core()
        spread(0, 3)
        low.gather_parts()
        for dist in (2, 3, 1, 0):
            row_waits.append(mover.start(r_i.at[me ^ dist], r_o.at[me], dist))
            row_waits.append(mover.start(l_i.at[:, me ^ dist], l_o.at[me], dist))
        low.middle()
        spread(1, 3)
        low.share()
        for group in range(3, groups):
            send_first(group)
        low.spread_core()
        low.settle()
        scale = lax.rsqrt(jnp.float32(whole))
        for entry in row_waits + far_waits:
            mover.arrived(entry)
        low_in = jnp.concatenate([low.rows(dist, pl.ds(0, rank)) for dist in range(n_tok)], axis=0)
        low_back = jnp.concatenate(
            [low.rows(dist, pl.ds(rank, rank)) for dist in range(n_tok)], axis=0
        )
        touched = set()
        staged = {}
        for group in range(groups):
            turn = group % 2

            def spot(k):
                if k < len(near_shifts):
                    return 0, pl.ds((group ^ near_shifts[k]) * blk, blk)
                return k - len(near_shifts) + 1, pl.ds(group * blk, blk)

            def second(k):
                return second_i[pl.ds(group * per, per), k].reshape(per * fine, blk)

            left = l_o[group].reshape(per * fine, rank)
            for entry in first_waits[group] + staged.pop(group - 2, []):
                mover.arrived(entry)
            total = jnp.dot(low_in, r_o[group], preferred_element_type=jnp.float32)
            for k in range(slots):
                place, lanes = spot(k)
                total = total + jnp.dot(
                    x_all[1, place, :, lanes],
                    first_o[group, k],
                    preferred_element_type=jnp.float32,
                )
            active, slopes = gelu_parts(total)
            hidden[...] = active.astype(jnp.bfloat16)
            total = dot_cols(low_back, left)
            for k in range(slots):
                place, lanes = spot(k)
                total = total + dot_cols(x_all[0, place, :, lanes], second(k))
            slope[...] = (total * slopes).astype(jnp.bfloat16)
            low_one = jnp.dot(hidden[...], left, preferred_element_type=jnp.float32)
            low_two = dot_cols(slope[...], r_o[group])
            if group == 0:
                low_o[:, :rank] = low_one
                low_o[:, rank:] = low_two
            else:
                low_o[:, :rank] += low_one
                low_o[:, rank:] += low_two
            entries = []
            for k in range(slots):
                place, lanes = spot(k)
                values = (
                    jnp.dot(hidden[...], second(k), preferred_element_type=jnp.float32),
                    dot_cols(slope[...], first_o[group, k]),
                )
                for which in range(2):
                    if k >= len(near_shifts):
                        stage_far[turn, which, place - 1] = values[which].astype(jnp.bfloat16)
                    elif (which, group ^ near_shifts[k]) in touched:
                        sum_o[which, :, lanes] = (
                            sum_o[which, :, lanes].astype(jnp.float32) + values[which]
                        ).astype(jnp.bfloat16)
                    else:
                        touched.add((which, group ^ near_shifts[k]))
                        sum_o[which, :, lanes] = values[which].astype(jnp.bfloat16)
            for which, dst in enumerate((outf_o, backf_o)):
                entries.append(
                    mover.start(
                        stage_far.at[turn, which], dst.at[:, :, pl.ds(group * blk, blk)]
                    )
                )
            for k in range(slots):
                place, lanes = spot(k)
                stage_first[turn, k] = (
                    scale * dot_rows(x_all[1, place, :, lanes], slope[...])
                ).astype(jnp.bfloat16)
                stage_second[turn, :, k] = (
                    (scale * dot_rows(hidden[...], x_all[0, place, :, lanes]))
                    .astype(jnp.bfloat16)
                    .reshape(per, fine, blk)
                )
            entries.append(mover.start(stage_first.at[turn], gfirst_o.at[group]))
            entries.append(
                mover.start(stage_second.at[turn], gsecond_o.at[pl.ds(group * per, per)])
            )
            gr_o[group] = (scale * dot_rows(low_in, slope[...])).astype(jnp.bfloat16)
            gl_o[group] = (
                (scale * dot_rows(hidden[...], low_back))
                .astype(jnp.bfloat16)
                .reshape(per, fine, rank)
            )
            staged[group] = entries
        mover.finish()

    f32 = jnp.float32
    return run_exchange(
        body,
        (
            tokens, cotangent, codes, in_left, out_right, out_blocks,
            first_t, right_t, left_t,
        ),
        [
            (2, wide, rank),
            (2, whole, blk),
            (2, whole, width),
            ((whole, 2 * rank), f32),
            (groups, rank, blk),
            (groups, per, fine, rank),
            (places - 1, whole, width),
            (places - 1, whole, width),
            (groups, slots, blk, blk),
            out_blocks.shape,
        ],
        8 * len(far) + groups * n_tok + 6 + 2 * n_tok * len(far) + 2 * n_tok
        + LowSum.copies(n_tok) + 4 * groups,
        1,
        (0, 1, 3, 4, 5),
        (
            pltpu.VMEM((2, len(far), rows, width), jnp.bfloat16),
            pltpu.VMEM((2, len(far), rows, width), jnp.bfloat16),
            pltpu.VMEM((2, len(far), wide, rank), jnp.bfloat16),
            pltpu.VMEM((2, len(far), wide, rank), jnp.bfloat16),
            pltpu.VMEM((2, places, whole, width), jnp.bfloat16),
            pltpu.VMEM((n_tok, 2, rows // 2, 2 * rank), jnp.float32),
        )
        + LowSum.scratch(rows, 2 * rank, n_tok)
        + (
            pltpu.VMEM((groups, slots, blk, blk), jnp.bfloat16),
            pltpu.VMEM((groups, rank, blk), jnp.bfloat16),
            pltpu.VMEM((groups, per, fine, rank), jnp.bfloat16),
            pltpu.VMEM((whole, blk), jnp.bfloat16),
            pltpu.VMEM((whole, blk), jnp.bfloat16),
            pltpu.VMEM((2, 2, places - 1, whole, blk), jnp.bfloat16),
            pltpu.VMEM((2, slots, blk, blk), jnp.bfloat16),
            pltpu.VMEM((2, per, slots, fine, blk), jnp.bfloat16),
        ),
        in_smem=(2,),
        out_vmem=(0, 1, 2, 3, 4, 5),
    )


def send_out(
    low_parts, own_sums, codes, own, picks,
    out_far, back_far, grads, right_g, left_g,
):
    n_tok, n_hid = lax.axis_size("tok"), lax.axis_size("hid")
    far = hid_shifts(n_hid)
    _, whole, width = out_far.shape
    rows = whole // n_tok
    rank = picks.shape[2]
    groups, slots, full, blk = grads.shape
    deep = full // n_tok
    _, per, fine, _ = left_g.shape
    wide = picks.shape[1]

    def body(
        low_i, sum_i, code_i, own_i, pick_i,
        outf_i, backf_i, grad_i, r_i, l_i,
        layer_o, gtok_o, gleft_o, gright_o, grad_o, r_o, l_o,
        send, recv, held, kept, got_one, pair, got_two, low_grad, spots,
        got_mid, held_mid, got_low, held_low,
        core_got, low_mine, low_got, steps, taken, final,
    ):
        me = lax.axis_index("tok")
        scale = lax.rsqrt(jnp.float32(whole))
        near_bits = n_tok.bit_length() - 1
        far_bits = n_hid.bit_length() - 1
        lows = [code_bits(code_i, which, 0, near_bits) for which in range(2)]
        highs = [code_bits(code_i, which, near_bits, far_bits) for which in range(2)]
        own_bits = [
            [bit ^ ((me >> at) & 1) for at, bit in enumerate(lows[which])] for which in range(2)
        ]
        greet(tok_peers(n_tok) + [(0, dist) for dist in (1, *range(2, n_hid, 2))])
        mover = Mover(send, recv)
        part = [pl.ds(dist * rows, rows) for dist in range(n_tok)]
        fars = (outf_i, backf_i)
        low = LowSum(mover, n_tok, low_i, core_got, low_mine, low_got, steps, taken, final)
        low.begin()
        waits = {}

        def send_far(which, dist):
            for pos, far_dist in enumerate(far):
                waits[which, dist, pos] = mover.start(
                    fars[which].at[pos, part[dist], :],
                    held.at[which, pos, part[dist], :],
                    0,
                    far_dist,
                )

        def send_grads(group):
            for dist in (2, 3, 1, 0):
                mover.start(
                    grad_i.at[group, :, span(me ^ dist, deep), :], grad_o.at[me, group], dist
                )

        first, second = {}, {}

        def settle(which, dist):
            total = sum_i[which, part[dist], :].astype(jnp.float32) + jnp.dot(
                low.rows(dist, pl.ds(which * rank, rank)),
                spots[which],
                preferred_element_type=jnp.float32,
            )
            for pos in range(len(far)):
                mover.arrived(waits[which, dist, pos])
                total = total + held[which, pos, part[dist], :].astype(jnp.float32)
            kept[which, part[dist], :] = total.astype(jnp.bfloat16)
            if dist % 2 == 1:
                first[which, dist - 1] = mover.start(
                    kept.at[which, part[dist], :], got_one.at[which, dist // 2], 1
                )

        def pass_on(which):
            mover.arrived(first[which, 2])
            pair[which] = (
                kept[which, part[2], :].astype(jnp.float32)
                + got_one[which, 1].astype(jnp.float32)
            ).astype(jnp.bfloat16)
            second[which] = mover.start(pair.at[which], got_two.at[which], 2)

        def close(which):
            mover.arrived(first[which, 0])
            mover.arrived(second[which])
            pair[which + 2] = (
                kept[which, part[0], :].astype(jnp.float32)
                + got_one[which, 0].astype(jnp.float32)
                + got_two[which].astype(jnp.float32)
            ).astype(jnp.bfloat16)
            route = Route(
                mover, pair.at[which + 2], got_mid.at[which], held_mid.at[which], highs[which]
            )
            route.send(0)
            return route

        send_grads(0)
        low.fold_core()
        send_far(0, 3)
        for which in range(2):
            weight = pick_i[which].astype(jnp.float32)
            if which == 1:
                weight = weight.T
            for place in range(width // blk):
                here = 1
                for at, bit in enumerate(own_bits[which]):
                    here = here * (bit if (place >> at) & 1 else 1 - bit)
                spots[which, :, pl.ds(place * blk, blk)] = (
                    weight * here.astype(jnp.float32)
                ).astype(jnp.bfloat16)
        low.gather_parts()
        send_far(0, 1)
        low.middle()
        send_far(0, 2)
        low.share()
        send_far(0, 0)
        send_grads(1)
        for dist in (2, 3, 1, 0):
            mover.start(r_i.at[me ^ dist], r_o.at[me], dist)
            mover.start(l_i.at[me ^ dist], l_o.at[:, me], dist)
        low.spread_core()
        low.settle()
        settle(0, 3)
        settle(0, 1)
        send_grads(2)
        for dist in (3, 1, 2, 0):
            send_far(1, dist)
        settle(0, 2)
        pass_on(0)
        settle(0, 0)
        low_mid = jnp.concatenate([low.rows(dist, pl.ds(0, rank)) for dist in range(n_tok)], axis=0)
        low_grad[0] = (scale * dot_rows(low_mid, own_i[0])).astype(jnp.bfloat16)
        low_back = jnp.concatenate(
            [low.rows(dist, pl.ds(rank, rank)) for dist in range(n_tok)], axis=0
        )
        low_grad[1] = (scale * dot_rows(own_i[1], low_back)).astype(jnp.bfloat16)
        settle(1, 3)
        settle(1, 1)
        routes = [close(0)]
        more = [
            Route(mover, low_grad.at[which], got_low.at[which], held_low.at[which], highs[which])
            for which in range(2)
        ]
        for route in more:
            route.send(0)
        settle(1, 2)
        pass_on(1)
        settle(1, 0)

        def advance(route, stage):
            route.take(stage)
            if stage + 1 < far_bits:
                route.send(stage + 1)

        last = far_bits - 1
        for stage in range(far_bits):
            for route in routes + more:
                advance(route, stage)
        routes.append(close(1))
        send_grads(3)
        gright_o[...] = held_low[0, last]
        gleft_o[...] = held_low[1, last]
        outs = (layer_o, gtok_o)
        for which in range(2):
            if which == 1:
                for stage in range(far_bits):
                    advance(routes[1], stage)

            def store_out(rows_at, lanes, value):
                outs[which][rows_at, lanes] = value

            swap_lanes(
                store_out,
                lambda rows_at, lanes: held_mid[which, last, rows_at, lanes],
                lows[which], rows, blk, width // blk,
            )
        mover.finish()

    return run_exchange(
        body,
        (
            low_parts, own_sums, codes, own, picks,
            out_far, back_far, grads, right_g, left_g,
        ),
        [
            (rows, width),
            (rows, width),
            (wide, rank),
            (rank, wide),
            (n_tok, groups, slots, deep, blk),
            (n_tok, rank, blk),
            (per, n_tok, fine, rank),
        ],
        n_tok * (2 * len(far) + groups + 2) + 8 + 8 * len(far) + LowSum.copies(n_tok),
        2,
        (0, 1, 3, 4),
        (
            pltpu.VMEM((2, len(far), whole, width), jnp.bfloat16),
            pltpu.VMEM((2, whole, width), jnp.bfloat16),
            pltpu.VMEM((2, 2, rows, width), jnp.bfloat16),
            pltpu.VMEM((4, rows, width), jnp.bfloat16),
            pltpu.VMEM((2, rows, width), jnp.bfloat16),
            pltpu.VMEM((2, wide, rank), jnp.bfloat16),
            pltpu.VMEM((2, rank, width), jnp.bfloat16),
            pltpu.VMEM((2, len(far), rows, width), jnp.bfloat16),
            pltpu.VMEM((2, len(far), rows, width), jnp.bfloat16),
            pltpu.VMEM((2, len(far), wide, rank), jnp.bfloat16),
            pltpu.VMEM((2, len(far), wide, rank), jnp.bfloat16),
        )
        + LowSum.scratch(rows, 2 * rank, n_tok),
        in_smem=(2,),
        out_vmem=(0, 1, 2, 3),
    )


def local_moved(
    tokens,
    in_blocks,
    in_left,
    in_right,
    in_lists,
    out_blocks,
    out_left,
    out_right,
    out_lists,
    cotangent,
):
    hid_blocks, slots, deep, blk = in_blocks.shape
    n_tok = lax.axis_size("tok")
    groups = tokens.shape[1] // blk
    per = hid_blocks // groups
    rank = in_left.shape[1]
    fine = blk // n_tok
    heads = jnp.stack([out_lists, in_lists])[:, 0, 0]
    codes = (heads[:, None] >> jnp.arange(8, dtype=jnp.int32)[None, :]) & 1
    first_t = swap_pieces(
        in_blocks.reshape(groups, per, slots * deep, blk), per, groups, True, False
    ).reshape(n_tok, groups, slots, deep, blk)
    right_t = swap_pieces(in_right, per, 1, None, False).reshape(n_tok, rank, blk)
    (
        picks,
        own,
        own_sums,
        low_parts,
        right_g,
        left_g,
        out_far,
        back_far,
        grad_first,
        grad_out_blocks,
    ) = bring_in(
        tokens,
        cotangent,
        codes,
        in_left,
        out_right,
        out_blocks,
        first_t,
        right_t,
        out_left.reshape(per, n_tok, fine, rank),
    )
    layer_out, grad_tokens, grad_in_left, grad_out_right, grad_got, right_got, left_got = send_out(
        low_parts.reshape(n_tok, 2, tokens.shape[0] // 2, 2 * rank),
        own_sums,
        codes,
        own,
        picks,
        out_far,
        back_far,
        grad_first,
        right_g,
        left_g,
    )
    grad_in_blocks = swap_pieces(
        grad_got.reshape(n_tok, groups, slots * deep, blk), per, groups, False, True
    ).reshape(hid_blocks, slots, deep, blk)
    grad_in_right = swap_pieces(right_got.reshape(n_tok, 1, rank, blk), per, 1, False, None)
    return (
        layer_out,
        grad_tokens,
        grad_in_blocks,
        grad_in_left,
        grad_in_right,
        grad_out_blocks,
        left_got.reshape(out_left.shape),
        grad_out_right,
    )


def power_of_two(count):
    return count & (count - 1) == 0


def local(*arrays):
    tokens, in_blocks = arrays[0], arrays[1]
    n_tok = lax.axis_size("tok")
    n_hid = lax.axis_size("hid")
    whole_groups = (
        n_tok == 4
        and n_hid == 2 * n_tok
        and tokens.shape[1] == n_tok * in_blocks.shape[3]
        and in_blocks.shape[0] == n_tok * n_tok
    )
    return local_moved(*arrays) if whole_groups else local_gathered(*arrays)


def solution(mesh):
    return jax.shard_map(
        local,
        mesh=mesh,
        in_specs=(
            P("tok", "hid"),
            P("hid", None, "tok", None),
            P(("hid", "tok"), None),
            P(None, ("hid", "tok")),
            P(),
            P("hid", None, "tok", None),
            P(("hid", "tok"), None),
            P(None, ("hid", "tok")),
            P(),
            P("tok", "hid"),
        ),
        out_specs=(
            P("tok", "hid"),
            P("tok", "hid"),
            P("hid", None, "tok", None),
            P(("hid", "tok"), None),
            P(None, ("hid", "tok")),
            P("hid", None, "tok", None),
            P(("hid", "tok"), None),
            P(None, ("hid", "tok")),
        ),
        check_vma=False,
    )
```

```python
import jax
import jax.numpy as jnp
from jax import lax
from jax.experimental import pallas as pl
from jax.experimental.pallas import tpu as pltpu
from jax.sharding import PartitionSpec as P

D = 8192
BLK = 256


def gelu_parts(preact):
    inner_coef = 0.7978845608028654
    cubic_coef = 0.044715
    inner_arg = inner_coef * (preact + cubic_coef * preact * preact * preact)
    tanh_val = jnp.tanh(inner_arg)
    active = 0.5 * preact * (1.0 + tanh_val)
    slopes = 0.5 * (1.0 + tanh_val) + 0.5 * preact * (1.0 - tanh_val * tanh_val) * inner_coef * (
        1.0 + 3.0 * cubic_coef * preact * preact
    )
    return (active, slopes)


def dot_rows(left_arr, right_arr):
    return lax.dot_general(
        left_arr, right_arr, (((0,), (0,)), ((), ())), preferred_element_type=jnp.float32
    )


def dot_cols(left_arr, right_arr):
    return lax.dot_general(
        left_arr, right_arr, (((1,), (1,)), ((), ())), preferred_element_type=jnp.float32
    )


def rank_sum(values):
    return lax.psum(values, "hid")


def own_lists(lists, hid_blocks):
    return lax.dynamic_slice_in_dim(lists, lax.axis_index("hid") * hid_blocks, hid_blocks, 0)


def gather_in(values, lists, hid_blocks, blk_width):
    whole = lax.all_gather(values, "hid", axis=1, tiled=True)
    mine = own_lists(lists, hid_blocks)
    blocks = whole.reshape(whole.shape[0], whole.shape[1] // blk_width, blk_width)
    return jnp.stack(
        [
            jnp.stack(
                [
                    lax.dynamic_index_in_dim(blocks, mine[at, slot], axis=1, keepdims=False)
                    for at in range(hid_blocks)
                ],
                axis=1,
            )
            for slot in range(mine.shape[1])
        ],
        axis=1,
    )


def scatter_out(parts, lists, hid_blocks):
    mine = own_lists(lists, hid_blocks)
    picker = (mine.T[:, :, None] == jnp.arange(D // BLK, dtype=jnp.int32)[None, None, :]).astype(
        jnp.float32
    )
    dense = jnp.einsum("nsho,shc->nco", parts, picker, precision=lax.Precision.HIGHEST)
    return lax.psum_scatter(
        dense.reshape(dense.shape[0], -1), "hid", scatter_dimension=1, tiled=True
    )


def route_in(values, lists, hid_blocks, blk_width):
    return gather_in(values, lists, hid_blocks, blk_width)


def route_out(parts, lists, hid_blocks):
    return scatter_out(parts, lists, hid_blocks)


def local_gathered(
    tokens,
    in_blocks,
    in_left,
    in_right,
    in_lists,
    out_blocks,
    out_left,
    out_right,
    out_lists,
    cotangent,
):
    row_count, col_span = tokens.shape
    hid_blocks = in_blocks.shape[0]
    slot_count = in_blocks.shape[1]
    blk_width = in_blocks.shape[3]
    tok_count = lax.axis_size("tok")
    w_first, w_second, left_one, right_one, left_two, right_two = (
        lax.all_gather(in_blocks, "tok", axis=2, tiled=True),
        lax.all_gather(out_blocks, "tok", axis=2, tiled=True),
        lax.all_gather(in_left, "tok", axis=0, tiled=True),
        lax.all_gather(in_right, "tok", axis=1, tiled=True),
        lax.all_gather(out_left, "tok", axis=0, tiled=True),
        lax.all_gather(out_right, "tok", axis=1, tiled=True),
    )
    low_in, low_back = rank_sum(
        (
            jnp.dot(tokens, left_one, preferred_element_type=jnp.float32),
            dot_cols(cotangent, right_two),
        )
    )
    low_in = low_in.astype(jnp.bfloat16)
    low_back = low_back.astype(jnp.bfloat16)
    gathered = route_in(tokens, in_lists, hid_blocks, blk_width)
    group_count = gathered.shape[2]
    per_group = hid_blocks // group_count
    first_r = w_first.reshape(group_count, per_group, slot_count, blk_width, blk_width)
    second_r = w_second.reshape(group_count, per_group, slot_count, blk_width, blk_width)
    preact = jnp.einsum(
        "nseb,eqsbf->neqf", gathered, first_r, preferred_element_type=jnp.float32
    ).reshape(row_count, -1)
    preact = preact + jnp.dot(low_in, right_one, preferred_element_type=jnp.float32)
    active, slopes = gelu_parts(preact)
    hidden = active.astype(jnp.bfloat16)
    low_mid = rank_sum(jnp.dot(hidden, left_two, preferred_element_type=jnp.float32)).astype(
        jnp.bfloat16
    )
    hidden_r = hidden.reshape(row_count, group_count, per_group, blk_width)
    out_parts = jnp.einsum(
        "neqf,eqsfo->nseo", hidden_r, second_r, preferred_element_type=jnp.float32
    )
    sparse_out = route_out(out_parts, out_lists, hid_blocks)
    layer_out = (
        sparse_out + jnp.dot(low_mid, right_two, preferred_element_type=jnp.float32)
    ).astype(jnp.bfloat16)
    grad_in = route_in(cotangent, out_lists, hid_blocks, blk_width)
    grad_hidden = jnp.einsum(
        "nseo,eqsfo->neqf", grad_in, second_r, preferred_element_type=jnp.float32
    ).reshape(row_count, -1)
    grad_hidden = grad_hidden + dot_cols(low_back, left_two)
    grad_pre = (grad_hidden * slopes).astype(jnp.bfloat16)
    low_grad = rank_sum(dot_cols(grad_pre, right_one)).astype(jnp.bfloat16)
    grad_pre_r = grad_pre.reshape(row_count, group_count, per_group, blk_width)
    back_parts = jnp.einsum(
        "neqf,eqsbf->nseb", grad_pre_r, first_r, preferred_element_type=jnp.float32
    )
    sparse_back = route_out(back_parts, in_lists, hid_blocks)
    grad_tokens = (sparse_back + dot_cols(low_grad, left_one)).astype(jnp.bfloat16)
    loss_scale = lax.rsqrt(jnp.float32(row_count * tok_count))
    terms = (
        loss_scale
        * jnp.einsum(
            "nseb,neqf->eqsbf", gathered, grad_pre_r, preferred_element_type=jnp.float32
        ).reshape(w_first.shape),
        loss_scale
        * jnp.einsum(
            "neqf,nseo->eqsfo", hidden_r, grad_in, preferred_element_type=jnp.float32
        ).reshape(w_second.shape),
        loss_scale * dot_rows(tokens, low_grad),
        loss_scale * dot_rows(low_in, grad_pre),
        loss_scale * dot_rows(hidden, low_back),
        loss_scale * dot_rows(low_mid, cotangent),
    )
    shares = (
        lax.psum_scatter(
            terms[0].astype(jnp.bfloat16), "tok", scatter_dimension=2, tiled=True
        ).astype(jnp.float32),
        lax.psum_scatter(
            terms[1].astype(jnp.bfloat16), "tok", scatter_dimension=2, tiled=True
        ).astype(jnp.float32),
        lax.psum_scatter(
            terms[2].astype(jnp.bfloat16), "tok", scatter_dimension=0, tiled=True
        ).astype(jnp.float32),
        lax.psum_scatter(
            terms[3].astype(jnp.bfloat16), "tok", scatter_dimension=1, tiled=True
        ).astype(jnp.float32),
        lax.psum_scatter(
            terms[4].astype(jnp.bfloat16), "tok", scatter_dimension=0, tiled=True
        ).astype(jnp.float32),
        lax.psum_scatter(
            terms[5].astype(jnp.bfloat16), "tok", scatter_dimension=1, tiled=True
        ).astype(jnp.float32),
    )
    return (
        layer_out,
        grad_tokens,
        shares[0].astype(jnp.bfloat16),
        shares[2].astype(jnp.bfloat16),
        shares[3].astype(jnp.bfloat16),
        shares[1].astype(jnp.bfloat16),
        shares[4].astype(jnp.bfloat16),
        shares[5].astype(jnp.bfloat16),
    )


def in_group_shifts(count):
    return [0] + [1 << bit for bit in range(count.bit_length() - 1)]


def hid_shifts(count):
    return [1 << bit for bit in range(count.bit_length() - 1)]


def span(index, size):
    return pl.ds(pl.multiple_of(index * size, size), size)


def greet(partners):
    me_tok, me_hid = lax.axis_index("tok"), lax.axis_index("hid")
    barrier = pltpu.get_barrier_semaphore()
    for tok_dist, hid_dist in partners:
        pl.semaphore_signal(
            barrier,
            inc=1,
            device_id={"hid": me_hid ^ hid_dist, "tok": me_tok ^ tok_dist},
            device_id_type=pl.DeviceIdType.MESH,
        )
    pl.semaphore_wait(barrier, len(partners))


class Mover:
    def __init__(self, send, recv):
        self.send, self.recv, self.used = send, recv, 0
        self.open_copies = []

    def start(self, src, dst, tok_dist=0, hid_dist=0):
        at = self.used
        self.used += 1
        if tok_dist == 0 and hid_dist == 0:
            copy = pltpu.make_async_copy(src, dst, self.recv.at[at])
            copy.start()
            entry = [copy, True, False, True]
        else:
            copy = pltpu.make_async_remote_copy(
                src_ref=src,
                dst_ref=dst,
                send_sem=self.send.at[at],
                recv_sem=self.recv.at[at],
                device_id={
                    "hid": lax.axis_index("hid") ^ hid_dist,
                    "tok": lax.axis_index("tok") ^ tok_dist,
                },
                device_id_type=pl.DeviceIdType.MESH,
            )
            copy.start()
            entry = [copy, False, False, False]
        self.open_copies.append(entry)
        return entry

    def arrived(self, entry):
        if not entry[2]:
            if entry[1]:
                entry[0].wait()
            else:
                entry[0].wait_recv()
            entry[2] = True

    def sent(self, entry):
        if entry[1]:
            self.arrived(entry)
        elif not entry[3]:
            entry[0].wait_send()
            entry[3] = True

    def finish(self):
        for entry in self.open_copies:
            self.arrived(entry)
        for entry in self.open_copies:
            self.sent(entry)


def double_sum(mover, far, totals, held):
    for pos, dist in enumerate(far):
        mover.arrived(mover.start(totals.at[pos], held.at[pos], 0, dist))
        totals[pos + 1] = totals[pos] + held[pos]
    return totals[len(far)]


def run_exchange(
    body, inputs, shapes, copies, ident, in_vmem=(), scratch=(), in_smem=(), out_vmem=()
):
    any_spec = pl.BlockSpec(memory_space=pl.ANY)
    vmem_spec = pl.BlockSpec(memory_space=pltpu.VMEM)
    smem_spec = pl.BlockSpec(memory_space=pltpu.SMEM)
    return pl.pallas_call(
        body,
        out_shape=[
            jax.ShapeDtypeStruct(*shape)
            if isinstance(shape[0], tuple)
            else jax.ShapeDtypeStruct(shape, jnp.bfloat16)
            for shape in shapes
        ],
        in_specs=[
            vmem_spec if at in in_vmem else smem_spec if at in in_smem else any_spec
            for at in range(len(inputs))
        ],
        out_specs=[
            vmem_spec if at in out_vmem else any_spec for at in range(len(shapes))
        ],
        scratch_shapes=[
            pltpu.SemaphoreType.DMA((copies,)),
            pltpu.SemaphoreType.DMA((copies,)),
            *scratch,
        ],
        compiler_params=pltpu.CompilerParams(
            collective_id=ident, has_side_effects=True, vmem_limit_bytes=62 * 2**20
        ),
        cost_estimate=pl.CostEstimate(
            flops=0, bytes_accessed=200_000_000, transcendentals=0
        ),
    )(*inputs)


def gather_order(n_hid, turn):
    shifts = hid_shifts(n_hid)
    wide = shifts[1:]
    turn = turn % len(wide)
    return wide[turn:] + wide[:turn] + shifts[:1]


def tok_peers(n_tok):
    return [(dist, 0) for dist in range(1, n_tok)]


class Route:
    def __init__(self, mover, src, got, held, bits):
        self.mover, self.src, self.got, self.held, self.bits = mover, src, got, held, bits
        top = len(bits) - 1
        self.orders = (
            (top, *range(1, top), 0),
            (*range(1, top), top, 0),
        )
        self.half = src.shape[0] // 2

    def part(self, at):
        return pl.ds(at * self.half, self.half)

    def current(self, stage):
        return self.src if stage == 0 else self.held.at[stage - 1]

    def send(self, stage):
        self.waits = [
            self.mover.start(
                self.current(stage).at[self.part(at), :],
                self.got.at[stage, self.part(at), :],
                0,
                1 << order[stage],
            )
            for at, order in enumerate(self.orders)
        ]

    def take(self, stage):
        for at, order in enumerate(self.orders):
            self.mover.arrived(self.waits[at])
            part = self.part(at)
            self.held[stage, part, :] = jnp.where(
                self.bits[order[stage]] == 1,
                self.got[stage, part, :],
                self.current(stage)[part, :],
            )


def route_all(routes, stages):
    for route in routes:
        route.send(0)
    for stage in range(stages):
        for route in routes:
            route.take(stage)
            if stage + 1 < stages:
                route.send(stage + 1)


def tok_peers(n_tok):
    return [(dist, 0) for dist in range(1, n_tok)]


class Gather:
    def __init__(self, mover, src, dst, order):
        self.mover, self.src, self.dst, self.order = mover, src, dst, order
        self.have = {0: None}
        self.depth = 0
        self.own = mover.start(src, dst.at[0])
        for dist in order:
            self.have[dist] = mover.start(src, dst.at[dist], 0, dist)

    def relay(self):
        order = self.order
        for at, dist in enumerate(order[:-1]):
            for known in [
                sum(bits) for bits in subsets(order[:at])
            ]:
                held = known ^ dist
                self.mover.arrived(self.have[held])
                for later in order[at + 1 :]:
                    self.have[held ^ later] = self.mover.start(
                        self.dst.at[held], self.dst.at[held ^ later], 0, later
                    )


    def settle(self):
        self.mover.arrived(self.own)
        for entry in self.have.values():
            if entry is not None:
                self.mover.arrived(entry)


def subsets(items):
    found = [()]
    for item in items:
        found = found + [entry + (item,) for entry in found]
    return found


def swap_halves(first, second, odd):
    lane = lax.broadcasted_iota(jnp.int32, first.shape, 1)
    half = first.shape[1] // 2

    def turn(values):
        return jnp.concatenate([values[:, half:], values[:, :half]], axis=1)

    if odd:
        return jnp.where(lane < half, turn(first), second)
    return jnp.where(lane < half, first, turn(second))


def swap_pieces(values, count, places, in_major, out_major):
    rows, width = values.shape[-2:]
    lanes = 128

    def block(ref, at, lane):
        if ref.ndim == 2:
            return ref, (slice(None), pl.ds(at * (ref.shape[1] // count) + lane, lanes))
        lead = (0, at) if ref.shape[0] == 1 else (at, 0)
        return ref, lead + (slice(None), pl.ds(lane, lanes))

    def body(src, dst):
        def load(at, lane):
            ref, where = block(src, at, lane)
            return ref[where]

        for to in range(count):
            for pair in range(count // 2):
                lane = (to // 2) * lanes
                ref, where = block(dst, to, pair * lanes)
                ref[where] = swap_halves(
                    load(2 * pair, lane), load(2 * pair + 1, lane), to % 2 == 1
                )

    def spec(major):
        if major is None:
            full = (rows, width if values.ndim == 2 else width * count)
            return full, pl.BlockSpec(full, lambda at: (0, 0))
        piece = width if values.ndim == 4 else width // count
        if major:
            return (places, count, rows, piece), pl.BlockSpec(
                (1, count, rows, piece), lambda at: (at, 0, 0, 0)
            )
        return (count, places, rows, piece), pl.BlockSpec(
            (count, 1, rows, piece), lambda at: (0, at, 0, 0)
        )

    shape, out_spec = spec(out_major)
    return pl.pallas_call(
        body,
        grid=(places,),
        out_shape=jax.ShapeDtypeStruct(shape, values.dtype),
        in_specs=[spec(in_major)[1]],
        out_specs=out_spec,
        compiler_params=pltpu.CompilerParams(vmem_limit_bytes=60 * 2**20),
    )(values)


def choose(load, count, bits, turn=0):
    held = [load(at) for at in range(count)]
    for at, bit in enumerate(bits):
        want = 1 - ((turn >> at) & 1)
        held = [
            jnp.where(bit == want, held[pos + 1], held[pos]) for pos in range(0, len(held), 2)
        ]
    return held[0]


def code_bits(code_i, which, first, count):
    return [code_i[which, first + at] for at in range(count)]


def swap_lanes(store, load, bits, rows, blk, places):
    step = 32

    def rows_of(at, carry):
        part = span(at, step)
        held = [load(part, pl.ds(pos * blk, blk)) for pos in range(places)]
        for place in range(places):
            store(
                part,
                pl.ds(place * blk, blk),
                choose(lambda pos: held[pos], places, bits, place),
            )
        return carry

    lax.fori_loop(0, rows // step, rows_of, 0)


class LowSum:
    def __init__(self, mover, n_tok, parts, core_got, mine, got, steps, taken, final):
        self.mover, self.n_tok = mover, n_tok
        self.parts, self.core_got, self.mine, self.got = parts, core_got, mine, got
        self.steps, self.taken, self.final = steps, taken, final
        self.me_hid = lax.axis_index("hid")
        self.core = self.me_hid % 2
        self.chips = [2 * dist for dist in range(1, n_tok)]

    def chunk(self, hid_index):
        return lax.axis_index("tok") ^ (hid_index // 2)

    def begin(self):
        self.waits = [self.mover.start(self.parts.at[:, 1 - self.core], self.core_got, 0, 1)]

    def fold_core(self):
        self.mover.arrived(self.waits[0])
        for at in range(self.n_tok):
            self.mine[at] = (self.parts[at, self.core] + self.core_got[at]).astype(jnp.bfloat16)
        self.waits = [
            self.mover.start(
                self.mine.at[self.chunk(self.me_hid ^ dist)], self.got.at[at], 0, dist
            )
            for at, dist in enumerate(self.chips)
        ]

    def gather_parts(self):
        total = self.mine[self.chunk(self.me_hid)].astype(jnp.float32)
        for at, entry in enumerate(self.waits):
            self.mover.arrived(entry)
            total = total + self.got[at].astype(jnp.float32)
        self.steps[0] = total.astype(jnp.bfloat16)
        self.waits = [self.mover.start(self.steps.at[0], self.taken.at[0], 2)]

    def step(self, at):
        self.mover.arrived(self.waits[0])
        self.steps[at] = (
            self.steps[at - 1].astype(jnp.float32) + self.taken[at - 1].astype(jnp.float32)
        ).astype(jnp.bfloat16)

    def middle(self):
        self.step(1)
        self.waits = [self.mover.start(self.steps.at[1], self.taken.at[1], 1)]

    def share(self):
        self.step(2)
        here = self.final.at[self.chunk(self.me_hid), self.core]
        self.waits = [
            self.mover.start(self.steps.at[2], here, 0, dist) for dist in [0] + self.chips
        ]

    def spread_core(self):
        for entry in self.waits:
            self.mover.arrived(entry)
        mine = self.final.at[:, self.core]
        self.waits = [self.mover.start(mine, mine, 0, 1)]

    def settle(self):
        self.mover.arrived(self.waits[0])

    def rows(self, dist, lanes):
        found = self.final[dist, :, :, lanes]
        return found.reshape(found.shape[0] * found.shape[1], found.shape[2])

    @staticmethod
    def copies(n_tok):
        return 2 * n_tok + 3

    @staticmethod
    def scratch(rows, width, n_tok):
        half = rows // 2
        return (
            pltpu.VMEM((n_tok, half, width), jnp.float32),
            pltpu.VMEM((n_tok, half, width), jnp.bfloat16),
            pltpu.VMEM((n_tok - 1, half, width), jnp.bfloat16),
            pltpu.VMEM((3, half, width), jnp.bfloat16),
            pltpu.VMEM((2, half, width), jnp.bfloat16),
            pltpu.VMEM((n_tok, 2, half, width), jnp.bfloat16),
        )


def bring_in(
    tokens, cotangent, codes, in_left, out_right, out_blocks, first_t, right_t, left_t
):
    n_tok, n_hid = lax.axis_size("tok"), lax.axis_size("hid")
    _, groups, slots, deep, blk = first_t.shape
    wide, rank = in_left.shape
    rows, width = tokens.shape
    whole = rows * n_tok
    far = hid_shifts(n_hid)

    places = 1 + len(far)
    near_shifts = in_group_shifts(groups)
    per, fine = left_t.shape[0], left_t.shape[2]
    early = groups // 2

    def body(
        tok_i, cot_i, code_i, left_i, right_i, second_i, first_i, r_i, l_i,
        pick_o, own_o, sum_o, low_o, gr_o, gl_o, outf_o, backf_o, gearly_o, gfirst_o, gsecond_o,
        send, recv, got_mid, held_mid, got_low, held_low, x_all, parts,
        core_got, low_mine, low_got, steps, taken, final,
        first_o, r_o, l_o, hidden, slope, stage_far, stage_first, stage_second,
    ):
        me = lax.axis_index("tok")
        near_bits = n_tok.bit_length() - 1
        far_bits = n_hid.bit_length() - 1
        lows = [code_bits(code_i, which, 0, near_bits) for which in range(2)]
        highs = [code_bits(code_i, which, near_bits, far_bits) for which in range(2)]
        own_bits = [
            [bit ^ ((me >> at) & 1) for at, bit in enumerate(lows[which])] for which in range(2)
        ]
        greet(tok_peers(n_tok) + [(0, dist) for dist in (1, *range(2, n_hid, 2))])
        mover = Mover(send, recv)
        part = [pl.ds(dist * rows, rows) for dist in range(n_tok)]
        first_waits, far_waits, row_waits = {}, [], []
        arrived = {}

        def send_first(group):
            first_waits[group] = [
                mover.start(
                    first_i.at[me ^ dist, group], first_o.at[group, :, span(me, deep), :], dist
                )
                for dist in (2, 3, 1, 0)
            ]

        def spread(at, dist):
            for pos, far_dist in enumerate(far):
                far_waits.append(
                    mover.start(
                        x_all.at[at, 0, part[dist], :],
                        x_all.at[at, 1 + pos, part[dist], :],
                        0,
                        far_dist,
                    )
                )

        routes = [
            Route(mover, src, got_mid.at[at], held_mid.at[at], highs[at])
            for at, src in enumerate((cot_i, tok_i))
        ]
        for route in routes:
            route.send(0)
        send_first(0)
        last = far_bits - 1
        for stage in range(far_bits):
            for at, route in enumerate(routes):
                route.take(stage)
                if stage < last:
                    route.send(stage + 1)
                    continue

                def store_near(rows_at, lanes, value):
                    x_all[at, 0, rows_at, lanes] = value

                swap_lanes(
                    store_near,
                    lambda rows_at, lanes: held_mid[at, last, rows_at, lanes],
                    lows[at], rows, blk, width // blk,
                )
                for dist in (1, 2):
                    arrived[at, dist] = mover.start(
                        x_all.at[at, 0, part[0], :], x_all.at[at, 0, part[dist], :], dist
                    )
        for at in range(2):
            spread(at, 0)
        more = [
            Route(mover, src, got_low.at[at], held_low.at[at], highs[at])
            for at, src in enumerate((right_i, left_i))
        ]
        route_all(more, far_bits)
        for at in range(2):
            pick_o[at] = held_low[at, last]
        send_first(1)
        for at in range(2):
            mover.arrived(arrived[at, 1])
            spread(at, 1)
        for at in range(2):
            mover.arrived(arrived[at, 2])
            arrived[at, 3] = mover.start(
                x_all.at[at, 0, part[2], :], x_all.at[at, 0, part[3], :], 1
            )
        send_first(2)
        for at in range(2):
            spread(at, 2)
        half = rows // 2
        for dist in range(n_tok):
            for at in range(2):
                if dist == 3:
                    mover.arrived(arrived[at, 3])
                own_o[at, part[dist], :] = choose(
                    lambda pos: x_all[at, 0, part[dist], pl.ds(pos * blk, blk)], n_tok, own_bits[at]
                )
            for side in range(2):
                piece = pl.ds(dist * rows + side * half, half)
                parts[dist, side, :, :rank] = jnp.dot(
                    own_o[1, piece, :], pick_o[1], preferred_element_type=jnp.float32
                )
                parts[dist, side, :, rank:] = dot_cols(own_o[0, piece, :], pick_o[0])
        low = LowSum(mover, n_tok, parts, core_got, low_mine, low_got, steps, taken, final)
        low.begin()
        low.fold_core()
        spread(0, 3)
        low.gather_parts()
        for dist in (2, 3, 1, 0):
            row_waits.append(mover.start(r_i.at[me ^ dist], r_o.at[me], dist))
            row_waits.append(mover.start(l_i.at[:, me ^ dist], l_o.at[me], dist))
        low.middle()
        spread(1, 3)
        low.share()
        for group in range(3, groups):
            send_first(group)
        low.spread_core()
        low.settle()
        scale = lax.rsqrt(jnp.float32(whole))
        for entry in row_waits + far_waits:
            mover.arrived(entry)
        low_in = jnp.concatenate([low.rows(dist, pl.ds(0, rank)) for dist in range(n_tok)], axis=0)
        low_back = jnp.concatenate(
            [low.rows(dist, pl.ds(rank, rank)) for dist in range(n_tok)], axis=0
        )
        touched = set()
        staged, far_sent = {}, {}
        far_turns = stage_far.shape[0]
        for group in range(groups):
            turn, far_turn = group % 2, group % far_turns

            def spot(k):
                if k < len(near_shifts):
                    return 0, pl.ds((group ^ near_shifts[k]) * blk, blk)
                return k - len(near_shifts) + 1, pl.ds(group * blk, blk)

            def second(k):
                return second_i[pl.ds(group * per, per), k].reshape(per * fine, blk)

            left = l_o[group].reshape(per * fine, rank)
            for entry in first_waits[group]:
                mover.arrived(entry)
            for entry in far_sent.pop(group - far_turns, []) + staged.pop(group - 2, []):
                mover.sent(entry)
            total = jnp.dot(low_in, r_o[group], preferred_element_type=jnp.float32)
            for k in range(slots):
                place, lanes = spot(k)
                total = total + jnp.dot(
                    x_all[1, place, :, lanes],
                    first_o[group, k],
                    preferred_element_type=jnp.float32,
                )
            active, slopes = gelu_parts(total)
            hidden[...] = active.astype(jnp.bfloat16)
            total = dot_cols(low_back, left)
            for k in range(slots):
                place, lanes = spot(k)
                total = total + dot_cols(x_all[0, place, :, lanes], second(k))
            slope[...] = (total * slopes).astype(jnp.bfloat16)
            low_one = jnp.dot(hidden[...], left, preferred_element_type=jnp.float32)
            low_two = dot_cols(slope[...], r_o[group])
            if group == 0:
                low_o[:, :rank] = low_one
                low_o[:, rank:] = low_two
            else:
                low_o[:, :rank] += low_one
                low_o[:, rank:] += low_two
            entries = []
            for k in range(slots):
                place, lanes = spot(k)
                values = (
                    jnp.dot(hidden[...], second(k), preferred_element_type=jnp.float32),
                    dot_cols(slope[...], first_o[group, k]),
                )
                for which in range(2):
                    if k >= len(near_shifts):
                        stage_far[far_turn, which, place - 1] = values[which].astype(jnp.bfloat16)
                    elif (which, group ^ near_shifts[k]) in touched:
                        sum_o[which, :, lanes] = (
                            sum_o[which, :, lanes].astype(jnp.float32) + values[which]
                        ).astype(jnp.bfloat16)
                    else:
                        touched.add((which, group ^ near_shifts[k]))
                        sum_o[which, :, lanes] = values[which].astype(jnp.bfloat16)
            lanes = pl.ds(group * blk, blk)
            far_sent[group] = [
                mover.start(
                    stage_far.at[far_turn, which, pos],
                    dst.at[pos, :, lanes],
                    0,
                    far_dist if group < early else 0,
                )
                for which, dst in enumerate((outf_o, backf_o))
                for pos, far_dist in enumerate(far)
            ]
            for k in range(slots):
                place, lanes = spot(k)
                stage_first[turn, k] = (
                    scale * dot_rows(x_all[1, place, :, lanes], slope[...])
                ).astype(jnp.bfloat16)
                stage_second[turn, :, k] = (
                    (scale * dot_rows(hidden[...], x_all[0, place, :, lanes]))
                    .astype(jnp.bfloat16)
                    .reshape(per, fine, blk)
                )
            if group < early:
                for dist in (2, 3, 1, 0):
                    entries.append(
                        mover.start(
                            stage_first.at[turn, :, span(me ^ dist, deep), :],
                            gearly_o.at[me, group],
                            dist,
                        )
                    )
            else:
                entries.append(mover.start(stage_first.at[turn], gfirst_o.at[group - early]))
            entries.append(
                mover.start(stage_second.at[turn], gsecond_o.at[pl.ds(group * per, per)])
            )
            gr_o[group] = (scale * dot_rows(low_in, slope[...])).astype(jnp.bfloat16)
            gl_o[group] = (
                (scale * dot_rows(hidden[...], low_back))
                .astype(jnp.bfloat16)
                .reshape(per, fine, rank)
            )
            staged[group] = entries
        mover.finish()

    f32 = jnp.float32
    return run_exchange(
        body,
        (
            tokens, cotangent, codes, in_left, out_right, out_blocks,
            first_t, right_t, left_t,
        ),
        [
            (2, wide, rank),
            (2, whole, blk),
            (2, whole, width),
            ((whole, 2 * rank), f32),
            (groups, rank, blk),
            (groups, per, fine, rank),
            (places - 1, whole, width),
            (places - 1, whole, width),
            (n_tok, early, slots, deep, blk),
            (groups - early, slots, blk, blk),
            out_blocks.shape,
        ],
        8 * len(far) + groups * n_tok + 6 + 2 * n_tok * len(far) + 2 * n_tok
        + LowSum.copies(n_tok) + (2 * len(far) + n_tok + 1) * groups,
        1,
        (0, 1, 3, 4, 5),
        (
            pltpu.VMEM((2, len(far), rows, width), jnp.bfloat16),
            pltpu.VMEM((2, len(far), rows, width), jnp.bfloat16),
            pltpu.VMEM((2, len(far), wide, rank), jnp.bfloat16),
            pltpu.VMEM((2, len(far), wide, rank), jnp.bfloat16),
            pltpu.VMEM((2, places, whole, width), jnp.bfloat16),
            pltpu.VMEM((n_tok, 2, rows // 2, 2 * rank), jnp.float32),
        )
        + LowSum.scratch(rows, 2 * rank, n_tok)
        + (
            pltpu.VMEM((groups, slots, blk, blk), jnp.bfloat16),
            pltpu.VMEM((groups, rank, blk), jnp.bfloat16),
            pltpu.VMEM((groups, per, fine, rank), jnp.bfloat16),
            pltpu.VMEM((whole, blk), jnp.bfloat16),
            pltpu.VMEM((whole, blk), jnp.bfloat16),
            pltpu.VMEM((3, 2, places - 1, whole, blk), jnp.bfloat16),
            pltpu.VMEM((2, slots, blk, blk), jnp.bfloat16),
            pltpu.VMEM((2, per, slots, fine, blk), jnp.bfloat16),
        ),
        in_smem=(2,),
        out_vmem=(0, 1, 2, 3, 4, 5),
    )


def send_out(
    low_parts, own_sums, codes, own, picks,
    out_far, back_far, grads, right_g, left_g,
):
    n_tok, n_hid = lax.axis_size("tok"), lax.axis_size("hid")
    far = hid_shifts(n_hid)
    _, whole, width = out_far.shape
    rows = whole // n_tok
    rank = picks.shape[2]
    groups, slots, full, blk = grads.shape
    deep = full // n_tok
    early = width // 2
    _, per, fine, _ = left_g.shape
    wide = picks.shape[1]

    def body(
        low_i, sum_i, code_i, own_i, pick_i,
        outf_i, backf_i, grad_i, r_i, l_i,
        layer_o, gtok_o, gleft_o, gright_o, grad_o, r_o, l_o,
        send, recv, held, kept, got_one, pair, got_two, low_grad, spots,
        got_mid, held_mid, got_low, held_low,
        core_got, low_mine, low_got, steps, taken, final,
    ):
        me = lax.axis_index("tok")
        scale = lax.rsqrt(jnp.float32(whole))
        near_bits = n_tok.bit_length() - 1
        far_bits = n_hid.bit_length() - 1
        lows = [code_bits(code_i, which, 0, near_bits) for which in range(2)]
        highs = [code_bits(code_i, which, near_bits, far_bits) for which in range(2)]
        own_bits = [
            [bit ^ ((me >> at) & 1) for at, bit in enumerate(lows[which])] for which in range(2)
        ]
        greet(tok_peers(n_tok) + [(0, dist) for dist in (1, *range(2, n_hid, 2))])
        mover = Mover(send, recv)
        part = [pl.ds(dist * rows, rows) for dist in range(n_tok)]
        fars = (outf_i, backf_i)
        low = LowSum(mover, n_tok, low_i, core_got, low_mine, low_got, steps, taken, final)
        low.begin()
        waits = {}

        def send_far(which, dist):
            for pos, far_dist in enumerate(far):
                waits[which, dist, pos] = [
                    mover.start(
                        fars[which].at[pos, part[dist], lanes],
                        held.at[which, pos, part[dist], lanes],
                        0,
                        to,
                    )
                    for lanes, to in ((pl.ds(early, width - early), far_dist), (pl.ds(0, early), 0))
                ]

        def send_grads(group):
            for dist in (2, 3, 1, 0):
                mover.start(
                    grad_i.at[group, :, span(me ^ dist, deep), :], grad_o.at[me, group], dist
                )

        first, second = {}, {}

        def settle(which, dist):
            total = sum_i[which, part[dist], :].astype(jnp.float32) + jnp.dot(
                low.rows(dist, pl.ds(which * rank, rank)),
                spots[which],
                preferred_element_type=jnp.float32,
            )
            for pos in range(len(far)):
                for entry in waits[which, dist, pos]:
                    mover.arrived(entry)
                total = total + held[which, pos, part[dist], :].astype(jnp.float32)
            kept[which, part[dist], :] = total.astype(jnp.bfloat16)
            if dist % 2 == 1:
                first[which, dist - 1] = mover.start(
                    kept.at[which, part[dist], :], got_one.at[which, dist // 2], 1
                )

        def pass_on(which):
            mover.arrived(first[which, 2])
            pair[which] = (
                kept[which, part[2], :].astype(jnp.float32)
                + got_one[which, 1].astype(jnp.float32)
            ).astype(jnp.bfloat16)
            second[which] = mover.start(pair.at[which], got_two.at[which], 2)

        def close(which):
            mover.arrived(first[which, 0])
            mover.arrived(second[which])
            pair[which + 2] = (
                kept[which, part[0], :].astype(jnp.float32)
                + got_one[which, 0].astype(jnp.float32)
                + got_two[which].astype(jnp.float32)
            ).astype(jnp.bfloat16)
            route = Route(
                mover, pair.at[which + 2], got_mid.at[which], held_mid.at[which], highs[which]
            )
            route.send(0)
            return route

        send_grads(0)
        low.fold_core()
        send_far(0, 3)
        for which in range(2):
            weight = pick_i[which].astype(jnp.float32)
            if which == 1:
                weight = weight.T
            for place in range(width // blk):
                here = 1
                for at, bit in enumerate(own_bits[which]):
                    here = here * (bit if (place >> at) & 1 else 1 - bit)
                spots[which, :, pl.ds(place * blk, blk)] = (
                    weight * here.astype(jnp.float32)
                ).astype(jnp.bfloat16)
        low.gather_parts()
        send_far(0, 1)
        low.middle()
        send_far(0, 2)
        low.share()
        send_far(0, 0)
        send_grads(1)
        low.spread_core()
        low.settle()
        settle(0, 3)
        settle(0, 1)
        for dist in (3, 1, 2, 0):
            send_far(1, dist)
        settle(0, 2)
        pass_on(0)
        settle(0, 0)
        low_mid = jnp.concatenate([low.rows(dist, pl.ds(0, rank)) for dist in range(n_tok)], axis=0)
        low_grad[0] = (scale * dot_rows(low_mid, own_i[0])).astype(jnp.bfloat16)
        low_back = jnp.concatenate(
            [low.rows(dist, pl.ds(rank, rank)) for dist in range(n_tok)], axis=0
        )
        low_grad[1] = (scale * dot_rows(own_i[1], low_back)).astype(jnp.bfloat16)
        settle(1, 3)
        settle(1, 1)
        routes = [close(0)]
        more = [
            Route(mover, low_grad.at[which], got_low.at[which], held_low.at[which], highs[which])
            for which in range(2)
        ]
        for route in more:
            route.send(0)
        settle(1, 2)
        pass_on(1)
        for dist in (2, 3, 1, 0):
            mover.start(r_i.at[me ^ dist], r_o.at[me], dist)
            mover.start(l_i.at[me ^ dist], l_o.at[:, me], dist)
        settle(1, 0)

        def advance(route, stage):
            route.take(stage)
            if stage + 1 < far_bits:
                route.send(stage + 1)

        last = far_bits - 1
        for stage in range(far_bits):
            for route in routes + more:
                advance(route, stage)
        routes.append(close(1))
        gright_o[...] = held_low[0, last]
        gleft_o[...] = held_low[1, last]
        outs = (layer_o, gtok_o)
        for which in range(2):
            if which == 1:
                for stage in range(far_bits):
                    advance(routes[1], stage)

            def store_out(rows_at, lanes, value):
                outs[which][rows_at, lanes] = value

            swap_lanes(
                store_out,
                lambda rows_at, lanes: held_mid[which, last, rows_at, lanes],
                lows[which], rows, blk, width // blk,
            )
        mover.finish()

    return run_exchange(
        body,
        (
            low_parts, own_sums, codes, own, picks,
            out_far, back_far, grads, right_g, left_g,
        ),
        [
            (rows, width),
            (rows, width),
            (wide, rank),
            (rank, wide),
            (n_tok, groups, slots, deep, blk),
            (n_tok, rank, blk),
            (per, n_tok, fine, rank),
        ],
        n_tok * (4 * len(far) + groups + 2) + 8 + 8 * len(far) + LowSum.copies(n_tok),
        2,
        (0, 1, 3, 4),
        (
            pltpu.VMEM((2, len(far), whole, width), jnp.bfloat16),
            pltpu.VMEM((2, whole, width), jnp.bfloat16),
            pltpu.VMEM((2, 2, rows, width), jnp.bfloat16),
            pltpu.VMEM((4, rows, width), jnp.bfloat16),
            pltpu.VMEM((2, rows, width), jnp.bfloat16),
            pltpu.VMEM((2, wide, rank), jnp.bfloat16),
            pltpu.VMEM((2, rank, width), jnp.bfloat16),
            pltpu.VMEM((2, len(far), rows, width), jnp.bfloat16),
            pltpu.VMEM((2, len(far), rows, width), jnp.bfloat16),
            pltpu.VMEM((2, len(far), wide, rank), jnp.bfloat16),
            pltpu.VMEM((2, len(far), wide, rank), jnp.bfloat16),
        )
        + LowSum.scratch(rows, 2 * rank, n_tok),
        in_smem=(2,),
        out_vmem=(0, 1, 2, 3),
    )


def local_moved(
    tokens,
    in_blocks,
    in_left,
    in_right,
    in_lists,
    out_blocks,
    out_left,
    out_right,
    out_lists,
    cotangent,
):
    hid_blocks, slots, deep, blk = in_blocks.shape
    n_tok = lax.axis_size("tok")
    groups = tokens.shape[1] // blk
    per = hid_blocks // groups
    rank = in_left.shape[1]
    fine = blk // n_tok
    heads = jnp.stack([out_lists, in_lists])[:, 0, 0]
    codes = (heads[:, None] >> jnp.arange(8, dtype=jnp.int32)[None, :]) & 1
    first_t = swap_pieces(
        in_blocks.reshape(groups, per, slots * deep, blk), per, groups, True, False
    ).reshape(n_tok, groups, slots, deep, blk)
    right_t = swap_pieces(in_right, per, 1, None, False).reshape(n_tok, rank, blk)
    (
        picks,
        own,
        own_sums,
        low_parts,
        right_g,
        left_g,
        out_far,
        back_far,
        grad_early,
        grad_first,
        grad_out_blocks,
    ) = bring_in(
        tokens,
        cotangent,
        codes,
        in_left,
        out_right,
        out_blocks,
        first_t,
        right_t,
        out_left.reshape(per, n_tok, fine, rank),
    )
    layer_out, grad_tokens, grad_in_left, grad_out_right, grad_got, right_got, left_got = send_out(
        low_parts.reshape(n_tok, 2, tokens.shape[0] // 2, 2 * rank),
        own_sums,
        codes,
        own,
        picks,
        out_far,
        back_far,
        grad_first,
        right_g,
        left_g,
    )
    grad_in_blocks = jnp.concatenate(
        [
            swap_pieces(
                values.reshape(n_tok, groups // 2, slots * deep, blk), per, groups // 2, False, True
            )
            for values in (grad_early, grad_got)
        ],
        axis=0,
    ).reshape(hid_blocks, slots, deep, blk)
    grad_in_right = swap_pieces(right_got.reshape(n_tok, 1, rank, blk), per, 1, False, None)
    return (
        layer_out,
        grad_tokens,
        grad_in_blocks,
        grad_in_left,
        grad_in_right,
        grad_out_blocks,
        left_got.reshape(out_left.shape),
        grad_out_right,
    )


def power_of_two(count):
    return count & (count - 1) == 0


def local(*arrays):
    tokens, in_blocks = arrays[0], arrays[1]
    n_tok = lax.axis_size("tok")
    n_hid = lax.axis_size("hid")
    whole_groups = (
        n_tok == 4
        and n_hid == 2 * n_tok
        and tokens.shape[1] == n_tok * in_blocks.shape[3]
        and in_blocks.shape[0] == n_tok * n_tok
    )
    return local_moved(*arrays) if whole_groups else local_gathered(*arrays)


def solution(mesh):
    return jax.shard_map(
        local,
        mesh=mesh,
        in_specs=(
            P("tok", "hid"),
            P("hid", None, "tok", None),
            P(("hid", "tok"), None),
            P(None, ("hid", "tok")),
            P(),
            P("hid", None, "tok", None),
            P(("hid", "tok"), None),
            P(None, ("hid", "tok")),
            P(),
            P("tok", "hid"),
        ),
        out_specs=(
            P("tok", "hid"),
            P("tok", "hid"),
            P("hid", None, "tok", None),
            P(("hid", "tok"), None),
            P(None, ("hid", "tok")),
            P("hid", None, "tok", None),
            P(("hid", "tok"), None),
            P(None, ("hid", "tok")),
        ),
        check_vma=False,
    )
```

```python
import jax
import jax.numpy as jnp
from jax import lax
from jax.experimental import pallas as pl
from jax.experimental.pallas import tpu as pltpu
from jax.sharding import PartitionSpec as P

D = 8192
BLK = 256


def gelu_parts(preact):
    inner_coef = 0.7978845608028654
    cubic_coef = 0.044715
    inner_arg = inner_coef * (preact + cubic_coef * preact * preact * preact)
    tanh_val = jnp.tanh(inner_arg)
    active = 0.5 * preact * (1.0 + tanh_val)
    slopes = 0.5 * (1.0 + tanh_val) + 0.5 * preact * (1.0 - tanh_val * tanh_val) * inner_coef * (
        1.0 + 3.0 * cubic_coef * preact * preact
    )
    return (active, slopes)


def dot_rows(left_arr, right_arr):
    return lax.dot_general(
        left_arr, right_arr, (((0,), (0,)), ((), ())), preferred_element_type=jnp.float32
    )


def dot_cols(left_arr, right_arr):
    return lax.dot_general(
        left_arr, right_arr, (((1,), (1,)), ((), ())), preferred_element_type=jnp.float32
    )


def rank_sum(values):
    return lax.psum(values, "hid")


def own_lists(lists, hid_blocks):
    return lax.dynamic_slice_in_dim(lists, lax.axis_index("hid") * hid_blocks, hid_blocks, 0)


def gather_in(values, lists, hid_blocks, blk_width):
    whole = lax.all_gather(values, "hid", axis=1, tiled=True)
    mine = own_lists(lists, hid_blocks)
    blocks = whole.reshape(whole.shape[0], whole.shape[1] // blk_width, blk_width)
    return jnp.stack(
        [
            jnp.stack(
                [
                    lax.dynamic_index_in_dim(blocks, mine[at, slot], axis=1, keepdims=False)
                    for at in range(hid_blocks)
                ],
                axis=1,
            )
            for slot in range(mine.shape[1])
        ],
        axis=1,
    )


def scatter_out(parts, lists, hid_blocks):
    mine = own_lists(lists, hid_blocks)
    picker = (mine.T[:, :, None] == jnp.arange(D // BLK, dtype=jnp.int32)[None, None, :]).astype(
        jnp.float32
    )
    dense = jnp.einsum("nsho,shc->nco", parts, picker, precision=lax.Precision.HIGHEST)
    return lax.psum_scatter(
        dense.reshape(dense.shape[0], -1), "hid", scatter_dimension=1, tiled=True
    )


def route_in(values, lists, hid_blocks, blk_width):
    return gather_in(values, lists, hid_blocks, blk_width)


def route_out(parts, lists, hid_blocks):
    return scatter_out(parts, lists, hid_blocks)


def local_gathered(
    tokens,
    in_blocks,
    in_left,
    in_right,
    in_lists,
    out_blocks,
    out_left,
    out_right,
    out_lists,
    cotangent,
):
    row_count, col_span = tokens.shape
    hid_blocks = in_blocks.shape[0]
    slot_count = in_blocks.shape[1]
    blk_width = in_blocks.shape[3]
    tok_count = lax.axis_size("tok")
    w_first, w_second, left_one, right_one, left_two, right_two = (
        lax.all_gather(in_blocks, "tok", axis=2, tiled=True),
        lax.all_gather(out_blocks, "tok", axis=2, tiled=True),
        lax.all_gather(in_left, "tok", axis=0, tiled=True),
        lax.all_gather(in_right, "tok", axis=1, tiled=True),
        lax.all_gather(out_left, "tok", axis=0, tiled=True),
        lax.all_gather(out_right, "tok", axis=1, tiled=True),
    )
    low_in, low_back = rank_sum(
        (
            jnp.dot(tokens, left_one, preferred_element_type=jnp.float32),
            dot_cols(cotangent, right_two),
        )
    )
    low_in = low_in.astype(jnp.bfloat16)
    low_back = low_back.astype(jnp.bfloat16)
    gathered = route_in(tokens, in_lists, hid_blocks, blk_width)
    group_count = gathered.shape[2]
    per_group = hid_blocks // group_count
    first_r = w_first.reshape(group_count, per_group, slot_count, blk_width, blk_width)
    second_r = w_second.reshape(group_count, per_group, slot_count, blk_width, blk_width)
    preact = jnp.einsum(
        "nseb,eqsbf->neqf", gathered, first_r, preferred_element_type=jnp.float32
    ).reshape(row_count, -1)
    preact = preact + jnp.dot(low_in, right_one, preferred_element_type=jnp.float32)
    active, slopes = gelu_parts(preact)
    hidden = active.astype(jnp.bfloat16)
    low_mid = rank_sum(jnp.dot(hidden, left_two, preferred_element_type=jnp.float32)).astype(
        jnp.bfloat16
    )
    hidden_r = hidden.reshape(row_count, group_count, per_group, blk_width)
    out_parts = jnp.einsum(
        "neqf,eqsfo->nseo", hidden_r, second_r, preferred_element_type=jnp.float32
    )
    sparse_out = route_out(out_parts, out_lists, hid_blocks)
    layer_out = (
        sparse_out + jnp.dot(low_mid, right_two, preferred_element_type=jnp.float32)
    ).astype(jnp.bfloat16)
    grad_in = route_in(cotangent, out_lists, hid_blocks, blk_width)
    grad_hidden = jnp.einsum(
        "nseo,eqsfo->neqf", grad_in, second_r, preferred_element_type=jnp.float32
    ).reshape(row_count, -1)
    grad_hidden = grad_hidden + dot_cols(low_back, left_two)
    grad_pre = (grad_hidden * slopes).astype(jnp.bfloat16)
    low_grad = rank_sum(dot_cols(grad_pre, right_one)).astype(jnp.bfloat16)
    grad_pre_r = grad_pre.reshape(row_count, group_count, per_group, blk_width)
    back_parts = jnp.einsum(
        "neqf,eqsbf->nseb", grad_pre_r, first_r, preferred_element_type=jnp.float32
    )
    sparse_back = route_out(back_parts, in_lists, hid_blocks)
    grad_tokens = (sparse_back + dot_cols(low_grad, left_one)).astype(jnp.bfloat16)
    loss_scale = lax.rsqrt(jnp.float32(row_count * tok_count))
    terms = (
        loss_scale
        * jnp.einsum(
            "nseb,neqf->eqsbf", gathered, grad_pre_r, preferred_element_type=jnp.float32
        ).reshape(w_first.shape),
        loss_scale
        * jnp.einsum(
            "neqf,nseo->eqsfo", hidden_r, grad_in, preferred_element_type=jnp.float32
        ).reshape(w_second.shape),
        loss_scale * dot_rows(tokens, low_grad),
        loss_scale * dot_rows(low_in, grad_pre),
        loss_scale * dot_rows(hidden, low_back),
        loss_scale * dot_rows(low_mid, cotangent),
    )
    shares = (
        lax.psum_scatter(
            terms[0].astype(jnp.bfloat16), "tok", scatter_dimension=2, tiled=True
        ).astype(jnp.float32),
        lax.psum_scatter(
            terms[1].astype(jnp.bfloat16), "tok", scatter_dimension=2, tiled=True
        ).astype(jnp.float32),
        lax.psum_scatter(
            terms[2].astype(jnp.bfloat16), "tok", scatter_dimension=0, tiled=True
        ).astype(jnp.float32),
        lax.psum_scatter(
            terms[3].astype(jnp.bfloat16), "tok", scatter_dimension=1, tiled=True
        ).astype(jnp.float32),
        lax.psum_scatter(
            terms[4].astype(jnp.bfloat16), "tok", scatter_dimension=0, tiled=True
        ).astype(jnp.float32),
        lax.psum_scatter(
            terms[5].astype(jnp.bfloat16), "tok", scatter_dimension=1, tiled=True
        ).astype(jnp.float32),
    )
    return (
        layer_out,
        grad_tokens,
        shares[0].astype(jnp.bfloat16),
        shares[2].astype(jnp.bfloat16),
        shares[3].astype(jnp.bfloat16),
        shares[1].astype(jnp.bfloat16),
        shares[4].astype(jnp.bfloat16),
        shares[5].astype(jnp.bfloat16),
    )


def in_group_shifts(count):
    return [0] + [1 << bit for bit in range(count.bit_length() - 1)]


def hid_shifts(count):
    return [1 << bit for bit in range(count.bit_length() - 1)]


def span(index, size):
    return pl.ds(pl.multiple_of(index * size, size), size)


def greet(partners):
    me_tok, me_hid = lax.axis_index("tok"), lax.axis_index("hid")
    barrier = pltpu.get_barrier_semaphore()
    for tok_dist, hid_dist in partners:
        pl.semaphore_signal(
            barrier,
            inc=1,
            device_id={"hid": me_hid ^ hid_dist, "tok": me_tok ^ tok_dist},
            device_id_type=pl.DeviceIdType.MESH,
        )
    pl.semaphore_wait(barrier, len(partners))


class Mover:
    def __init__(self, send, recv):
        self.send, self.recv, self.used = send, recv, 0
        self.open_copies = []

    def start(self, src, dst, tok_dist=0, hid_dist=0):
        at = self.used
        self.used += 1
        if tok_dist == 0 and hid_dist == 0:
            copy = pltpu.make_async_copy(src, dst, self.recv.at[at])
            copy.start()
            entry = [copy, True, False]
        else:
            copy = pltpu.make_async_remote_copy(
                src_ref=src,
                dst_ref=dst,
                send_sem=self.send.at[at],
                recv_sem=self.recv.at[at],
                device_id={
                    "hid": lax.axis_index("hid") ^ hid_dist,
                    "tok": lax.axis_index("tok") ^ tok_dist,
                },
                device_id_type=pl.DeviceIdType.MESH,
            )
            copy.start()
            entry = [copy, False, False]
        self.open_copies.append(entry)
        return entry

    def arrived(self, entry):
        if not entry[2]:
            if entry[1]:
                entry[0].wait()
            else:
                entry[0].wait_recv()
            entry[2] = True

    def finish(self):
        for entry in self.open_copies:
            self.arrived(entry)
        for entry in self.open_copies:
            if not entry[1]:
                entry[0].wait_send()


def double_sum(mover, far, totals, held):
    for pos, dist in enumerate(far):
        mover.arrived(mover.start(totals.at[pos], held.at[pos], 0, dist))
        totals[pos + 1] = totals[pos] + held[pos]
    return totals[len(far)]


def run_exchange(
    body, inputs, shapes, copies, ident, in_vmem=(), scratch=(), in_smem=(), out_vmem=()
):
    any_spec = pl.BlockSpec(memory_space=pl.ANY)
    vmem_spec = pl.BlockSpec(memory_space=pltpu.VMEM)
    smem_spec = pl.BlockSpec(memory_space=pltpu.SMEM)
    return pl.pallas_call(
        body,
        out_shape=[
            jax.ShapeDtypeStruct(*shape)
            if isinstance(shape[0], tuple)
            else jax.ShapeDtypeStruct(shape, jnp.bfloat16)
            for shape in shapes
        ],
        in_specs=[
            vmem_spec if at in in_vmem else smem_spec if at in in_smem else any_spec
            for at in range(len(inputs))
        ],
        out_specs=[
            vmem_spec if at in out_vmem else any_spec for at in range(len(shapes))
        ],
        scratch_shapes=[
            pltpu.SemaphoreType.DMA((copies,)),
            pltpu.SemaphoreType.DMA((copies,)),
            *scratch,
        ],
        compiler_params=pltpu.CompilerParams(
            collective_id=ident, has_side_effects=True, vmem_limit_bytes=62 * 2**20
        ),
        cost_estimate=pl.CostEstimate(
            flops=0, bytes_accessed=200_000_000, transcendentals=0
        ),
    )(*inputs)


def gather_order(n_hid, turn):
    shifts = hid_shifts(n_hid)
    wide = shifts[1:]
    turn = turn % len(wide)
    return wide[turn:] + wide[:turn] + shifts[:1]


def tok_peers(n_tok):
    return [(dist, 0) for dist in range(1, n_tok)]


class Route:
    def __init__(self, mover, src, got, held, bits):
        self.mover, self.src, self.got, self.held, self.bits = mover, src, got, held, bits
        top = len(bits) - 1
        self.orders = (
            (top, *range(1, top), 0),
            (*range(1, top), top, 0),
        )
        self.half = src.shape[0] // 2

    def part(self, at):
        return pl.ds(at * self.half, self.half)

    def current(self, stage):
        return self.src if stage == 0 else self.held.at[stage - 1]

    def send(self, stage):
        self.waits = [
            self.mover.start(
                self.current(stage).at[self.part(at), :],
                self.got.at[stage, self.part(at), :],
                0,
                1 << order[stage],
            )
            for at, order in enumerate(self.orders)
        ]

    def take(self, stage):
        for at, order in enumerate(self.orders):
            self.mover.arrived(self.waits[at])
            part = self.part(at)
            self.held[stage, part, :] = jnp.where(
                self.bits[order[stage]] == 1,
                self.got[stage, part, :],
                self.current(stage)[part, :],
            )


def route_all(routes, stages):
    for route in routes:
        route.send(0)
    for stage in range(stages):
        for route in routes:
            route.take(stage)
            if stage + 1 < stages:
                route.send(stage + 1)


def tok_peers(n_tok):
    return [(dist, 0) for dist in range(1, n_tok)]


class Gather:
    def __init__(self, mover, src, dst, order):
        self.mover, self.src, self.dst, self.order = mover, src, dst, order
        self.have = {0: None}
        self.depth = 0
        self.own = mover.start(src, dst.at[0])
        for dist in order:
            self.have[dist] = mover.start(src, dst.at[dist], 0, dist)

    def relay(self):
        order = self.order
        for at, dist in enumerate(order[:-1]):
            for known in [
                sum(bits) for bits in subsets(order[:at])
            ]:
                held = known ^ dist
                self.mover.arrived(self.have[held])
                for later in order[at + 1 :]:
                    self.have[held ^ later] = self.mover.start(
                        self.dst.at[held], self.dst.at[held ^ later], 0, later
                    )


    def settle(self):
        self.mover.arrived(self.own)
        for entry in self.have.values():
            if entry is not None:
                self.mover.arrived(entry)


def subsets(items):
    found = [()]
    for item in items:
        found = found + [entry + (item,) for entry in found]
    return found


def swap_halves(first, second, odd):
    lane = lax.broadcasted_iota(jnp.int32, first.shape, 1)
    half = first.shape[1] // 2

    def turn(values):
        return jnp.concatenate([values[:, half:], values[:, :half]], axis=1)

    if odd:
        return jnp.where(lane < half, turn(first), second)
    return jnp.where(lane < half, first, turn(second))


def swap_pieces(values, count, places, in_major, out_major):
    rows, width = values.shape[-2:]
    lanes = 128

    def block(ref, at, lane):
        if ref.ndim == 2:
            return ref, (slice(None), pl.ds(at * (ref.shape[1] // count) + lane, lanes))
        lead = (0, at) if ref.shape[0] == 1 else (at, 0)
        return ref, lead + (slice(None), pl.ds(lane, lanes))

    def body(src, dst):
        def load(at, lane):
            ref, where = block(src, at, lane)
            return ref[where]

        for to in range(count):
            for pair in range(count // 2):
                lane = (to // 2) * lanes
                ref, where = block(dst, to, pair * lanes)
                ref[where] = swap_halves(
                    load(2 * pair, lane), load(2 * pair + 1, lane), to % 2 == 1
                )

    def spec(major):
        if major is None:
            full = (rows, width if values.ndim == 2 else width * count)
            return full, pl.BlockSpec(full, lambda at: (0, 0))
        piece = width if values.ndim == 4 else width // count
        if major:
            return (places, count, rows, piece), pl.BlockSpec(
                (1, count, rows, piece), lambda at: (at, 0, 0, 0)
            )
        return (count, places, rows, piece), pl.BlockSpec(
            (count, 1, rows, piece), lambda at: (0, at, 0, 0)
        )

    shape, out_spec = spec(out_major)
    return pl.pallas_call(
        body,
        grid=(places,),
        out_shape=jax.ShapeDtypeStruct(shape, values.dtype),
        in_specs=[spec(in_major)[1]],
        out_specs=out_spec,
        compiler_params=pltpu.CompilerParams(vmem_limit_bytes=24 * 2**20),
    )(values)


def choose(load, count, bits, turn=0):
    held = [load(at) for at in range(count)]
    for at, bit in enumerate(bits):
        want = 1 - ((turn >> at) & 1)
        held = [
            jnp.where(bit == want, held[pos + 1], held[pos]) for pos in range(0, len(held), 2)
        ]
    return held[0]


def code_bits(code_i, which, first, count):
    return [code_i[which, first + at] for at in range(count)]


def swap_lanes(store, load, bits, rows, blk, places):
    step = 32

    def rows_of(at, carry):
        part = span(at, step)
        held = [load(part, pl.ds(pos * blk, blk)) for pos in range(places)]
        for place in range(places):
            store(
                part,
                pl.ds(place * blk, blk),
                choose(lambda pos: held[pos], places, bits, place),
            )
        return carry

    lax.fori_loop(0, rows // step, rows_of, 0)


class LowSum:
    def __init__(self, mover, n_tok, parts, core_got, mine, got, steps, taken, final):
        self.mover, self.n_tok = mover, n_tok
        self.parts, self.core_got, self.mine, self.got = parts, core_got, mine, got
        self.steps, self.taken, self.final = steps, taken, final
        self.me_hid = lax.axis_index("hid")
        self.core = self.me_hid % 2
        self.chips = [2 * dist for dist in range(1, n_tok)]

    def chunk(self, hid_index):
        return lax.axis_index("tok") ^ (hid_index // 2)

    def begin(self):
        self.waits = [self.mover.start(self.parts.at[:, 1 - self.core], self.core_got, 0, 1)]

    def fold_core(self):
        self.mover.arrived(self.waits[0])
        for at in range(self.n_tok):
            self.mine[at] = (self.parts[at, self.core] + self.core_got[at]).astype(jnp.bfloat16)
        self.waits = [
            self.mover.start(
                self.mine.at[self.chunk(self.me_hid ^ dist)], self.got.at[at], 0, dist
            )
            for at, dist in enumerate(self.chips)
        ]

    def gather_parts(self):
        total = self.mine[self.chunk(self.me_hid)].astype(jnp.float32)
        for at, entry in enumerate(self.waits):
            self.mover.arrived(entry)
            total = total + self.got[at].astype(jnp.float32)
        self.steps[0] = total.astype(jnp.bfloat16)
        self.waits = [self.mover.start(self.steps.at[0], self.taken.at[0], 2)]

    def step(self, at):
        self.mover.arrived(self.waits[0])
        self.steps[at] = (
            self.steps[at - 1].astype(jnp.float32) + self.taken[at - 1].astype(jnp.float32)
        ).astype(jnp.bfloat16)

    def middle(self):
        self.step(1)
        self.waits = [self.mover.start(self.steps.at[1], self.taken.at[1], 1)]

    def share(self):
        self.step(2)
        here = self.final.at[self.chunk(self.me_hid), self.core]
        self.waits = [
            self.mover.start(self.steps.at[2], here, 0, dist) for dist in [0] + self.chips
        ]

    def spread_core(self):
        for entry in self.waits:
            self.mover.arrived(entry)
        mine = self.final.at[:, self.core]
        self.waits = [self.mover.start(mine, mine, 0, 1)]

    def settle(self):
        self.mover.arrived(self.waits[0])

    def rows(self, dist, lanes):
        found = self.final[dist, :, :, lanes]
        return found.reshape(found.shape[0] * found.shape[1], found.shape[2])

    @staticmethod
    def copies(n_tok):
        return 2 * n_tok + 3

    @staticmethod
    def scratch(rows, width, n_tok):
        half = rows // 2
        return (
            pltpu.VMEM((n_tok, half, width), jnp.float32),
            pltpu.VMEM((n_tok, half, width), jnp.bfloat16),
            pltpu.VMEM((n_tok - 1, half, width), jnp.bfloat16),
            pltpu.VMEM((3, half, width), jnp.bfloat16),
            pltpu.VMEM((2, half, width), jnp.bfloat16),
            pltpu.VMEM((n_tok, 2, half, width), jnp.bfloat16),
        )


def bring_in(
    tokens, cotangent, codes, in_left, out_right, out_blocks, first_t, right_t, left_t
):
    n_tok, n_hid = lax.axis_size("tok"), lax.axis_size("hid")
    _, groups, slots, deep, blk = first_t.shape
    wide, rank = in_left.shape
    rows, width = tokens.shape
    whole = rows * n_tok
    far = hid_shifts(n_hid)

    places = 1 + len(far)
    near_shifts = in_group_shifts(groups)
    per, fine = left_t.shape[0], left_t.shape[2]

    def body(
        tok_i, cot_i, code_i, left_i, right_i, second_i, first_i, r_i, l_i,
        pick_o, own_o, sum_o, low_o, gr_o, gl_o, outf_o, backf_o, gfirst_o, gsecond_o,
        send, recv, got_mid, held_mid, got_low, held_low, x_all, parts,
        core_got, low_mine, low_got, steps, taken, final,
        first_o, r_o, l_o, hidden, slope, stage_far, stage_first, stage_second,
    ):
        me = lax.axis_index("tok")
        near_bits = n_tok.bit_length() - 1
        far_bits = n_hid.bit_length() - 1
        lows = [code_bits(code_i, which, 0, near_bits) for which in range(2)]
        highs = [code_bits(code_i, which, near_bits, far_bits) for which in range(2)]
        own_bits = [
            [bit ^ ((me >> at) & 1) for at, bit in enumerate(lows[which])] for which in range(2)
        ]
        greet(tok_peers(n_tok) + [(0, dist) for dist in (1, *range(2, n_hid, 2))])
        mover = Mover(send, recv)
        part = [pl.ds(dist * rows, rows) for dist in range(n_tok)]
        first_waits, far_waits, row_waits = {}, [], []
        arrived = {}

        def send_first(group):
            first_waits[group] = [
                mover.start(
                    first_i.at[me ^ dist, group], first_o.at[group, :, span(me, deep), :], dist
                )
                for dist in (2, 3, 1, 0)
            ]

        def spread(at, dist):
            for pos, far_dist in enumerate(far):
                far_waits.append(
                    mover.start(
                        x_all.at[at, 0, part[dist], :],
                        x_all.at[at, 1 + pos, part[dist], :],
                        0,
                        far_dist,
                    )
                )

        routes = [
            Route(mover, src, got_mid.at[at], held_mid.at[at], highs[at])
            for at, src in enumerate((cot_i, tok_i))
        ]
        for route in routes:
            route.send(0)
        send_first(0)
        last = far_bits - 1
        for stage in range(far_bits):
            for at, route in enumerate(routes):
                route.take(stage)
                if stage < last:
                    route.send(stage + 1)
                    continue

                def store_near(rows_at, lanes, value):
                    x_all[at, 0, rows_at, lanes] = value

                swap_lanes(
                    store_near,
                    lambda rows_at, lanes: held_mid[at, last, rows_at, lanes],
                    lows[at], rows, blk, width // blk,
                )
                for dist in (1, 2):
                    arrived[at, dist] = mover.start(
                        x_all.at[at, 0, part[0], :], x_all.at[at, 0, part[dist], :], dist
                    )
        for at in range(2):
            spread(at, 0)
        more = [
            Route(mover, src, got_low.at[at], held_low.at[at], highs[at])
            for at, src in enumerate((right_i, left_i))
        ]
        route_all(more, far_bits)
        for at in range(2):
            pick_o[at] = held_low[at, last]
        for dist in (2, 3, 1, 0):
            row_waits.append(mover.start(r_i.at[me ^ dist], r_o.at[me], dist))
            row_waits.append(mover.start(l_i.at[:, me ^ dist], l_o.at[me], dist))
        for at in range(2):
            mover.arrived(arrived[at, 1])
            spread(at, 1)
        for at in range(2):
            mover.arrived(arrived[at, 2])
            arrived[at, 3] = mover.start(
                x_all.at[at, 0, part[2], :], x_all.at[at, 0, part[3], :], 1
            )
        send_first(1)
        for at in range(2):
            spread(at, 2)
        half = rows // 2
        for dist in range(n_tok):
            for at in range(2):
                if dist == 3:
                    mover.arrived(arrived[at, 3])
                own_o[at, part[dist], :] = choose(
                    lambda pos: x_all[at, 0, part[dist], pl.ds(pos * blk, blk)], n_tok, own_bits[at]
                )
            for side in range(2):
                piece = pl.ds(dist * rows + side * half, half)
                parts[dist, side, :, :rank] = jnp.dot(
                    own_o[1, piece, :], pick_o[1], preferred_element_type=jnp.float32
                )
                parts[dist, side, :, rank:] = dot_cols(own_o[0, piece, :], pick_o[0])
        low = LowSum(mover, n_tok, parts, core_got, low_mine, low_got, steps, taken, final)
        low.begin()
        low.fold_core()
        spread(0, 3)
        low.gather_parts()
        low.middle()
        spread(1, 3)
        for group in range(2, groups - 1):
            send_first(group)
        low.share()
        for group in range(groups - 1, groups):
            send_first(group)
        low.spread_core()
        low.settle()
        scale = lax.rsqrt(jnp.float32(whole))
        for entry in row_waits + far_waits:
            mover.arrived(entry)
        low_in = jnp.concatenate([low.rows(dist, pl.ds(0, rank)) for dist in range(n_tok)], axis=0)
        low_back = jnp.concatenate(
            [low.rows(dist, pl.ds(rank, rank)) for dist in range(n_tok)], axis=0
        )
        touched = set()
        staged = {}
        for group in range(groups):
            turn = group % 2

            def spot(k):
                if k < len(near_shifts):
                    return 0, pl.ds((group ^ near_shifts[k]) * blk, blk)
                return k - len(near_shifts) + 1, pl.ds(group * blk, blk)

            def second(k):
                return second_i[pl.ds(group * per, per), k].reshape(per * fine, blk)

            left = l_o[group].reshape(per * fine, rank)
            for entry in first_waits[group] + staged.pop(group - 2, []):
                mover.arrived(entry)
            total = jnp.dot(low_in, r_o[group], preferred_element_type=jnp.float32)
            for k in range(slots):
                place, lanes = spot(k)
                total = total + jnp.dot(
                    x_all[1, place, :, lanes],
                    first_o[group, k],
                    preferred_element_type=jnp.float32,
                )
            active, slopes = gelu_parts(total)
            hidden[...] = active.astype(jnp.bfloat16)
            total = dot_cols(low_back, left)
            for k in range(slots):
                place, lanes = spot(k)
                total = total + dot_cols(x_all[0, place, :, lanes], second(k))
            slope[...] = (total * slopes).astype(jnp.bfloat16)
            low_one = jnp.dot(hidden[...], left, preferred_element_type=jnp.float32)
            low_two = dot_cols(slope[...], r_o[group])
            if group == 0:
                low_o[:, :rank] = low_one
                low_o[:, rank:] = low_two
            else:
                low_o[:, :rank] += low_one
                low_o[:, rank:] += low_two
            entries = []
            for k in range(slots):
                place, lanes = spot(k)
                values = (
                    jnp.dot(hidden[...], second(k), preferred_element_type=jnp.float32),
                    dot_cols(slope[...], first_o[group, k]),
                )
                for which in range(2):
                    if k >= len(near_shifts):
                        stage_far[turn, which, place - 1] = values[which].astype(jnp.bfloat16)
                    elif (which, group ^ near_shifts[k]) in touched:
                        sum_o[which, :, lanes] = (
                            sum_o[which, :, lanes].astype(jnp.float32) + values[which]
                        ).astype(jnp.bfloat16)
                    else:
                        touched.add((which, group ^ near_shifts[k]))
                        sum_o[which, :, lanes] = values[which].astype(jnp.bfloat16)
            for which, dst in enumerate((outf_o, backf_o)):
                entries.append(
                    mover.start(
                        stage_far.at[turn, which], dst.at[:, :, pl.ds(group * blk, blk)]
                    )
                )
            for k in range(slots):
                place, lanes = spot(k)
                stage_first[turn, k] = (
                    scale * dot_rows(x_all[1, place, :, lanes], slope[...])
                ).astype(jnp.bfloat16)
                stage_second[turn, :, k] = (
                    (scale * dot_rows(hidden[...], x_all[0, place, :, lanes]))
                    .astype(jnp.bfloat16)
                    .reshape(per, fine, blk)
                )
            entries.append(mover.start(stage_first.at[turn], gfirst_o.at[group]))
            entries.append(
                mover.start(stage_second.at[turn], gsecond_o.at[pl.ds(group * per, per)])
            )
            gr_o[group] = (scale * dot_rows(low_in, slope[...])).astype(jnp.bfloat16)
            gl_o[group] = (
                (scale * dot_rows(hidden[...], low_back))
                .astype(jnp.bfloat16)
                .reshape(per, fine, rank)
            )
            staged[group] = entries
        mover.finish()

    f32 = jnp.float32
    return run_exchange(
        body,
        (
            tokens, cotangent, codes, in_left, out_right, out_blocks,
            first_t, right_t, left_t,
        ),
        [
            (2, wide, rank),
            (2, whole, blk),
            (2, whole, width),
            ((whole, 2 * rank), f32),
            (groups, rank, blk),
            (groups, per, fine, rank),
            (places - 1, whole, width),
            (places - 1, whole, width),
            (groups, slots, blk, blk),
            out_blocks.shape,
        ],
        8 * len(far) + groups * n_tok + 6 + 2 * n_tok * len(far) + 2 * n_tok
        + LowSum.copies(n_tok) + 4 * groups,
        1,
        (0, 1, 3, 4, 5),
        (
            pltpu.VMEM((2, len(far), rows, width), jnp.bfloat16),
            pltpu.VMEM((2, len(far), rows, width), jnp.bfloat16),
            pltpu.VMEM((2, len(far), wide, rank), jnp.bfloat16),
            pltpu.VMEM((2, len(far), wide, rank), jnp.bfloat16),
            pltpu.VMEM((2, places, whole, width), jnp.bfloat16),
            pltpu.VMEM((n_tok, 2, rows // 2, 2 * rank), jnp.float32),
        )
        + LowSum.scratch(rows, 2 * rank, n_tok)
        + (
            pltpu.VMEM((groups, slots, blk, blk), jnp.bfloat16),
            pltpu.VMEM((groups, rank, blk), jnp.bfloat16),
            pltpu.VMEM((groups, per, fine, rank), jnp.bfloat16),
            pltpu.VMEM((whole, blk), jnp.bfloat16),
            pltpu.VMEM((whole, blk), jnp.bfloat16),
            pltpu.VMEM((2, 2, places - 1, whole, blk), jnp.bfloat16),
            pltpu.VMEM((2, slots, blk, blk), jnp.bfloat16),
            pltpu.VMEM((2, per, slots, fine, blk), jnp.bfloat16),
        ),
        in_smem=(2,),
        out_vmem=(0, 1, 2, 3, 4, 5),
    )


def send_out(
    low_parts, own_sums, codes, own, picks,
    out_far, back_far, grads, right_g, left_g,
):
    n_tok, n_hid = lax.axis_size("tok"), lax.axis_size("hid")
    far = hid_shifts(n_hid)
    _, whole, width = out_far.shape
    rows = whole // n_tok
    rank = picks.shape[2]
    groups, slots, full, blk = grads.shape
    deep = full // n_tok
    _, per, fine, _ = left_g.shape
    wide = picks.shape[1]

    def body(
        low_i, sum_i, code_i, own_i, pick_i,
        outf_i, backf_i, grad_i, r_i, l_i,
        layer_o, gtok_o, gleft_o, gright_o, grad_o, r_o, l_o,
        send, recv, held, kept, got_one, pair, got_two, low_grad, spots,
        got_mid, held_mid, got_low, held_low,
        core_got, low_mine, low_got, steps, taken, final,
    ):
        me = lax.axis_index("tok")
        scale = lax.rsqrt(jnp.float32(whole))
        near_bits = n_tok.bit_length() - 1
        far_bits = n_hid.bit_length() - 1
        lows = [code_bits(code_i, which, 0, near_bits) for which in range(2)]
        highs = [code_bits(code_i, which, near_bits, far_bits) for which in range(2)]
        own_bits = [
            [bit ^ ((me >> at) & 1) for at, bit in enumerate(lows[which])] for which in range(2)
        ]
        greet(tok_peers(n_tok) + [(0, dist) for dist in (1, *range(2, n_hid, 2))])
        mover = Mover(send, recv)
        part = [pl.ds(dist * rows, rows) for dist in range(n_tok)]
        fars = (outf_i, backf_i)
        low = LowSum(mover, n_tok, low_i, core_got, low_mine, low_got, steps, taken, final)
        low.begin()
        waits = {}

        def send_far(which, dist):
            for pos, far_dist in enumerate(far):
                waits[which, dist, pos] = mover.start(
                    fars[which].at[pos, part[dist], :],
                    held.at[which, pos, part[dist], :],
                    0,
                    far_dist,
                )

        def send_grads(group):
            for dist in (2, 3, 1, 0):
                mover.start(
                    grad_i.at[group, :, span(me ^ dist, deep), :], grad_o.at[me, group], dist
                )

        first, second = {}, {}

        def settle(which, dist):
            total = sum_i[which, part[dist], :].astype(jnp.float32) + jnp.dot(
                low.rows(dist, pl.ds(which * rank, rank)),
                spots[which],
                preferred_element_type=jnp.float32,
            )
            for pos in range(len(far)):
                mover.arrived(waits[which, dist, pos])
                total = total + held[which, pos, part[dist], :].astype(jnp.float32)
            kept[which, part[dist], :] = total.astype(jnp.bfloat16)
            if dist % 2 == 1:
                first[which, dist - 1] = mover.start(
                    kept.at[which, part[dist], :], got_one.at[which, dist // 2], 1
                )

        def pass_on(which):
            mover.arrived(first[which, 2])
            pair[which] = (
                kept[which, part[2], :].astype(jnp.float32)
                + got_one[which, 1].astype(jnp.float32)
            ).astype(jnp.bfloat16)
            second[which] = mover.start(pair.at[which], got_two.at[which], 2)

        def close(which):
            mover.arrived(first[which, 0])
            mover.arrived(second[which])
            pair[which + 2] = (
                kept[which, part[0], :].astype(jnp.float32)
                + got_one[which, 0].astype(jnp.float32)
                + got_two[which].astype(jnp.float32)
            ).astype(jnp.bfloat16)
            route = Route(
                mover, pair.at[which + 2], got_mid.at[which], held_mid.at[which], highs[which]
            )
            route.send(0)
            return route

        send_grads(0)
        low.fold_core()
        send_far(0, 3)
        for which in range(2):
            weight = pick_i[which].astype(jnp.float32)
            if which == 1:
                weight = weight.T
            for place in range(width // blk):
                here = 1
                for at, bit in enumerate(own_bits[which]):
                    here = here * (bit if (place >> at) & 1 else 1 - bit)
                spots[which, :, pl.ds(place * blk, blk)] = (
                    weight * here.astype(jnp.float32)
                ).astype(jnp.bfloat16)
        low.gather_parts()
        send_far(0, 1)
        low.middle()
        send_far(0, 2)
        low.share()
        send_far(0, 0)
        send_grads(1)
        for dist in (2, 3, 1, 0):
            mover.start(r_i.at[me ^ dist], r_o.at[me], dist)
            mover.start(l_i.at[me ^ dist], l_o.at[:, me], dist)
        low.spread_core()
        low.settle()
        settle(0, 3)
        settle(0, 1)
        send_grads(2)
        for dist in (3, 1, 2, 0):
            send_far(1, dist)
        settle(0, 2)
        pass_on(0)
        settle(0, 0)
        low_mid = jnp.concatenate([low.rows(dist, pl.ds(0, rank)) for dist in range(n_tok)], axis=0)
        low_grad[0] = (scale * dot_rows(low_mid, own_i[0])).astype(jnp.bfloat16)
        low_back = jnp.concatenate(
            [low.rows(dist, pl.ds(rank, rank)) for dist in range(n_tok)], axis=0
        )
        low_grad[1] = (scale * dot_rows(own_i[1], low_back)).astype(jnp.bfloat16)
        settle(1, 3)
        settle(1, 1)
        routes = [close(0)]
        more = [
            Route(mover, low_grad.at[which], got_low.at[which], held_low.at[which], highs[which])
            for which in range(2)
        ]
        for route in more:
            route.send(0)
        settle(1, 2)
        pass_on(1)
        settle(1, 0)

        def advance(route, stage):
            route.take(stage)
            if stage + 1 < far_bits:
                route.send(stage + 1)

        last = far_bits - 1
        for stage in range(far_bits):
            for route in routes + more:
                advance(route, stage)
        routes.append(close(1))
        send_grads(3)
        gright_o[...] = held_low[0, last]
        gleft_o[...] = held_low[1, last]
        outs = (layer_o, gtok_o)
        for which in range(2):
            if which == 1:
                for stage in range(far_bits):
                    advance(routes[1], stage)

            def store_out(rows_at, lanes, value):
                outs[which][rows_at, lanes] = value

            swap_lanes(
                store_out,
                lambda rows_at, lanes: held_mid[which, last, rows_at, lanes],
                lows[which], rows, blk, width // blk,
            )
        mover.finish()

    return run_exchange(
        body,
        (
            low_parts, own_sums, codes, own, picks,
            out_far, back_far, grads, right_g, left_g,
        ),
        [
            (rows, width),
            (rows, width),
            (wide, rank),
            (rank, wide),
            (n_tok, groups, slots, deep, blk),
            (n_tok, rank, blk),
            (per, n_tok, fine, rank),
        ],
        n_tok * (2 * len(far) + groups + 2) + 8 + 8 * len(far) + LowSum.copies(n_tok),
        2,
        (0, 1, 3, 4),
        (
            pltpu.VMEM((2, len(far), whole, width), jnp.bfloat16),
            pltpu.VMEM((2, whole, width), jnp.bfloat16),
            pltpu.VMEM((2, 2, rows, width), jnp.bfloat16),
            pltpu.VMEM((4, rows, width), jnp.bfloat16),
            pltpu.VMEM((2, rows, width), jnp.bfloat16),
            pltpu.VMEM((2, wide, rank), jnp.bfloat16),
            pltpu.VMEM((2, rank, width), jnp.bfloat16),
            pltpu.VMEM((2, len(far), rows, width), jnp.bfloat16),
            pltpu.VMEM((2, len(far), rows, width), jnp.bfloat16),
            pltpu.VMEM((2, len(far), wide, rank), jnp.bfloat16),
            pltpu.VMEM((2, len(far), wide, rank), jnp.bfloat16),
        )
        + LowSum.scratch(rows, 2 * rank, n_tok),
        in_smem=(2,),
        out_vmem=(0, 1, 2, 3),
    )


def local_moved(
    tokens,
    in_blocks,
    in_left,
    in_right,
    in_lists,
    out_blocks,
    out_left,
    out_right,
    out_lists,
    cotangent,
):
    hid_blocks, slots, deep, blk = in_blocks.shape
    n_tok = lax.axis_size("tok")
    groups = tokens.shape[1] // blk
    per = hid_blocks // groups
    rank = in_left.shape[1]
    fine = blk // n_tok
    heads = jnp.stack([out_lists, in_lists])[:, 0, 0]
    codes = (heads[:, None] >> jnp.arange(8, dtype=jnp.int32)[None, :]) & 1
    first_t = swap_pieces(
        in_blocks.reshape(groups, per, slots * deep, blk), per, groups, True, False
    ).reshape(n_tok, groups, slots, deep, blk)
    right_t = swap_pieces(in_right, per, 1, None, False).reshape(n_tok, rank, blk)
    (
        picks,
        own,
        own_sums,
        low_parts,
        right_g,
        left_g,
        out_far,
        back_far,
        grad_first,
        grad_out_blocks,
    ) = bring_in(
        tokens,
        cotangent,
        codes,
        in_left,
        out_right,
        out_blocks,
        first_t,
        right_t,
        out_left.reshape(per, n_tok, fine, rank),
    )
    layer_out, grad_tokens, grad_in_left, grad_out_right, grad_got, right_got, left_got = send_out(
        low_parts.reshape(n_tok, 2, tokens.shape[0] // 2, 2 * rank),
        own_sums,
        codes,
        own,
        picks,
        out_far,
        back_far,
        grad_first,
        right_g,
        left_g,
    )
    grad_in_blocks = swap_pieces(
        grad_got.reshape(n_tok, groups, slots * deep, blk), per, groups, False, True
    ).reshape(hid_blocks, slots, deep, blk)
    grad_in_right = swap_pieces(right_got.reshape(n_tok, 1, rank, blk), per, 1, False, None)
    return (
        layer_out,
        grad_tokens,
        grad_in_blocks,
        grad_in_left,
        grad_in_right,
        grad_out_blocks,
        left_got.reshape(out_left.shape),
        grad_out_right,
    )


def power_of_two(count):
    return count & (count - 1) == 0


def local(*arrays):
    tokens, in_blocks = arrays[0], arrays[1]
    n_tok = lax.axis_size("tok")
    n_hid = lax.axis_size("hid")
    whole_groups = (
        n_tok == 4
        and n_hid == 2 * n_tok
        and tokens.shape[1] == n_tok * in_blocks.shape[3]
        and in_blocks.shape[0] == n_tok * n_tok
    )
    return local_moved(*arrays) if whole_groups else local_gathered(*arrays)


def solution(mesh):
    return jax.shard_map(
        local,
        mesh=mesh,
        in_specs=(
            P("tok", "hid"),
            P("hid", None, "tok", None),
            P(("hid", "tok"), None),
            P(None, ("hid", "tok")),
            P(),
            P("hid", None, "tok", None),
            P(("hid", "tok"), None),
            P(None, ("hid", "tok")),
            P(),
            P("tok", "hid"),
        ),
        out_specs=(
            P("tok", "hid"),
            P("tok", "hid"),
            P("hid", None, "tok", None),
            P(("hid", "tok"), None),
            P(None, ("hid", "tok")),
            P("hid", None, "tok", None),
            P(("hid", "tok"), None),
            P(None, ("hid", "tok")),
        ),
        check_vma=False,
    )
```
